512 devices in a mesh: section: 16 (over y, core), lat: 32 (over z, x).
Axes of the slice: x: 4, y: 8, z: 8, core: 2. Of those that a mesh axis runs over, the one named last changes fastest.
Arguments:
- section_input: bfloat16 [16, 64, 128, 1024], P('section', 'lat'), may hold values from -6 to 6
- handoff: bfloat16 [16, 64, 128, 1024], P('section', 'lat'), may hold values from -6 to 6
- loss_grad: bfloat16 [64, 128, 1024], P('lat'), may hold values from -6 to 6
- w_first: bfloat16 [16, 2, 2, 1024, 128], P('section'), may hold values from -0.375 to 0.375
- w_second: bfloat16 [16, 2, 2, 1024, 128], P('section'), may hold values from -0.375 to 0.375
- bias: float32 [16, 2, 2, 2, 1024], P('section'), may hold values from -3 to 3
- kept: int32 [16, 2, 8], P('section'), may hold values from 1 to 32, as said below
Outputs:
- handed_on: bfloat16 [16, 64, 128, 1024], P('section', 'lat')
- grad_first: float32 [16, 2, 2, 1024, 128], P('section', None, None, 'lat')
- grad_second: float32 [16, 2, 2, 1024, 128], P('section', None, None, 'lat')
- grad_bias: float32 [16, 2, 2, 2, 1024], P('section', None, None, None, 'lat')
The draws below stay inside these ranges and needn't reach their ends.
Inputs may be any that keep to these rules, and one draw needn't show every extreme that they name: `kept`: in every section and block layer one channel block keeps 32 modes and another keeps 1.
All inputs are finite; a program needn't handle non-finite values.
Results may differ from the reference program's by a relative error of at most 0.025.
Values may be sent and summed in bfloat16 or wider, within the bound.
No kernel may reach another device: no remote copies, remote signals or barrier semaphores. Data moves between devices by JAX's collectives and lax.ppermute only.
A program may use at most 64 MiB of HBM per device.

```python
import math
import jax
import jax.numpy as jnp
from jax import lax

NB = 8
BS = 128
CH = 1024
LON = 128
LAYERS = 2
LAT = 64
MODES = 64
MAXK = 32
SECTIONS = 16
N_LAT = 32


def draw_kept(key, part):
    first, second = jax.random.split(key)
    counts = jax.random.randint(first, (SECTIONS, LAYERS, NB), 1, MAXK + 1)
    chosen = jax.random.randint(second, (SECTIONS, LAYERS, 1), 0, NB)
    blocks = jnp.arange(NB, dtype=jnp.int32)[None, None, :]
    counts = jnp.where(blocks == chosen, MAXK, counts)
    counts = jnp.where(blocks == (chosen + 1) % NB, 1, counts)
    return counts.astype(jnp.int32)


def shard_levels(key, shape, cuts, least, top_value):
    def one(dim, blocks):
        steps = jax.random.uniform(jax.random.fold_in(jax.random.fold_in(key, 6), dim), (blocks,), jnp.float32, least / len(cuts), top_value / len(cuts))
        return jnp.repeat(jnp.exp(steps), shape[dim] // blocks).reshape((-1,) + (1,) * (len(shape) - dim - 1))

    factor_of = one(*cuts[0])
    for cut in cuts[1:]:
        factor_of = factor_of * one(*cut)
    return factor_of


def bell_draw(own_key, dims, width, bound, cuts=(), kind=jnp.bfloat16):
    values = width * jax.random.normal(own_key, dims, jnp.float32)
    if cuts:
        values = values * shard_levels(own_key, dims, cuts, -0.22, 0.18)
    return jnp.clip(values, -bound, bound).astype(kind)


def setup_inputs(seed: int = 0) -> dict:
    seeds = jax.random.split(jax.random.key(seed), 8)
    return {
        "section_input": bell_draw(seeds[0], (SECTIONS, LAT, LON, CH), 1.0, 6.0, ((0, 16), (1, 32))),
        "handoff": bell_draw(seeds[1], (SECTIONS, LAT, LON, CH), 1.0, 6.0, ((0, 16), (1, 32))),
        "loss_grad": bell_draw(seeds[2], (LAT, LON, CH), 1.0, 6.0, ((0, 32),)),
        "w_first": bell_draw(seeds[3], (SECTIONS, LAYERS, 2, CH, BS), (2 * BS) ** -0.5, 0.375, ((0, 16),)),
        "w_second": bell_draw(seeds[4], (SECTIONS, LAYERS, 2, CH, BS), (2 * BS) ** -0.5, 0.375, ((0, 16),)),
        "bias": bell_draw(seeds[5], (SECTIONS, LAYERS, 2, 2, CH), 0.5, 3.0, ((0, 16),), jnp.float32),
        "kept": draw_kept(jax.random.fold_in(seeds[7], 71), 0),
    }


def lon_tables(lon, freqs):
    cells = jnp.arange(lon, dtype=jnp.int32)
    phase = (freqs[:, None] * cells[None, :] % lon).astype(jnp.float32) * (2.0 * math.pi / lon)
    scale = 1.0 / math.sqrt(lon)
    forward = jnp.stack([jnp.cos(phase) * scale, -jnp.sin(phase) * scale])
    weights = jnp.where(freqs == 0, 1.0, 2.0).astype(jnp.float32)
    inverse = forward * weights[None, :, None]
    return (forward.astype(jnp.bfloat16), inverse.astype(jnp.bfloat16))

def lat_table(lat):
    rows = jnp.arange(lat, dtype=jnp.int32)
    phase = (rows[:, None] * rows[None, :] % lat).astype(jnp.float32) * (2.0 * math.pi / lat)
    scale = 1.0 / math.sqrt(lat)
    cosine = jnp.cos(phase) * scale
    sine = jnp.sin(phase) * scale
    upper = jnp.concatenate([cosine, sine], axis=1)
    lower = jnp.concatenate([-sine, cosine], axis=1)
    return jnp.concatenate([upper, lower], axis=0).astype(jnp.bfloat16)

def complex_mix(real, imag, weight):

    def prod(left, right):
        return jnp.einsum('rnb,nbh->rnh', left, right)
    return (prod(real, weight[0]) - prod(imag, weight[1]), prod(real, weight[1]) + prod(imag, weight[0]))

def complex_adjoint(real, imag, weight):

    def prod(left, right):
        return jnp.einsum('rnh,nbh->rnb', left, right)
    return (prod(real, weight[0]) + prod(imag, weight[1]), prod(imag, weight[0]) - prod(real, weight[1]))

def grouped_outer(left, right):
    shape = (LAT, MODES // N_LAT, N_LAT, NB, BS)

    def prod(first, second):
        return jnp.einsum('pkdnb,pkdnh->dnbh', first.reshape(shape), second.reshape(shape))
    parts = jnp.stack([prod(left[0], right[0]) + prod(left[1], right[1]), prod(left[0], right[1]) - prod(left[1], right[0])], axis=1)
    rounded = lax.optimization_barrier(parts.astype(jnp.bfloat16))
    return lax.optimization_barrier(jnp.sum(rounded.astype(jnp.float32), axis=0)).reshape(2, CH, BS)

def grouped_bias(values):
    shape = (2, LAT, MODES // N_LAT, N_LAT, CH)
    parts = lax.optimization_barrier(jnp.sum(values.reshape(shape), axis=(1, 2)))
    rounded = lax.optimization_barrier(parts.astype(jnp.bfloat16))
    return lax.optimization_barrier(jnp.sum(rounded.astype(jnp.float32), axis=1))

def spectral_state(x, tab_fwd, mixer, w_one, b_one):
    spec = jnp.einsum('rmj,ijc->rimc', tab_fwd.astype(jnp.float32), x.astype(jnp.float32)).astype(jnp.bfloat16)
    z = jnp.dot(mixer, spec.reshape(2 * LAT, -1), preferred_element_type=jnp.float32).astype(jnp.bfloat16)
    z = z.reshape(2, LAT * MODES, NB, BS).astype(jnp.float32)
    pre_r, pre_i = complex_mix(z[0], z[1], w_one)
    return (z, jnp.stack([pre_r, pre_i]) + b_one[:, None])

def layer_params(w_first, w_second, bias, kept, section, layer):
    w_one = w_first[section, layer].astype(jnp.float32).reshape(2, NB, BS, BS)
    w_two = w_second[section, layer].astype(jnp.float32).reshape(2, NB, BS, BS)
    b_one = bias[section, layer, 0].reshape(2, NB, BS)
    b_two = bias[section, layer, 1].reshape(2, NB, BS)
    freqs = jnp.arange(MODES, dtype=jnp.int32)
    mask = (freqs[:, None] < kept[section, layer][None, :]).astype(jnp.float32)
    mask = jnp.tile(mask, (LAT, 1))[:, :, None]
    return (w_one, w_two, b_one, b_two, mask)

def layer_output(x, z, pre, tab_inv, mixer, params):
    w_one, w_two, b_one, b_two, mask = params
    hidden = jax.nn.silu(pre).astype(jnp.bfloat16).astype(jnp.float32)
    out_r, out_i = complex_mix(hidden[0], hidden[1], w_two)
    out = ((jnp.stack([out_r, out_i]) + b_two[:, None]) * mask).astype(jnp.bfloat16)
    u = jnp.dot(mixer.T, out.reshape(2 * LAT, -1), preferred_element_type=jnp.float32).astype(jnp.bfloat16)
    u = u.reshape(2, LAT, MODES, CH)
    y = jnp.einsum('rmj,rimc->ijc', tab_inv.astype(jnp.float32), u.astype(jnp.float32))
    return (x.astype(jnp.float32) + y).astype(jnp.bfloat16)

def layer_backward(grad, z, pre, tab_fwd, tab_inv, mixer, params):
    w_one, w_two, b_one, b_two, mask = params
    hidden = jax.nn.silu(pre).astype(jnp.bfloat16).astype(jnp.float32)
    du = jnp.einsum('rmj,ijc->rimc', tab_inv.astype(jnp.float32), grad.astype(jnp.float32)).astype(jnp.bfloat16)
    dout = jnp.dot(mixer, du.reshape(2 * LAT, -1), preferred_element_type=jnp.float32)
    dout = (dout.reshape(2, LAT * MODES, NB, BS) * mask).astype(jnp.bfloat16).astype(jnp.float32)
    dhid_r, dhid_i = complex_adjoint(dout[0], dout[1], w_two)
    sig = jax.nn.sigmoid(pre)
    dpre = (jnp.stack([dhid_r, dhid_i]) * (sig * (1.0 + pre * (1.0 - sig)))).astype(jnp.bfloat16).astype(jnp.float32)
    dz_r, dz_i = complex_adjoint(dpre[0], dpre[1], w_one)
    dz = jnp.stack([dz_r, dz_i]).astype(jnp.bfloat16)
    da = jnp.dot(mixer.T, dz.reshape(2 * LAT, -1), preferred_element_type=jnp.float32).astype(jnp.bfloat16)
    da = da.reshape(2, LAT, MODES, CH)
    dx = grad.astype(jnp.float32) + jnp.einsum('rmj,rimc->ijc', tab_fwd.astype(jnp.float32), da.astype(jnp.float32))
    g_one = grouped_outer(z, dpre)
    g_two = grouped_outer(hidden, dout)
    g_bias = jnp.stack([grouped_bias(dpre.reshape(2, LAT * MODES, CH)), grouped_bias(dout.reshape(2, LAT * MODES, CH))])
    return (dx.astype(jnp.bfloat16), g_one, g_two, g_bias)

def reference(section_input, handoff, loss_grad, w_first, w_second, bias, kept):
    tab_fwd, tab_inv = lon_tables(LON, jnp.arange(MODES, dtype=jnp.int32))
    mixer = lat_table(LAT)
    handed, first_all, second_all, bias_all = ([], [], [], [])
    for section in range(SECTIONS):
        cot = loss_grad if section == SECTIONS - 1 else handoff[section + 1]
        params = [layer_params(w_first, w_second, bias, kept, section, layer) for layer in range(LAYERS)]
        inputs, states = ([section_input[section]], [])
        for layer in range(LAYERS):
            z, pre = spectral_state(inputs[layer], tab_fwd, mixer, params[layer][0], params[layer][2])
            states.append((z, pre))
            if layer + 1 < LAYERS:
                inputs.append(layer_output(inputs[layer], z, pre, tab_inv, mixer, params[layer]))
        grad = cot
        ones, twos, biases = ([None] * LAYERS, [None] * LAYERS, [None] * LAYERS)
        for layer in reversed(range(LAYERS)):
            z, pre = states[layer]
            grad, ones[layer], twos[layer], biases[layer] = layer_backward(grad, z, pre, tab_fwd, tab_inv, mixer, params[layer])
        handed.append(grad)
        first_all.append(jnp.stack(ones))
        second_all.append(jnp.stack(twos))
        bias_all.append(jnp.stack(biases))
    return (jnp.stack(handed), jnp.stack(first_all), jnp.stack(second_all), jnp.stack(bias_all))
```

```python
import math

import jax
import jax.numpy as jnp
import numpy as np
from jax import lax
from jax.experimental import pallas as pl
from jax.experimental.pallas import tpu as pltpu
from jax.sharding import PartitionSpec as P

LAYERS = 2
MAXK = 32
F32 = jnp.float32
BF16 = jnp.bfloat16


def lon_table(lon, rows, quarters, weighted):
    per = MAXK // quarters
    freqs = np.arange(MAXK)
    phase = 2.0 * math.pi * ((freqs[:, None] * np.arange(lon)[None, :]) % lon) / lon
    table = np.stack([np.cos(phase), -np.sin(phase)]) / math.sqrt(lon)
    table[1, 0] = 0.0
    table = table.astype(jnp.bfloat16).astype(np.float32)
    if weighted:
        table = table * np.where(freqs == 0, 1.0, 2.0)[None, :, None]
    split = table.reshape(2, quarters, per, lon).transpose(1, 0, 2, 3)
    full = np.zeros((quarters, 2, rows, per, rows, lon), np.float32)
    for row in range(rows):
        full[:, :, row, :, row, :] = split
    return full.reshape(quarters * 2 * rows * per, rows * lon).astype(jnp.bfloat16)


def lat_table(lat, rows):
    phase = 2.0 * math.pi * ((np.arange(lat)[:, None] * np.arange(lat)[None, :]) % lat) / lat
    cosine = np.cos(phase) / math.sqrt(lat)
    sine = np.sin(phase) / math.sqrt(lat)
    mixer = np.block([[cosine, sine], [-sine, cosine]])
    mixer = mixer.reshape(2 * lat, 2, lat // rows, rows).transpose(0, 2, 1, 3)
    return mixer.reshape(2 * lat, 2 * lat).astype(jnp.bfloat16)


def dot(left, right):
    return jnp.dot(left, right, preferred_element_type=F32)


def dot_rows(left, right):
    return lax.dot_general(left, right, (((1,), (1,)), ((), ())), preferred_element_type=F32)


def dot_cols(left, right):
    return lax.dot_general(left, right, (((0,), (0,)), ((), ())), preferred_element_type=F32)


def params(**kw):
    return pltpu.CompilerParams(vmem_limit_bytes=48 * 1024 * 1024, **kw)


def to_spectral(x, table, quarters, width):
    cells, channels = x.shape
    rows = table.shape[0] // quarters
    blocks = channels // width
    step = 2

    def body(t_ref, x_ref, o_ref):
        y = dot(t_ref[...], x_ref[...]).astype(BF16)
        for b in range(step):
            for q in range(quarters):
                o_ref[b * quarters + q] = y[q * rows : (q + 1) * rows, b * width : (b + 1) * width]

    return pl.pallas_call(
        body,
        grid=(blocks // step,),
        in_specs=[
            pl.BlockSpec(table.shape, lambda i: (0, 0)),
            pl.BlockSpec((cells, step * width), lambda i: (0, i)),
        ],
        out_specs=pl.BlockSpec((step * quarters, rows, width), lambda i: (i, 0, 0)),
        out_shape=jax.ShapeDtypeStruct((blocks * quarters, rows, width), BF16),
        compiler_params=params(),
        name="to_spectral",
    )(table, x)


def to_cells(parts, table_t, grid_add, quarters, width):
    cells, channels = grid_add.shape
    rows = parts.shape[1]
    blocks = channels // width
    step = 2

    def body(t_ref, p_ref, g_ref, o_ref):
        for b in range(step):
            part = p_ref[b * quarters : (b + 1) * quarters].reshape(quarters * rows, width)
            lanes = slice(b * width, (b + 1) * width)
            o_ref[:, lanes] = (g_ref[:, lanes].astype(F32) + dot(t_ref[...], part)).astype(BF16)

    return pl.pallas_call(
        body,
        grid=(blocks // step,),
        in_specs=[
            pl.BlockSpec(table_t.shape, lambda i: (0, 0)),
            pl.BlockSpec((step * quarters, rows, width), lambda i: (i, 0, 0)),
            pl.BlockSpec((cells, step * width), lambda i: (0, i)),
        ],
        out_specs=pl.BlockSpec((cells, step * width), lambda i: (0, i)),
        out_shape=jax.ShapeDtypeStruct((cells, channels), BF16),
        compiler_params=params(),
        name="to_cells",
    )(table_t, parts, grid_add)


def complex_square(w_ref, layer):
    real, imag = (w_ref[0, layer, 0], w_ref[0, layer, 1])
    return jnp.concatenate(
        [jnp.concatenate([real, imag], axis=1), jnp.concatenate([-imag, real], axis=1)], axis=0
    )


def spectral_chain(scalars, spec, du, mixer, w_first, w_second, bias, lat, width):
    per = spec.shape[0] * spec.shape[1] // (2 * lat)
    chunk = spec.shape
    tall = per * lat

    def body(s_ref, spec_ref, du_ref, l_ref, lt_ref, w1_ref, w2_ref, b_ref, da_ref, keep_ref, tmp):
        block, quarter = (s_ref[0], s_ref[1])
        mix, mix_t = (l_ref[...], lt_ref[...])

        def mixed(ref):
            tmp[...] = ref[...].reshape(2 * lat * per, width).astype(F32)
            parts = []
            for k in range(per):
                column = tmp[pl.ds(k, 2 * lat, stride=per), :].astype(BF16)
                z = dot(mix, column)
                parts.append(jnp.concatenate([z[:lat], z[lat:]], axis=1))
            return jnp.concatenate(parts, axis=0)

        rows = lax.broadcasted_iota(jnp.int32, (lat, lat), 0)
        cols = lax.broadcasted_iota(jnp.int32, (lat, lat), 1)
        eye = (rows == cols).astype(F32)
        back = ((rows + cols) % lat == 0).astype(F32)
        has_zero = (quarter == 0).astype(F32)
        even = (eye + 0.5 * has_zero * (back - eye)).astype(BF16)
        odd = (eye - 0.5 * has_zero * (back + eye)).astype(BF16)

        def through_grid(v):
            first = v[:lat]
            first = jnp.concatenate(
                [dot(even, first[:, :width]), dot(odd, first[:, width:])], axis=1
            )
            return jnp.concatenate([first, v[lat:].astype(F32)], axis=0)

        def mask_of(layer):
            mode = quarter * per + lax.broadcasted_iota(jnp.int32, (tall, 1), 0) // lat
            return (mode < s_ref[2 + layer * 8 + block]).astype(F32)

        def bias_of(layer, which):
            part = b_ref[0, layer, which]
            return jnp.concatenate([part[0:1], part[1:2]], axis=1)

        w_one = [complex_square(w1_ref, layer) for layer in range(LAYERS)]
        w_two = [complex_square(w2_ref, layer) for layer in range(LAYERS)]

        z = mixed(spec_ref)
        slopes = []
        for layer in range(LAYERS):
            z_low = z.astype(BF16)
            keep_ref[layer] = z_low
            pre = dot(z_low, w_one[layer]) + bias_of(layer, 0)
            sig = jax.nn.sigmoid(pre)
            hidden = (pre * sig).astype(BF16)
            keep_ref[2 + layer] = hidden
            slopes.append(sig * (1.0 + pre * (1.0 - sig)))
            if layer + 1 < LAYERS:
                out = ((dot(hidden, w_two[layer]) + bias_of(layer, 1)) * mask_of(layer)).astype(BF16)
                z = z + through_grid(out)
        grad = mixed(du_ref)
        total = None
        for layer in reversed(range(LAYERS)):
            dout = (grad * mask_of(layer)).astype(BF16)
            keep_ref[6 + layer] = dout
            dpre = (dot_rows(dout, w_two[layer]) * slopes[layer]).astype(BF16)
            keep_ref[4 + layer] = dpre
            dz = dot_rows(dpre, w_one[layer])
            if layer:
                grad = grad + through_grid(dz.astype(BF16))
            total = dz if total is None else total + dz
        total = total.astype(BF16)
        for k in range(per):
            part = total[k * lat : (k + 1) * lat]
            part = jnp.concatenate([part[:, :width], part[:, width:]], axis=0)
            tmp[pl.ds(k, 2 * lat, stride=per), :] = dot(mix_t, part)
        da_ref[...] = tmp[...].astype(BF16).reshape(chunk)

    whole = lambda shape: pl.BlockSpec(shape, lambda i, s: (0,) * len(shape))
    weight = pl.BlockSpec((1, LAYERS, 2, width, width), lambda i, s: (0, 0, 0, s[0], 0))
    return pl.pallas_call(
        body,
        grid_spec=pltpu.PrefetchScalarGridSpec(
            num_scalar_prefetch=1,
            grid=(1,),
            in_specs=[
                whole(chunk),
                whole(chunk),
                whole(mixer.shape),
                whole(mixer.shape),
                weight,
                weight,
                pl.BlockSpec((1, LAYERS, 2, 2, width), lambda i, s: (0, 0, 0, 0, s[0])),
            ],
            out_specs=[whole(chunk), whole((8, tall, 2 * width))],
            scratch_shapes=[pltpu.VMEM((2 * lat * per, width), F32)],
        ),
        out_shape=[
            jax.ShapeDtypeStruct(chunk, BF16),
            jax.ShapeDtypeStruct((8, tall, 2 * width), BF16),
        ],
        compiler_params=params(),
        name="spectral_chain",
    )(scalars, spec, du, mixer, mixer.T.copy(), w_first, w_second, bias)


def gradient_parts(scalars, kept_values, quarters, width):
    own = width // quarters
    count = 4 * LAYERS * own + 16

    def body(s_ref, v_ref, mine_ref, *rest):
        others, all_ref = (rest[:-1], rest[-1])
        index = lax.broadcasted_iota(jnp.int32, (16, width), 0)
        sums = jnp.zeros((16, width), F32)
        for which in range(2):
            for layer in range(LAYERS):
                right = v_ref[4 + 2 * which + layer]
                outer = dot_cols(v_ref[2 * which + layer], right)
                total = jnp.sum(right.astype(F32), axis=0, keepdims=True)
                squares = (
                    outer[:width, :width] + outer[width:, width:],
                    outer[:width, width:] - outer[width:, :width],
                )
                for r in range(2):
                    all_ref[(which * LAYERS + layer) * 2 + r] = squares[r]
                    slot = (layer * 2 + which) * 2 + r
                    sums = sums + jnp.where(index == slot, total[:, r * width : (r + 1) * width], 0.0)
        for step, o_ref in enumerate((mine_ref,) + others):
            start = pl.multiple_of((s_ref[1] + step) % quarters * own, own)
            for square in range(4 * LAYERS):
                part = all_ref[square, pl.ds(start, own), :]
                o_ref[square * own : (square + 1) * own] = part.astype(o_ref.dtype)
            o_ref[4 * LAYERS * own :] = sums.astype(o_ref.dtype)

    whole = lambda shape: pl.BlockSpec(shape, lambda i, s: (0,) * len(shape))
    return pl.pallas_call(
        body,
        grid_spec=pltpu.PrefetchScalarGridSpec(
            num_scalar_prefetch=1,
            grid=(1,),
            in_specs=[whole(kept_values.shape)],
            out_specs=[whole((count, width))] * quarters,
            scratch_shapes=[pltpu.VMEM((4 * LAYERS, width, width), F32)],
        ),
        out_shape=[jax.ShapeDtypeStruct((count, width), F32)]
        + [jax.ShapeDtypeStruct((count, width), BF16)] * (quarters - 1),
        compiler_params=params(),
        name="gradient_parts",
    )(scalars, kept_values)


def gradient_sum(scalars, parts, width):
    quarters = len(parts)
    own = width // quarters
    half = 2 * LAYERS * own

    def body(s_ref, *refs):
        first_ref, second_ref, bias_ref = refs[quarters:]
        total = refs[0][...]
        for ref in refs[1:quarters]:
            total = total + ref[...].astype(F32)
        first_ref[...] = total[:half]
        second_ref[...] = total[half : 2 * half]
        sums = total[2 * half : 2 * half + 8]
        mine = sums[:, :own]
        for q in range(1, quarters):
            mine = jnp.where(s_ref[1] == q, sums[:, q * own : (q + 1) * own], mine)
        bias_ref[...] = mine

    whole = lambda shape: pl.BlockSpec(shape, lambda i, s: (0,) * len(shape))
    return pl.pallas_call(
        body,
        grid_spec=pltpu.PrefetchScalarGridSpec(
            num_scalar_prefetch=1,
            grid=(1,),
            in_specs=[whole(part.shape) for part in parts],
            out_specs=[whole((half, width)), whole((half, width)), whole((8, own))],
        ),
        out_shape=[
            jax.ShapeDtypeStruct((half, width), F32),
            jax.ShapeDtypeStruct((half, width), F32),
            jax.ShapeDtypeStruct((8, own), F32),
        ],
        compiler_params=params(),
        name="gradient_sum",
    )(scalars, *parts)


def on_device(section_input, handoff, loss_grad, w_first, w_second, bias, kept):
    lat_count = lax.axis_size("lat")
    sections = lax.axis_size("section")
    _, rows, lon, channels = section_input.shape
    width = w_first.shape[-1]
    blocks = channels // width
    quarters = lat_count // blocks
    lat = rows * lat_count
    forward = lon_table(lon, rows, quarters, False)
    inverse = lon_table(lon, rows, quarters, True)
    mixer = lat_table(lat, rows)
    place = lax.axis_index("lat")
    scalars = jnp.concatenate(
        [jnp.stack([place // quarters, place % quarters]).astype(jnp.int32), kept.reshape(-1)]
    )

    received = lax.ppermute(handoff, "section", [(s, s - 1) for s in range(1, sections)])
    spec = to_spectral(section_input.reshape(rows * lon, channels), forward, quarters, width)
    spec = lax.all_to_all(spec, "lat", split_axis=0, concat_axis=0, tiled=True)
    cot = jnp.where(lax.axis_index("section") == sections - 1, loss_grad, received[0])
    cot = cot.reshape(rows * lon, channels)
    du = to_spectral(cot, inverse, quarters, width)
    du = lax.all_to_all(du, "lat", split_axis=0, concat_axis=0, tiled=True)
    da, values = spectral_chain(scalars, spec, du, mixer, w_first, w_second, bias, lat, width)
    da = lax.all_to_all(da, "lat", split_axis=0, concat_axis=0, tiled=True)
    parts = list(gradient_parts(scalars, values, quarters, width))
    for step in range(1, quarters):
        pairs = [
            (b * quarters + q, b * quarters + (q + step) % quarters)
            for b in range(blocks)
            for q in range(quarters)
        ]
        parts[step] = lax.ppermute(parts[step], "lat", pairs)
    handed = to_cells(da, forward.T.copy(), cot, quarters, width)
    first, second, biases = gradient_sum(scalars, parts, width)
    own = width // quarters
    return (
        handed.reshape(1, rows, lon, channels),
        first.reshape(1, LAYERS, 2, own, width),
        second.reshape(1, LAYERS, 2, own, width),
        biases.reshape(1, LAYERS, 2, 2, own),
    )


def solution(mesh):
    return jax.shard_map(
        on_device,
        mesh=mesh,
        in_specs=(
            P("section", "lat", None, None),
            P("section", "lat", None, None),
            P("lat", None, None),
            P("section", None, None, None, None),
            P("section", None, None, None, None),
            P("section", None, None, None, None),
            P("section", None, None),
        ),
        out_specs=(
            P("section", "lat", None, None),
            P("section", None, None, "lat", None),
            P("section", None, None, "lat", None),
            P("section", None, None, None, "lat"),
        ),
        check_vma=False,
    )
```

```python
import math

import jax
import jax.numpy as jnp
import numpy as np
from jax import lax
from jax.experimental import pallas as pl
from jax.experimental.pallas import tpu as pltpu
from jax.sharding import PartitionSpec as P

LAYERS = 2
MAXK = 32
F32 = jnp.float32
BF16 = jnp.bfloat16


def lon_table(lon, rows, quarters, weighted):
    per = MAXK // quarters
    freqs = np.arange(MAXK)
    phase = 2.0 * math.pi * ((freqs[:, None] * np.arange(lon)[None, :]) % lon) / lon
    table = np.stack([np.cos(phase), -np.sin(phase)]) / math.sqrt(lon)
    table[1, 0] = 0.0
    table = table.astype(jnp.bfloat16).astype(np.float32)
    if weighted:
        table = table * np.where(freqs == 0, 1.0, 2.0)[None, :, None]
    split = table.reshape(2, quarters, per, lon).transpose(1, 0, 2, 3)
    full = np.zeros((quarters, 2, rows, per, rows, lon), np.float32)
    for row in range(rows):
        full[:, :, row, :, row, :] = split
    return full.reshape(quarters * 2 * rows * per, rows * lon).astype(jnp.bfloat16)


def lat_table(lat, rows):
    phase = 2.0 * math.pi * ((np.arange(lat)[:, None] * np.arange(lat)[None, :]) % lat) / lat
    cosine = np.cos(phase) / math.sqrt(lat)
    sine = np.sin(phase) / math.sqrt(lat)
    mixer = np.block([[cosine, sine], [-sine, cosine]])
    mixer = mixer.reshape(2 * lat, 2, lat // rows, rows).transpose(0, 2, 1, 3)
    return mixer.reshape(2 * lat, 2 * lat).astype(jnp.bfloat16)


def dot(left, right):
    return jnp.dot(left, right, preferred_element_type=F32)


def dot_rows(left, right):
    return lax.dot_general(left, right, (((1,), (1,)), ((), ())), preferred_element_type=F32)


def dot_cols(left, right):
    return lax.dot_general(left, right, (((0,), (0,)), ((), ())), preferred_element_type=F32)


def params(**kw):
    return pltpu.CompilerParams(vmem_limit_bytes=12 * 1024 * 1024, **kw)


VMEM = pl.BlockSpec(memory_space=pltpu.VMEM)
SMEM = pl.BlockSpec(memory_space=pltpu.SMEM)
HBM = pl.BlockSpec(memory_space=pltpu.HBM)


def in_hbm(value):
    return pltpu.with_memory_space_constraint(value, pltpu.HBM)


def to_spectral(scalars, sources, table, quarters, width):
    cells, channels = sources[0].shape
    rows = table.shape[0] // quarters
    blocks = channels // width
    cuts = 4
    span = channels // cuts

    def body(s_ref, t_hbm, *refs):
        given = refs[: len(sources)]
        o_ref, t_buf, x_buf, t_sem, x_sem = refs[len(sources) :]

        def piece(source, cut):
            return pltpu.make_async_copy(
                source.at[:, pl.ds(cut * span, span)], x_buf.at[cut], x_sem.at[cut]
            )

        def begin(source):
            for cut in range(cuts):
                piece(source, cut).start()

        if len(given) == 1:
            begin(given[0])
        else:
            pl.when(s_ref[0] != 0)(lambda: begin(given[0]))
            pl.when(s_ref[0] == 0)(lambda: begin(given[1]))
        table_copy = pltpu.make_async_copy(t_hbm, t_buf, t_sem)
        table_copy.start()
        table_copy.wait()
        t = t_buf[...]
        for cut in range(cuts):
            piece(given[0], cut).wait()
            y = dot(t, x_buf[cut]).astype(BF16)
            for b in range(span // width):
                for q in range(quarters):
                    owner = (cut * (span // width) + b) * quarters + q
                    o_ref[owner] = y[q * rows : (q + 1) * rows, b * width : (b + 1) * width]

    return pl.pallas_call(
        body,
        in_specs=[SMEM, HBM] + [HBM] * len(sources),
        out_specs=VMEM,
        scratch_shapes=[
            pltpu.VMEM(table.shape, BF16),
            pltpu.VMEM((cuts, cells, span), BF16),
            pltpu.SemaphoreType.DMA(()),
            pltpu.SemaphoreType.DMA((cuts,)),
        ],
        out_shape=jax.ShapeDtypeStruct((blocks * quarters, rows, width), BF16),
        compiler_params=params(),
        name="to_spectral",
    )(scalars, in_hbm(jnp.asarray(table)), *[in_hbm(source) for source in sources])


def to_cells(parts, table_t, grid_add, quarters, width):
    cells, channels = grid_add.shape
    rows = parts.shape[1]
    cuts = 4
    span = channels // cuts
    step = span // width

    def body(t_ref, p_ref, g_ref, o_hbm, buf, sem):
        copies = []
        for cut in range(cuts):
            for b in range(step):
                block = cut * step + b
                part = p_ref[block * quarters : (block + 1) * quarters]
                part = part.reshape(quarters * rows, width)
                lanes = slice(block * width, (block + 1) * width)
                mixed = g_ref[:, lanes].astype(F32) + dot(t_ref[...], part)
                buf[cut, :, b * width : (b + 1) * width] = mixed.astype(BF16)
            copies.append(
                pltpu.make_async_copy(
                    buf.at[cut], o_hbm.at[:, pl.ds(cut * span, span)], sem.at[cut]
                )
            )
            copies[-1].start()
        for copy in copies:
            copy.wait()

    return pl.pallas_call(
        body,
        in_specs=[VMEM, VMEM, VMEM],
        out_specs=HBM,
        scratch_shapes=[
            pltpu.VMEM((cuts, cells, span), BF16),
            pltpu.SemaphoreType.DMA((cuts,)),
        ],
        out_shape=jax.ShapeDtypeStruct((cells, channels), BF16),
        compiler_params=params(),
        name="to_cells",
    )(table_t, parts, grid_add)


def block_params(scalars, w_first, w_second, bias, width):
    def body(s_ref, w1_hbm, w2_hbm, b_ref, w_ref, rows_ref, buf, sem):
        start = pl.multiple_of(s_ref[1] * width, width)
        copies = [
            pltpu.make_async_copy(w.at[0, :, :, pl.ds(start, width), :], buf.at[which], sem.at[which])
            for which, w in enumerate((w1_hbm, w2_hbm))
        ]
        for copy in copies:
            copy.start()
        for layer in range(LAYERS):
            for which in range(2):
                for r in range(2):
                    rows_ref[2 * layer + which, :, r * width : (r + 1) * width] = b_ref[
                        0, layer, which, pl.ds(r, 1), pl.ds(start, width)
                    ]
        for which in range(2):
            copies[which].wait()
            for layer in range(LAYERS):
                real, imag = (buf[which, layer, 0], buf[which, layer, 1])
                w_ref[2 * layer + which, :width, :width] = real
                w_ref[2 * layer + which, :width, width:] = imag
                w_ref[2 * layer + which, width:, :width] = -imag
                w_ref[2 * layer + which, width:, width:] = real

    return pl.pallas_call(
        body,
        in_specs=[SMEM, HBM, HBM, VMEM],
        out_specs=[VMEM, VMEM],
        scratch_shapes=[
            pltpu.VMEM((2, LAYERS, 2, width, width), BF16),
            pltpu.SemaphoreType.DMA((2,)),
        ],
        out_shape=[
            jax.ShapeDtypeStruct((2 * LAYERS, 2 * width, 2 * width), BF16),
            jax.ShapeDtypeStruct((2 * LAYERS, 1, 2 * width), F32),
        ],
        compiler_params=params(),
        name="block_params",
    )(scalars, in_hbm(w_first), in_hbm(w_second), bias)


def spectral_chain(scalars, parts, mixer, mixer_t, weights, biases, lat, width):
    sources, both, _ = parts.shape
    chunk = (sources, both // 2, width)
    per = sources * (both // 2) // (2 * lat)
    tall = per * lat

    def body(s_ref, parts_ref, l_ref, lt_ref, w_ref, b_ref, da_ref, keep_ref, tmp):
        quarter = s_ref[2]
        mix, mix_t = (l_ref[...], lt_ref[...])

        def mixed(slot):
            part = parts_ref[:, slot * (both // 2) : (slot + 1) * (both // 2), :]
            tmp[slot] = part.reshape(2 * lat * per, width).astype(F32)
            cells = []
            for k in range(per):
                column = tmp[slot, pl.ds(k, 2 * lat, stride=per), :].astype(BF16)
                z = dot(mix, column)
                cells.append(jnp.concatenate([z[:lat], z[lat:]], axis=1))
            return jnp.concatenate(cells, axis=0)

        rows = lax.broadcasted_iota(jnp.int32, (lat, lat), 0)
        cols = lax.broadcasted_iota(jnp.int32, (lat, lat), 1)
        eye = (rows == cols).astype(F32)
        back = ((rows + cols) % lat == 0).astype(F32)
        has_zero = (quarter == 0).astype(F32)
        even = (eye + 0.5 * has_zero * (back - eye)).astype(BF16)
        odd = (eye - 0.5 * has_zero * (back + eye)).astype(BF16)

        def through_grid(v):
            first = v[:lat]
            first = jnp.concatenate(
                [dot(even, first[:, :width]), dot(odd, first[:, width:])], axis=1
            )
            return jnp.concatenate([first, v[lat:].astype(F32)], axis=0)

        def mask_of(layer):
            mode = quarter * per + lax.broadcasted_iota(jnp.int32, (tall, 1), 0) // lat
            return (mode < s_ref[3 + layer]).astype(F32)

        z = mixed(0)
        slopes = []
        for layer in range(LAYERS):
            z_low = z.astype(BF16)
            keep_ref[layer] = z_low
            pre = dot(z_low, w_ref[2 * layer]) + b_ref[2 * layer]
            sig = jax.nn.sigmoid(pre)
            hidden = (pre * sig).astype(BF16)
            keep_ref[2 + layer] = hidden
            slopes.append(sig * (1.0 + pre * (1.0 - sig)))
            if layer + 1 < LAYERS:
                out = dot(hidden, w_ref[2 * layer + 1]) + b_ref[2 * layer + 1]
                z = z + through_grid((out * mask_of(layer)).astype(BF16))
        grad = mixed(1)
        total = None
        for layer in reversed(range(LAYERS)):
            dout = (grad * mask_of(layer)).astype(BF16)
            keep_ref[6 + layer] = dout
            dpre = (dot_rows(dout, w_ref[2 * layer + 1]) * slopes[layer]).astype(BF16)
            keep_ref[4 + layer] = dpre
            dz = dot_rows(dpre, w_ref[2 * layer])
            if layer:
                grad = grad + through_grid(dz.astype(BF16))
            total = dz if total is None else total + dz
        total = total.astype(BF16)
        for k in range(per):
            part = total[k * lat : (k + 1) * lat]
            part = jnp.concatenate([part[:, :width], part[:, width:]], axis=0)
            tmp[0, pl.ds(k, 2 * lat, stride=per), :] = dot(mix_t, part)
        da_ref[...] = tmp[0].astype(BF16).reshape(chunk)

    return pl.pallas_call(
        body,
        in_specs=[SMEM] + [VMEM] * 5,
        out_specs=[VMEM, VMEM],
        scratch_shapes=[pltpu.VMEM((2, 2 * lat * per, width), F32)],
        out_shape=[
            jax.ShapeDtypeStruct(chunk, BF16),
            jax.ShapeDtypeStruct((8, tall, 2 * width), BF16),
        ],
        compiler_params=params(),
        name="spectral_chain",
    )(scalars, parts, mixer, mixer_t, weights, biases)


def gradient_parts(scalars, kept_values, quarters, width):
    own = width // quarters
    count = 4 * LAYERS * own + 16

    def body(s_ref, v_ref, mine_ref, *rest):
        others, all_ref = (rest[:-1], rest[-1])
        index = lax.broadcasted_iota(jnp.int32, (16, width), 0)
        sums = jnp.zeros((16, width), F32)
        for which in range(2):
            for layer in range(LAYERS):
                right = v_ref[4 + 2 * which + layer]
                outer = dot_cols(v_ref[2 * which + layer], right)
                total = jnp.sum(right.astype(F32), axis=0, keepdims=True)
                squares = (
                    outer[:width, :width] + outer[width:, width:],
                    outer[:width, width:] - outer[width:, :width],
                )
                for r in range(2):
                    all_ref[(which * LAYERS + layer) * 2 + r] = squares[r]
                    slot = (layer * 2 + which) * 2 + r
                    sums = sums + jnp.where(index == slot, total[:, r * width : (r + 1) * width], 0.0)
        for step, o_ref in enumerate((mine_ref,) + others):
            start = pl.multiple_of((s_ref[2] + step) % quarters * own, own)
            for square in range(4 * LAYERS):
                part = all_ref[square, pl.ds(start, own), :]
                o_ref[square * own : (square + 1) * own] = part.astype(o_ref.dtype)
            o_ref[4 * LAYERS * own :] = sums.astype(o_ref.dtype)

    return pl.pallas_call(
        body,
        in_specs=[SMEM, VMEM],
        out_specs=[VMEM] * quarters,
        scratch_shapes=[pltpu.VMEM((4 * LAYERS, width, width), F32)],
        out_shape=[jax.ShapeDtypeStruct((count, width), F32)]
        + [jax.ShapeDtypeStruct((count, width), BF16)] * (quarters - 1),
        compiler_params=params(),
        name="gradient_parts",
    )(scalars, kept_values)


def gradient_sum(scalars, parts, width):
    quarters = len(parts)
    own = width // quarters
    half = 2 * LAYERS * own

    def body(s_ref, *refs):
        first_ref, second_ref, bias_ref = refs[quarters:]
        total = refs[0][...]
        for ref in refs[1:quarters]:
            total = total + ref[...].astype(F32)
        first_ref[...] = total[:half]
        second_ref[...] = total[half : 2 * half]
        sums = total[2 * half : 2 * half + 8]
        mine = sums[:, :own]
        for q in range(1, quarters):
            mine = jnp.where(s_ref[2] == q, sums[:, q * own : (q + 1) * own], mine)
        bias_ref[...] = mine

    return pl.pallas_call(
        body,
        in_specs=[SMEM] + [VMEM] * quarters,
        out_specs=[VMEM, VMEM, VMEM],
        out_shape=[
            jax.ShapeDtypeStruct((half, width), F32),
            jax.ShapeDtypeStruct((half, width), F32),
            jax.ShapeDtypeStruct((8, own), F32),
        ],
        compiler_params=params(),
        name="gradient_sum",
    )(scalars, *parts)


def on_device(section_input, handoff, loss_grad, w_first, w_second, bias, kept):
    lat_count = lax.axis_size("lat")
    sections = lax.axis_size("section")
    _, rows, lon, channels = section_input.shape
    width = w_first.shape[-1]
    blocks = channels // width
    quarters = lat_count // blocks
    lat = rows * lat_count
    forward = lon_table(lon, rows, quarters, False)
    inverse = lon_table(lon, rows, quarters, True)
    mixer = lat_table(lat, rows)
    place = lax.axis_index("lat")
    section = lax.axis_index("section")
    block = place // quarters
    limits = lax.dynamic_slice(kept, (0, 0, block), (1, LAYERS, 1)).reshape(-1)
    scalars = jnp.concatenate([jnp.stack([section, block, place % quarters]), limits])
    ring = [(s, (s - 1) % sections) for s in range(sections)]
    cells = (rows * lon, channels)

    handed_du = (handoff.reshape(cells), loss_grad.reshape(cells))
    du = to_spectral(section.reshape(1), handed_du, inverse, quarters, width)
    du = lax.ppermute(du, "section", ring)
    spec = to_spectral(section.reshape(1), (section_input.reshape(cells),), forward, quarters, width)
    both = jnp.concatenate([spec, du], axis=1)
    later, both = lax.optimization_barrier((handoff, both))
    both = lax.all_to_all(both, "lat", split_axis=0, concat_axis=0, tiled=True)
    received = lax.ppermute(later, "section", ring)
    cot = jnp.where(section == sections - 1, loss_grad, received[0]).reshape(cells)
    weights, biases = block_params(scalars, w_first, w_second, bias, width)
    da, values = spectral_chain(
        scalars, both, mixer, mixer.T.copy(), weights, biases, lat, width
    )
    da = lax.all_to_all(da, "lat", split_axis=0, concat_axis=0, tiled=True)
    parts = list(gradient_parts(scalars, values, quarters, width))
    for step in range(1, quarters):
        pairs = [
            (b * quarters + q, b * quarters + (q + step) % quarters)
            for b in range(blocks)
            for q in range(quarters)
        ]
        parts[step] = lax.ppermute(parts[step], "lat", pairs)
    handed = to_cells(da, forward.T.copy(), cot, quarters, width)
    handed, parts[0] = lax.optimization_barrier((handed, parts[0]))
    first, second, biases = gradient_sum(scalars, parts, width)
    own = width // quarters
    return (
        handed.reshape(1, rows, lon, channels),
        first.reshape(1, LAYERS, 2, own, width),
        second.reshape(1, LAYERS, 2, own, width),
        biases.reshape(1, LAYERS, 2, 2, own),
    )


def solution(mesh):
    return jax.shard_map(
        on_device,
        mesh=mesh,
        in_specs=(
            P("section", "lat", None, None),
            P("section", "lat", None, None),
            P("lat", None, None),
            P("section", None, None, None, None),
            P("section", None, None, None, None),
            P("section", None, None, None, None),
            P("section", None, None),
        ),
        out_specs=(
            P("section", "lat", None, None),
            P("section", None, None, "lat", None),
            P("section", None, None, "lat", None),
            P("section", None, None, None, "lat"),
        ),
        check_vma=False,
    )
```

```python
import math

import jax
import jax.numpy as jnp
import numpy as np
from jax import lax
from jax.experimental import pallas as pl
from jax.experimental.pallas import tpu as pltpu
from jax.sharding import PartitionSpec as P

LAYERS = 2
MAXK = 32
F32 = jnp.float32
BF16 = jnp.bfloat16


def lon_table(lon, rows, quarters, weighted):
    per = MAXK // quarters
    freqs = np.arange(MAXK)
    phase = 2.0 * math.pi * ((freqs[:, None] * np.arange(lon)[None, :]) % lon) / lon
    table = np.stack([np.cos(phase), -np.sin(phase)]) / math.sqrt(lon)
    table[1, 0] = 0.0
    table = table.astype(jnp.bfloat16).astype(np.float32)
    if weighted:
        table = table * np.where(freqs == 0, 1.0, 2.0)[None, :, None]
    split = table.reshape(2, quarters, per, lon).transpose(1, 0, 2, 3)
    full = np.zeros((quarters, 2, rows, per, rows, lon), np.float32)
    for row in range(rows):
        full[:, :, row, :, row, :] = split
    return full.reshape(quarters * 2 * rows * per, rows * lon).astype(jnp.bfloat16)


def lat_table(lat, rows):
    phase = 2.0 * math.pi * ((np.arange(lat)[:, None] * np.arange(lat)[None, :]) % lat) / lat
    cosine = np.cos(phase) / math.sqrt(lat)
    sine = np.sin(phase) / math.sqrt(lat)
    mixer = np.block([[cosine, sine], [-sine, cosine]])
    mixer = mixer.reshape(2 * lat, 2, lat // rows, rows).transpose(0, 2, 1, 3)
    return mixer.reshape(2 * lat, 2 * lat).astype(jnp.bfloat16)


def dot(left, right):
    return jnp.dot(left, right, preferred_element_type=F32)


def dot_rows(left, right):
    return lax.dot_general(left, right, (((1,), (1,)), ((), ())), preferred_element_type=F32)


def dot_cols(left, right):
    return lax.dot_general(left, right, (((0,), (0,)), ((), ())), preferred_element_type=F32)


def params(**kw):
    return pltpu.CompilerParams(vmem_limit_bytes=12 * 1024 * 1024, **kw)


VMEM = pl.BlockSpec(memory_space=pltpu.VMEM)
SMEM = pl.BlockSpec(memory_space=pltpu.SMEM)
HBM = pl.BlockSpec(memory_space=pltpu.HBM)


def in_hbm(value):
    return pltpu.with_memory_space_constraint(value, pltpu.HBM)


def to_spectral(scalars, sources, table, quarters, width):
    cells, channels = sources[0].shape
    rows = table.shape[0] // quarters
    blocks = channels // width
    cuts = 2
    span = cells // cuts

    def body(s_ref, t_hbm, *refs):
        given = refs[: len(sources)]
        o_ref, t_buf, x_buf, t_sem, x_sem = refs[len(sources) :]

        def piece(source, cut):
            part = pl.ds(cut * span, span)
            return pltpu.make_async_copy(source.at[part, :], x_buf.at[part, :], x_sem.at[cut])

        def begin(source):
            for cut in range(cuts):
                piece(source, cut).start()

        table_copy = pltpu.make_async_copy(t_hbm, t_buf, t_sem)
        table_copy.start()
        if len(given) == 1:
            begin(given[0])
        else:
            pl.when(s_ref[0] != 0)(lambda: begin(given[0]))
            pl.when(s_ref[0] == 0)(lambda: begin(given[1]))
        table_copy.wait()
        t = t_buf[...]
        for cut in range(cuts):
            piece(given[0], cut).wait()
        step = 2 * width
        for cut in range(channels // step):
            y = dot(t, x_buf[:, cut * step : (cut + 1) * step]).astype(BF16)
            for b in range(2):
                for q in range(quarters):
                    owner = (cut * 2 + b) * quarters + q
                    o_ref[owner] = y[q * rows : (q + 1) * rows, b * width : (b + 1) * width]

    return pl.pallas_call(
        body,
        in_specs=[SMEM, HBM] + [HBM] * len(sources),
        out_specs=VMEM,
        scratch_shapes=[
            pltpu.VMEM(table.shape, BF16),
            pltpu.VMEM((cells, channels), BF16),
            pltpu.SemaphoreType.DMA(()),
            pltpu.SemaphoreType.DMA((cuts,)),
        ],
        out_shape=jax.ShapeDtypeStruct((blocks * quarters, rows, width), BF16),
        compiler_params=params(),
        name="to_spectral",
    )(scalars, in_hbm(jnp.asarray(table)), *[in_hbm(source) for source in sources])


def to_cells(parts, table_t, grid_add, quarters, width):
    cells, channels = grid_add.shape
    rows = parts.shape[1]
    blocks = channels // width
    cuts = 2
    span = cells // cuts

    def body(t_ref, p_ref, g_ref, o_hbm, buf, sem):
        copies = []
        for cut in range(cuts):
            own = slice(cut * span, (cut + 1) * span)
            table = t_ref[own]
            for block in range(blocks):
                part = p_ref[block * quarters : (block + 1) * quarters]
                part = part.reshape(quarters * rows, width)
                lanes = slice(block * width, (block + 1) * width)
                mixed = g_ref[own, lanes].astype(F32) + dot(table, part)
                buf[own, lanes] = mixed.astype(BF16)
            copies.append(pltpu.make_async_copy(buf.at[own], o_hbm.at[own], sem.at[cut]))
            copies[-1].start()
        for copy in copies:
            copy.wait()

    return pl.pallas_call(
        body,
        in_specs=[VMEM, VMEM, VMEM],
        out_specs=HBM,
        scratch_shapes=[
            pltpu.VMEM((cells, channels), BF16),
            pltpu.SemaphoreType.DMA((cuts,)),
        ],
        out_shape=jax.ShapeDtypeStruct((cells, channels), BF16),
        compiler_params=params(),
        name="to_cells",
    )(table_t, parts, grid_add)


def block_params(scalars, w_first, w_second, bias, width):
    def body(s_ref, w1_hbm, w2_hbm, b_ref, w_ref, rows_ref, buf, sem):
        start = pl.multiple_of(s_ref[1] * width, width)
        copies = [
            pltpu.make_async_copy(w.at[0, :, :, pl.ds(start, width), :], buf.at[which], sem.at[which])
            for which, w in enumerate((w1_hbm, w2_hbm))
        ]
        for copy in copies:
            copy.start()
        for layer in range(LAYERS):
            for which in range(2):
                for r in range(2):
                    rows_ref[2 * layer + which, :, r * width : (r + 1) * width] = b_ref[
                        0, layer, which, pl.ds(r, 1), pl.ds(start, width)
                    ]
        for which in range(2):
            copies[which].wait()
            for layer in range(LAYERS):
                real, imag = (buf[which, layer, 0], buf[which, layer, 1])
                w_ref[2 * layer + which, :width, :width] = real
                w_ref[2 * layer + which, :width, width:] = imag
                w_ref[2 * layer + which, width:, :width] = -imag
                w_ref[2 * layer + which, width:, width:] = real

    return pl.pallas_call(
        body,
        in_specs=[SMEM, HBM, HBM, VMEM],
        out_specs=[VMEM, VMEM],
        scratch_shapes=[
            pltpu.VMEM((2, LAYERS, 2, width, width), BF16),
            pltpu.SemaphoreType.DMA((2,)),
        ],
        out_shape=[
            jax.ShapeDtypeStruct((2 * LAYERS, 2 * width, 2 * width), BF16),
            jax.ShapeDtypeStruct((2 * LAYERS, 1, 2 * width), F32),
        ],
        compiler_params=params(),
        name="block_params",
    )(scalars, in_hbm(w_first), in_hbm(w_second), bias)


def spectral_chain(scalars, parts, mixer, mixer_t, weights, biases, lat, width, quarters):
    sources, both, _ = parts.shape
    chunk = (sources, both // 2, width)
    per = sources * (both // 2) // (2 * lat)
    tall = per * lat

    own = width // quarters
    count = 4 * LAYERS * own + 16

    def body(s_ref, parts_ref, l_ref, lt_ref, w_ref, b_ref, da_ref, mine_ref, send_ref, tmp, all_ref):
        quarter = s_ref[2]
        mix, mix_t = (l_ref[...], lt_ref[...])

        def mixed(slot):
            part = parts_ref[:, slot * (both // 2) : (slot + 1) * (both // 2), :]
            tmp[slot] = part.reshape(2 * lat * per, width).astype(F32)
            cells = []
            for k in range(per):
                column = tmp[slot, pl.ds(k, 2 * lat, stride=per), :].astype(BF16)
                z = dot(mix, column)
                cells.append(jnp.concatenate([z[:lat], z[lat:]], axis=1))
            return jnp.concatenate(cells, axis=0)

        rows = lax.broadcasted_iota(jnp.int32, (lat, lat), 0)
        cols = lax.broadcasted_iota(jnp.int32, (lat, lat), 1)
        eye = (rows == cols).astype(F32)
        back = ((rows + cols) % lat == 0).astype(F32)
        has_zero = (quarter == 0).astype(F32)
        even = (eye + 0.5 * has_zero * (back - eye)).astype(BF16)
        odd = (eye - 0.5 * has_zero * (back + eye)).astype(BF16)

        def through_grid(v):
            first = v[:lat]
            first = jnp.concatenate(
                [dot(even, first[:, :width]), dot(odd, first[:, width:])], axis=1
            )
            return jnp.concatenate([first, v[lat:].astype(F32)], axis=0)

        def mask_of(layer):
            mode = quarter * per + lax.broadcasted_iota(jnp.int32, (tall, 1), 0) // lat
            return (mode < s_ref[3 + layer]).astype(F32)

        z = mixed(0)
        slopes = []
        lefts = {}
        index = lax.broadcasted_iota(jnp.int32, (16, width), 0)
        sums = jnp.zeros((16, width), F32)

        def products(which, layer, right, sums):
            outer = dot_cols(lefts[which, layer], right)
            total = jnp.sum(right.astype(F32), axis=0, keepdims=True)
            squares = (
                outer[:width, :width] + outer[width:, width:],
                outer[:width, width:] - outer[width:, :width],
            )
            for r in range(2):
                all_ref[(which * LAYERS + layer) * 2 + r] = squares[r]
                slot = (layer * 2 + which) * 2 + r
                sums = sums + jnp.where(index == slot, total[:, r * width : (r + 1) * width], 0.0)
            return sums

        for layer in range(LAYERS):
            z_low = z.astype(BF16)
            lefts[0, layer] = z_low
            pre = dot(z_low, w_ref[2 * layer]) + b_ref[2 * layer]
            sig = jax.nn.sigmoid(pre)
            hidden = (pre * sig).astype(BF16)
            lefts[1, layer] = hidden
            slopes.append(sig * (1.0 + pre * (1.0 - sig)))
            if layer + 1 < LAYERS:
                out = dot(hidden, w_ref[2 * layer + 1]) + b_ref[2 * layer + 1]
                z = z + through_grid((out * mask_of(layer)).astype(BF16))
        grad = mixed(1)
        total = None
        for layer in reversed(range(LAYERS)):
            dout = (grad * mask_of(layer)).astype(BF16)
            sums = products(1, layer, dout, sums)
            dpre = (dot_rows(dout, w_ref[2 * layer + 1]) * slopes[layer]).astype(BF16)
            sums = products(0, layer, dpre, sums)
            dz = dot_rows(dpre, w_ref[2 * layer])
            if layer:
                grad = grad + through_grid(dz.astype(BF16))
            total = dz if total is None else total + dz
        total = total.astype(BF16)
        for k in range(per):
            part = total[k * lat : (k + 1) * lat]
            part = jnp.concatenate([part[:, :width], part[:, width:]], axis=0)
            tmp[0, pl.ds(k, 2 * lat, stride=per), :] = dot(mix_t, part)
        da_ref[...] = tmp[0].astype(BF16).reshape(chunk)
        targets = (quarter, quarter ^ 2, quarter ^ 1, quarter ^ 3)
        for slot, target in enumerate(targets):
            o_ref = (mine_ref, send_ref)[slot // 2].at[slot % 2]
            start = pl.multiple_of(target * own, own)
            for square in range(4 * LAYERS):
                part = all_ref[square, pl.ds(start, own), :]
                o_ref[square * own : (square + 1) * own] = part.astype(o_ref.dtype)
            o_ref[4 * LAYERS * own :] = sums.astype(o_ref.dtype)

    return pl.pallas_call(
        body,
        in_specs=[SMEM] + [VMEM] * 5,
        out_specs=[VMEM] * 3,
        scratch_shapes=[
            pltpu.VMEM((2, 2 * lat * per, width), F32),
            pltpu.VMEM((4 * LAYERS, width, width), F32),
        ],
        out_shape=[
            jax.ShapeDtypeStruct(chunk, BF16),
            jax.ShapeDtypeStruct((2, count, width), F32),
            jax.ShapeDtypeStruct((2, count, width), BF16),
        ],
        compiler_params=params(),
        name="spectral_chain",
    )(scalars, parts, mixer, mixer_t, weights, biases)


def gradient_sum(scalars, mine, near, far, width, quarters):
    own = width // quarters
    half = 2 * LAYERS * own

    def body(s_ref, mine_ref, near_ref, far_ref, first_ref, second_ref, bias_ref):
        total = mine_ref[0] + near_ref[0].astype(F32) + far_ref[...].astype(F32)
        first_ref[...] = total[:half]
        second_ref[...] = total[half : 2 * half]
        sums = total[2 * half : 2 * half + 8]
        part = sums[:, :own]
        for q in range(1, quarters):
            part = jnp.where(s_ref[2] == q, sums[:, q * own : (q + 1) * own], part)
        bias_ref[...] = part

    return pl.pallas_call(
        body,
        in_specs=[SMEM, VMEM, VMEM, VMEM],
        out_specs=[VMEM, VMEM, VMEM],
        out_shape=[
            jax.ShapeDtypeStruct((half, width), F32),
            jax.ShapeDtypeStruct((half, width), F32),
            jax.ShapeDtypeStruct((8, own), F32),
        ],
        compiler_params=params(),
        name="gradient_sum",
    )(scalars, mine, near, far)


def on_device(section_input, handoff, loss_grad, w_first, w_second, bias, kept):
    lat_count = lax.axis_size("lat")
    sections = lax.axis_size("section")
    _, rows, lon, channels = section_input.shape
    width = w_first.shape[-1]
    blocks = channels // width
    quarters = lat_count // blocks
    lat = rows * lat_count
    forward = lon_table(lon, rows, quarters, False)
    inverse = lon_table(lon, rows, quarters, True)
    mixer = lat_table(lat, rows)
    place = lax.axis_index("lat")
    section = lax.axis_index("section")
    block = place // quarters
    limits = lax.dynamic_slice(kept, (0, 0, block), (1, LAYERS, 1)).reshape(-1)
    scalars = jnp.concatenate([jnp.stack([section, block, place % quarters]), limits])
    ring = [(s, (s - 1) % sections) for s in range(sections)]
    cells = (rows * lon, channels)

    handed_du = (handoff.reshape(cells), loss_grad.reshape(cells))
    du = to_spectral(section.reshape(1), handed_du, inverse, quarters, width)
    du = lax.ppermute(du, "section", ring)
    spec = to_spectral(section.reshape(1), (section_input.reshape(cells),), forward, quarters, width)
    both = jnp.concatenate([spec, du], axis=1)
    later, both = lax.optimization_barrier((handoff, both))
    both = lax.all_to_all(both, "lat", split_axis=0, concat_axis=0, tiled=True)
    received = lax.ppermute(later, "section", ring)
    cot = jnp.where(section == sections - 1, loss_grad, received[0]).reshape(cells)
    weights, biases = block_params(scalars, w_first, w_second, bias, width)
    cot, both = lax.optimization_barrier((cot, both))
    da, mine, send = spectral_chain(
        scalars, both, mixer, mixer.T.copy(), weights, biases, lat, width, quarters
    )

    def swapped(value, bit):
        return lax.ppermute(value, "lat", [(d, d ^ bit) for d in range(lat_count)])

    near = swapped(send, 1)
    da = lax.all_to_all(da, "lat", split_axis=0, concat_axis=0, tiled=True)
    far = swapped((mine[1] + near[1].astype(F32)).astype(BF16), 2)
    first, second, biases = gradient_sum(scalars, mine, near, far, width, quarters)
    handed = to_cells(da, forward.T.copy(), cot, quarters, width)
    own = width // quarters
    return (
        handed.reshape(1, rows, lon, channels),
        first.reshape(1, LAYERS, 2, own, width),
        second.reshape(1, LAYERS, 2, own, width),
        biases.reshape(1, LAYERS, 2, 2, own),
    )


def solution(mesh):
    return jax.shard_map(
        on_device,
        mesh=mesh,
        in_specs=(
            P("section", "lat", None, None),
            P("section", "lat", None, None),
            P("lat", None, None),
            P("section", None, None, None, None),
            P("section", None, None, None, None),
            P("section", None, None, None, None),
            P("section", None, None),
        ),
        out_specs=(
            P("section", "lat", None, None),
            P("section", None, None, "lat", None),
            P("section", None, None, "lat", None),
            P("section", None, None, None, "lat"),
        ),
        check_vma=False,
    )
```

```python
import math

import jax
import jax.numpy as jnp
import numpy as np
from jax import lax
from jax.experimental import pallas as pl
from jax.experimental.pallas import tpu as pltpu
from jax.sharding import PartitionSpec as P

LAYERS = 2
MAXK = 32
F32 = jnp.float32
BF16 = jnp.bfloat16


def lon_table(lon, rows, quarters, weighted):
    per = MAXK // quarters
    freqs = np.arange(MAXK)
    phase = 2.0 * math.pi * ((freqs[:, None] * np.arange(lon)[None, :]) % lon) / lon
    table = np.stack([np.cos(phase), -np.sin(phase)]) / math.sqrt(lon)
    table[1, 0] = 0.0
    table = table.astype(jnp.bfloat16).astype(np.float32)
    if weighted:
        table = table * np.where(freqs == 0, 1.0, 2.0)[None, :, None]
    split = table.reshape(2, quarters, per, lon).transpose(1, 0, 2, 3)
    full = np.zeros((quarters, 2, rows, per, rows, lon), np.float32)
    for row in range(rows):
        full[:, :, row, :, row, :] = split
    return full.reshape(quarters * 2 * rows * per, rows * lon).astype(jnp.bfloat16)


def lat_table(lat, rows):
    phase = 2.0 * math.pi * ((np.arange(lat)[:, None] * np.arange(lat)[None, :]) % lat) / lat
    cosine = np.cos(phase) / math.sqrt(lat)
    sine = np.sin(phase) / math.sqrt(lat)
    mixer = np.block([[cosine, sine], [-sine, cosine]])
    mixer = mixer.reshape(2 * lat, 2, lat // rows, rows).transpose(0, 2, 1, 3)
    return mixer.reshape(2 * lat, 2 * lat).astype(jnp.bfloat16)


def dot(left, right):
    return jnp.dot(left, right, preferred_element_type=F32)


def dot_rows(left, right):
    return lax.dot_general(left, right, (((1,), (1,)), ((), ())), preferred_element_type=F32)


def dot_cols(left, right):
    return lax.dot_general(left, right, (((0,), (0,)), ((), ())), preferred_element_type=F32)


def params(**kw):
    return pltpu.CompilerParams(vmem_limit_bytes=12 * 1024 * 1024, **kw)


VMEM = pl.BlockSpec(memory_space=pltpu.VMEM)
SMEM = pl.BlockSpec(memory_space=pltpu.SMEM)
HBM = pl.BlockSpec(memory_space=pltpu.HBM)


def in_hbm(value):
    return pltpu.with_memory_space_constraint(value, pltpu.HBM)


def to_spectral(scalars, sources, table, quarters, width):
    cells, channels = sources[0].shape
    rows = table.shape[0] // quarters
    blocks = channels // width
    cuts = 2
    span = cells // cuts

    def body(s_ref, t_hbm, *refs):
        given = refs[: len(sources)]
        o_ref, t_buf, x_buf, t_sem, x_sem = refs[len(sources) :]

        def piece(source, cut):
            part = pl.ds(cut * span, span)
            return pltpu.make_async_copy(source.at[part, :], x_buf.at[part, :], x_sem.at[cut])

        def begin(source):
            for cut in range(cuts):
                piece(source, cut).start()

        table_copy = pltpu.make_async_copy(t_hbm, t_buf, t_sem)
        table_copy.start()
        if len(given) == 1:
            begin(given[0])
        else:
            pl.when(s_ref[0] != 0)(lambda: begin(given[0]))
            pl.when(s_ref[0] == 0)(lambda: begin(given[1]))
        table_copy.wait()
        t = t_buf[...]
        for cut in range(cuts):
            piece(given[0], cut).wait()
        step = 2 * width
        for cut in range(channels // step):
            y = dot(t, x_buf[:, cut * step : (cut + 1) * step]).astype(BF16)
            for b in range(2):
                for q in range(quarters):
                    owner = (cut * 2 + b) * quarters + q
                    o_ref[owner] = y[q * rows : (q + 1) * rows, b * width : (b + 1) * width]

    return pl.pallas_call(
        body,
        in_specs=[SMEM, HBM] + [HBM] * len(sources),
        out_specs=VMEM,
        scratch_shapes=[
            pltpu.VMEM(table.shape, BF16),
            pltpu.VMEM((cells, channels), BF16),
            pltpu.SemaphoreType.DMA(()),
            pltpu.SemaphoreType.DMA((cuts,)),
        ],
        out_shape=jax.ShapeDtypeStruct((blocks * quarters, rows, width), BF16),
        compiler_params=params(),
        name="to_spectral",
    )(scalars, in_hbm(jnp.asarray(table)), *[in_hbm(source) for source in sources])


def to_cells(parts, table_t, grid_add, quarters, width):
    cells, channels = grid_add.shape
    rows = parts.shape[1]
    blocks = channels // width
    cuts = 2
    span = cells // cuts

    def body(t_ref, p_ref, g_ref, o_hbm, buf, sem):
        copies = []
        for cut in range(cuts):
            own = slice(cut * span, (cut + 1) * span)
            table = t_ref[own]
            for block in range(blocks):
                part = p_ref[block * quarters : (block + 1) * quarters]
                part = part.reshape(quarters * rows, width)
                lanes = slice(block * width, (block + 1) * width)
                mixed = g_ref[own, lanes].astype(F32) + dot(table, part)
                buf[own, lanes] = mixed.astype(BF16)
            copies.append(pltpu.make_async_copy(buf.at[own], o_hbm.at[own], sem.at[cut]))
            copies[-1].start()
        for copy in copies:
            copy.wait()

    return pl.pallas_call(
        body,
        in_specs=[VMEM, VMEM, VMEM],
        out_specs=HBM,
        scratch_shapes=[
            pltpu.VMEM((cells, channels), BF16),
            pltpu.SemaphoreType.DMA((cuts,)),
        ],
        out_shape=jax.ShapeDtypeStruct((cells, channels), BF16),
        compiler_params=params(),
        name="to_cells",
    )(table_t, parts, grid_add)


def block_params(scalars, w_first, w_second, bias, width):
    def body(s_ref, w1_hbm, w2_hbm, b_ref, w_ref, rows_ref, buf, sem):
        start = pl.multiple_of(s_ref[1] * width, width)
        copies = [
            pltpu.make_async_copy(w.at[0, :, :, pl.ds(start, width), :], buf.at[which], sem.at[which])
            for which, w in enumerate((w1_hbm, w2_hbm))
        ]
        for copy in copies:
            copy.start()
        for layer in range(LAYERS):
            for which in range(2):
                for r in range(2):
                    rows_ref[2 * layer + which, :, r * width : (r + 1) * width] = b_ref[
                        0, layer, which, pl.ds(r, 1), pl.ds(start, width)
                    ]
        for which in range(2):
            copies[which].wait()
            for layer in range(LAYERS):
                real, imag = (buf[which, layer, 0], buf[which, layer, 1])
                w_ref[2 * layer + which, :width, :width] = real
                w_ref[2 * layer + which, :width, width:] = imag
                w_ref[2 * layer + which, width:, :width] = -imag
                w_ref[2 * layer + which, width:, width:] = real

    return pl.pallas_call(
        body,
        in_specs=[SMEM, HBM, HBM, VMEM],
        out_specs=[VMEM, VMEM],
        scratch_shapes=[
            pltpu.VMEM((2, LAYERS, 2, width, width), BF16),
            pltpu.SemaphoreType.DMA((2,)),
        ],
        out_shape=[
            jax.ShapeDtypeStruct((2 * LAYERS, 2 * width, 2 * width), BF16),
            jax.ShapeDtypeStruct((2 * LAYERS, 1, 2 * width), F32),
        ],
        compiler_params=params(),
        name="block_params",
    )(scalars, in_hbm(w_first), in_hbm(w_second), bias)


def spectral_chain(scalars, parts, mixer, mixer_t, weights, biases, lat, width, quarters):
    sources, both, _ = parts.shape
    chunk = (sources, both // 2, width)
    per = sources * (both // 2) // (2 * lat)
    tall = per * lat

    own = width // quarters
    count = 4 * LAYERS * own + 16

    def body(s_ref, parts_ref, l_ref, lt_ref, w_ref, b_ref, da_ref, *rest):
        mine_and_sent, tmp, all_ref = (rest[:quarters], rest[quarters], rest[quarters + 1])
        quarter = s_ref[2]
        mix, mix_t = (l_ref[...], lt_ref[...])

        def mixed(slot):
            part = parts_ref[:, slot * (both // 2) : (slot + 1) * (both // 2), :]
            tmp[slot] = part.reshape(2 * lat * per, width).astype(F32)
            cells = []
            for k in range(per):
                column = tmp[slot, pl.ds(k, 2 * lat, stride=per), :].astype(BF16)
                z = dot(mix, column)
                cells.append(jnp.concatenate([z[:lat], z[lat:]], axis=1))
            return jnp.concatenate(cells, axis=0)

        rows = lax.broadcasted_iota(jnp.int32, (lat, lat), 0)
        cols = lax.broadcasted_iota(jnp.int32, (lat, lat), 1)
        eye = (rows == cols).astype(F32)
        back = ((rows + cols) % lat == 0).astype(F32)
        has_zero = (quarter == 0).astype(F32)
        even = (eye + 0.5 * has_zero * (back - eye)).astype(BF16)
        odd = (eye - 0.5 * has_zero * (back + eye)).astype(BF16)

        def through_grid(v):
            first = v[:lat]
            first = jnp.concatenate(
                [dot(even, first[:, :width]), dot(odd, first[:, width:])], axis=1
            )
            return jnp.concatenate([first, v[lat:].astype(F32)], axis=0)

        def mask_of(layer):
            mode = quarter * per + lax.broadcasted_iota(jnp.int32, (tall, 1), 0) // lat
            return (mode < s_ref[3 + layer]).astype(F32)

        z = mixed(0)
        slopes = []
        lefts = {}
        index = lax.broadcasted_iota(jnp.int32, (16, width), 0)
        sums = jnp.zeros((16, width), F32)

        def products(which, layer, right, sums):
            outer = dot_cols(lefts[which, layer], right)
            total = jnp.sum(right.astype(F32), axis=0, keepdims=True)
            squares = (
                outer[:width, :width] + outer[width:, width:],
                outer[:width, width:] - outer[width:, :width],
            )
            for r in range(2):
                all_ref[(which * LAYERS + layer) * 2 + r] = squares[r]
                slot = (layer * 2 + which) * 2 + r
                sums = sums + jnp.where(index == slot, total[:, r * width : (r + 1) * width], 0.0)
            return sums

        for layer in range(LAYERS):
            z_low = z.astype(BF16)
            lefts[0, layer] = z_low
            pre = dot(z_low, w_ref[2 * layer]) + b_ref[2 * layer]
            sig = jax.nn.sigmoid(pre)
            hidden = (pre * sig).astype(BF16)
            lefts[1, layer] = hidden
            slopes.append(sig * (1.0 + pre * (1.0 - sig)))
            if layer + 1 < LAYERS:
                out = dot(hidden, w_ref[2 * layer + 1]) + b_ref[2 * layer + 1]
                z = z + through_grid((out * mask_of(layer)).astype(BF16))
        grad = mixed(1)
        total = None
        for layer in reversed(range(LAYERS)):
            dout = (grad * mask_of(layer)).astype(BF16)
            sums = products(1, layer, dout, sums)
            dpre = (dot_rows(dout, w_ref[2 * layer + 1]) * slopes[layer]).astype(BF16)
            sums = products(0, layer, dpre, sums)
            dz = dot_rows(dpre, w_ref[2 * layer])
            if layer:
                grad = grad + through_grid(dz.astype(BF16))
            total = dz if total is None else total + dz
        total = total.astype(BF16)
        for k in range(per):
            part = total[k * lat : (k + 1) * lat]
            part = jnp.concatenate([part[:, :width], part[:, width:]], axis=0)
            tmp[0, pl.ds(k, 2 * lat, stride=per), :] = dot(mix_t, part)
        da_ref[...] = tmp[0].astype(BF16).reshape(chunk)
        for step, o_ref in enumerate(mine_and_sent):
            start = pl.multiple_of((quarter + step) % quarters * own, own)
            for square in range(4 * LAYERS):
                part = all_ref[square, pl.ds(start, own), :]
                o_ref[square * own : (square + 1) * own] = part.astype(o_ref.dtype)
            o_ref[4 * LAYERS * own :] = sums.astype(o_ref.dtype)

    return pl.pallas_call(
        body,
        in_specs=[SMEM] + [VMEM] * 5,
        out_specs=[VMEM] * (1 + quarters),
        scratch_shapes=[
            pltpu.VMEM((2, 2 * lat * per, width), F32),
            pltpu.VMEM((4 * LAYERS, width, width), F32),
        ],
        out_shape=[
            jax.ShapeDtypeStruct(chunk, BF16),
            jax.ShapeDtypeStruct((count, width), F32),
        ]
        + [jax.ShapeDtypeStruct((count, width), BF16)] * (quarters - 1),
        compiler_params=params(),
        name="spectral_chain",
    )(scalars, parts, mixer, mixer_t, weights, biases)


def gradient_sum(scalars, parts, width):
    quarters = len(parts)
    own = width // quarters
    half = 2 * LAYERS * own

    def body(s_ref, *refs):
        first_hbm, second_hbm, bias_hbm, buf, bias_buf, sem = refs[quarters:]

        def added(start, size):
            total = refs[0][start : start + size]
            for ref in refs[1:quarters]:
                total = total + ref[start : start + size].astype(F32)
            return total

        copies = [
            pltpu.make_async_copy(bias_buf, bias_hbm, sem.at[2]),
            pltpu.make_async_copy(buf.at[0], first_hbm, sem.at[0]),
            pltpu.make_async_copy(buf.at[1], second_hbm, sem.at[1]),
        ]
        sums = added(2 * half, 16)[:8]
        part = sums[:, :own]
        for q in range(1, quarters):
            part = jnp.where(s_ref[2] == q, sums[:, q * own : (q + 1) * own], part)
        bias_buf[...] = part
        copies[0].start()
        for which in range(2):
            buf[which] = added(which * half, half)
            copies[1 + which].start()
        for copy in copies:
            copy.wait()

    return pl.pallas_call(
        body,
        in_specs=[SMEM] + [VMEM] * quarters,
        out_specs=[HBM] * 3,
        scratch_shapes=[
            pltpu.VMEM((2, half, width), F32),
            pltpu.VMEM((8, own), F32),
            pltpu.SemaphoreType.DMA((3,)),
        ],
        out_shape=[
            jax.ShapeDtypeStruct((half, width), F32),
            jax.ShapeDtypeStruct((half, width), F32),
            jax.ShapeDtypeStruct((8, own), F32),
        ],
        compiler_params=params(),
        name="gradient_sum",
    )(scalars, *parts)


def on_device(section_input, handoff, loss_grad, w_first, w_second, bias, kept):
    lat_count = lax.axis_size("lat")
    sections = lax.axis_size("section")
    _, rows, lon, channels = section_input.shape
    width = w_first.shape[-1]
    blocks = channels // width
    quarters = lat_count // blocks
    lat = rows * lat_count
    forward = lon_table(lon, rows, quarters, False)
    inverse = lon_table(lon, rows, quarters, True)
    mixer = lat_table(lat, rows)
    place = lax.axis_index("lat")
    section = lax.axis_index("section")
    block = place // quarters
    limits = lax.dynamic_slice(kept, (0, 0, block), (1, LAYERS, 1)).reshape(-1)
    scalars = jnp.concatenate([jnp.stack([section, block, place % quarters]), limits])
    ring = [(s, (s - 1) % sections) for s in range(sections)]
    cells = (rows * lon, channels)

    handed_du = (handoff.reshape(cells), loss_grad.reshape(cells))
    du = to_spectral(section.reshape(1), handed_du, inverse, quarters, width)
    du = lax.ppermute(du, "section", ring)
    spec = to_spectral(section.reshape(1), (section_input.reshape(cells),), forward, quarters, width)
    later, spec = lax.optimization_barrier((handoff, spec))
    both = jnp.concatenate([spec, du], axis=1)
    both = lax.all_to_all(both, "lat", split_axis=0, concat_axis=0, tiled=True)
    received = lax.ppermute(later, "section", ring)
    cot = jnp.where(section == sections - 1, loss_grad, received[0]).reshape(cells)
    weights, biases = block_params(scalars, w_first, w_second, bias, width)
    cot, both = lax.optimization_barrier((cot, both))
    da, *parts = spectral_chain(
        scalars, both, mixer, mixer.T.copy(), weights, biases, lat, width, quarters
    )
    da = lax.all_to_all(da, "lat", split_axis=0, concat_axis=0, tiled=True)
    for step in range(1, quarters):
        pairs = [
            (b * quarters + q, b * quarters + (q + step) % quarters)
            for b in range(blocks)
            for q in range(quarters)
        ]
        parts[step] = lax.ppermute(parts[step], "lat", pairs)
    handed = to_cells(da, forward.T.copy(), cot, quarters, width)
    handed, parts[0] = lax.optimization_barrier((handed, parts[0]))
    first, second, biases = gradient_sum(scalars, parts, width)
    own = width // quarters
    return (
        handed.reshape(1, rows, lon, channels),
        first.reshape(1, LAYERS, 2, own, width),
        second.reshape(1, LAYERS, 2, own, width),
        biases.reshape(1, LAYERS, 2, 2, own),
    )


def solution(mesh):
    return jax.shard_map(
        on_device,
        mesh=mesh,
        in_specs=(
            P("section", "lat", None, None),
            P("section", "lat", None, None),
            P("lat", None, None),
            P("section", None, None, None, None),
            P("section", None, None, None, None),
            P("section", None, None, None, None),
            P("section", None, None),
        ),
        out_specs=(
            P("section", "lat", None, None),
            P("section", None, None, "lat", None),
            P("section", None, None, "lat", None),
            P("section", None, None, None, "lat"),
        ),
        check_vma=False,
    )
```

```python
import math

import jax
import jax.numpy as jnp
import numpy as np
from jax import lax
from jax.experimental import pallas as pl
from jax.experimental.pallas import tpu as pltpu
from jax.sharding import PartitionSpec as P

LAYERS = 2
MAXK = 32
F32 = jnp.float32
BF16 = jnp.bfloat16


def lon_table(lon, rows, quarters, weighted):
    per = MAXK // quarters
    freqs = np.arange(MAXK)
    phase = 2.0 * math.pi * ((freqs[:, None] * np.arange(lon)[None, :]) % lon) / lon
    table = np.stack([np.cos(phase), -np.sin(phase)]) / math.sqrt(lon)
    table[1, 0] = 0.0
    table = table.astype(jnp.bfloat16).astype(np.float32)
    if weighted:
        table = table * np.where(freqs == 0, 1.0, 2.0)[None, :, None]
    split = table.reshape(2, quarters, per, lon).transpose(1, 0, 2, 3)
    full = np.zeros((quarters, 2, rows, per, rows, lon), np.float32)
    for row in range(rows):
        full[:, :, row, :, row, :] = split
    return full.reshape(quarters * 2 * rows * per, rows * lon).astype(jnp.bfloat16)


def lat_table(lat, rows):
    phase = 2.0 * math.pi * ((np.arange(lat)[:, None] * np.arange(lat)[None, :]) % lat) / lat
    cosine = np.cos(phase) / math.sqrt(lat)
    sine = np.sin(phase) / math.sqrt(lat)
    mixer = np.block([[cosine, sine], [-sine, cosine]])
    mixer = mixer.reshape(2 * lat, 2, lat // rows, rows).transpose(0, 2, 1, 3)
    return mixer.reshape(2 * lat, 2 * lat).astype(jnp.bfloat16)


def dot(left, right):
    return jnp.dot(left, right, preferred_element_type=F32)


def dot_rows(left, right):
    return lax.dot_general(left, right, (((1,), (1,)), ((), ())), preferred_element_type=F32)


def dot_cols(left, right):
    return lax.dot_general(left, right, (((0,), (0,)), ((), ())), preferred_element_type=F32)


def params(**kw):
    return pltpu.CompilerParams(vmem_limit_bytes=12 * 1024 * 1024, **kw)


VMEM = pl.BlockSpec(memory_space=pltpu.VMEM)
SMEM = pl.BlockSpec(memory_space=pltpu.SMEM)
HBM = pl.BlockSpec(memory_space=pltpu.HBM)


def in_hbm(value):
    return pltpu.with_memory_space_constraint(value, pltpu.HBM)


def to_spectral(scalars, sources, table, quarters, width):
    cells, channels = sources[0].shape
    rows = table.shape[0] // quarters
    blocks = channels // width
    cuts = 2
    span = cells // cuts

    def body(s_ref, t_hbm, *refs):
        given = refs[: len(sources)]
        o_ref, t_buf, x_buf, t_sem, x_sem = refs[len(sources) :]

        def piece(source, cut):
            part = pl.ds(cut * span, span)
            return pltpu.make_async_copy(source.at[part, :], x_buf.at[part, :], x_sem.at[cut])

        def begin(source):
            for cut in range(cuts):
                piece(source, cut).start()

        table_copy = pltpu.make_async_copy(t_hbm, t_buf, t_sem)
        table_copy.start()
        if len(given) == 1:
            begin(given[0])
        else:
            pl.when(s_ref[0] != 0)(lambda: begin(given[0]))
            pl.when(s_ref[0] == 0)(lambda: begin(given[1]))
        table_copy.wait()
        t = t_buf[...]
        for cut in range(cuts):
            piece(given[0], cut).wait()
        step = 2 * width
        for cut in range(channels // step):
            y = dot(t, x_buf[:, cut * step : (cut + 1) * step]).astype(BF16)
            for b in range(2):
                for q in range(quarters):
                    owner = (cut * 2 + b) * quarters + q
                    o_ref[owner] = y[q * rows : (q + 1) * rows, b * width : (b + 1) * width]

    return pl.pallas_call(
        body,
        in_specs=[SMEM, HBM] + [HBM] * len(sources),
        out_specs=VMEM,
        scratch_shapes=[
            pltpu.VMEM(table.shape, BF16),
            pltpu.VMEM((cells, channels), BF16),
            pltpu.SemaphoreType.DMA(()),
            pltpu.SemaphoreType.DMA((cuts,)),
        ],
        out_shape=jax.ShapeDtypeStruct((blocks * quarters, rows, width), BF16),
        compiler_params=params(),
        name="to_spectral",
    )(scalars, in_hbm(jnp.asarray(table)), *[in_hbm(source) for source in sources])


def to_cells(parts, table_t, grid_add, quarters, width):
    cells, channels = grid_add.shape
    rows = parts.shape[1]
    blocks = channels // width
    cuts = 2
    span = cells // cuts

    def body(t_ref, p_ref, g_ref, o_hbm, buf, sem):
        copies = []
        for cut in range(cuts):
            own = slice(cut * span, (cut + 1) * span)
            table = t_ref[own]
            for block in range(blocks):
                part = p_ref[block * quarters : (block + 1) * quarters]
                part = part.reshape(quarters * rows, width)
                lanes = slice(block * width, (block + 1) * width)
                mixed = g_ref[own, lanes].astype(F32) + dot(table, part)
                buf[own, lanes] = mixed.astype(BF16)
            copies.append(pltpu.make_async_copy(buf.at[own], o_hbm.at[own], sem.at[cut]))
            copies[-1].start()
        for copy in copies:
            copy.wait()

    return pl.pallas_call(
        body,
        in_specs=[VMEM, VMEM, VMEM],
        out_specs=HBM,
        scratch_shapes=[
            pltpu.VMEM((cells, channels), BF16),
            pltpu.SemaphoreType.DMA((cuts,)),
        ],
        out_shape=jax.ShapeDtypeStruct((cells, channels), BF16),
        compiler_params=params(),
        name="to_cells",
    )(table_t, parts, grid_add)


def block_params(scalars, w_first, w_second, bias, width):
    def body(s_ref, w1_hbm, w2_hbm, b_ref, w_ref, rows_ref, buf, sem):
        start = pl.multiple_of(s_ref[1] * width, width)
        copies = [
            pltpu.make_async_copy(w.at[0, :, :, pl.ds(start, width), :], buf.at[which], sem.at[which])
            for which, w in enumerate((w1_hbm, w2_hbm))
        ]
        for copy in copies:
            copy.start()
        for layer in range(LAYERS):
            for which in range(2):
                for r in range(2):
                    rows_ref[2 * layer + which, :, r * width : (r + 1) * width] = b_ref[
                        0, layer, which, pl.ds(r, 1), pl.ds(start, width)
                    ]
        for which in range(2):
            copies[which].wait()
            for layer in range(LAYERS):
                real, imag = (buf[which, layer, 0], buf[which, layer, 1])
                w_ref[2 * layer + which, :width, :width] = real
                w_ref[2 * layer + which, :width, width:] = imag
                w_ref[2 * layer + which, width:, :width] = -imag
                w_ref[2 * layer + which, width:, width:] = real

    return pl.pallas_call(
        body,
        in_specs=[SMEM, HBM, HBM, VMEM],
        out_specs=[VMEM, VMEM],
        scratch_shapes=[
            pltpu.VMEM((2, LAYERS, 2, width, width), BF16),
            pltpu.SemaphoreType.DMA((2,)),
        ],
        out_shape=[
            jax.ShapeDtypeStruct((2 * LAYERS, 2 * width, 2 * width), BF16),
            jax.ShapeDtypeStruct((2 * LAYERS, 1, 2 * width), F32),
        ],
        compiler_params=params(),
        name="block_params",
    )(scalars, in_hbm(w_first), in_hbm(w_second), bias)


def spectral_chain(scalars, parts, mixer, mixer_t, weights, biases, lat, width, quarters):
    sources, both, _ = parts.shape
    chunk = (sources, both // 2, width)
    per = sources * (both // 2) // (2 * lat)
    tall = per * lat

    own = width // quarters
    count = 4 * LAYERS * own + 16

    def body(s_ref, parts_ref, l_ref, lt_ref, w_ref, b_ref, da_ref, send_ref, tmp, all_ref):
        quarter = s_ref[2]
        mix, mix_t = (l_ref[...], lt_ref[...])

        def mixed(slot):
            part = parts_ref[:, slot * (both // 2) : (slot + 1) * (both // 2), :]
            tmp[slot] = part.reshape(2 * lat * per, width).astype(F32)
            cells = []
            for k in range(per):
                column = tmp[slot, pl.ds(k, 2 * lat, stride=per), :].astype(BF16)
                z = dot(mix, column)
                cells.append(jnp.concatenate([z[:lat], z[lat:]], axis=1))
            return jnp.concatenate(cells, axis=0)

        rows = lax.broadcasted_iota(jnp.int32, (lat, lat), 0)
        cols = lax.broadcasted_iota(jnp.int32, (lat, lat), 1)
        eye = (rows == cols).astype(F32)
        back = ((rows + cols) % lat == 0).astype(F32)
        has_zero = (quarter == 0).astype(F32)
        even = (eye + 0.5 * has_zero * (back - eye)).astype(BF16)
        odd = (eye - 0.5 * has_zero * (back + eye)).astype(BF16)

        def through_grid(v):
            first = v[:lat]
            first = jnp.concatenate(
                [dot(even, first[:, :width]), dot(odd, first[:, width:])], axis=1
            )
            return jnp.concatenate([first, v[lat:].astype(F32)], axis=0)

        def mask_of(layer):
            mode = quarter * per + lax.broadcasted_iota(jnp.int32, (tall, 1), 0) // lat
            return (mode < s_ref[3 + layer]).astype(F32)

        z = mixed(0)
        slopes = []
        lefts = {}
        index = lax.broadcasted_iota(jnp.int32, (16, width), 0)
        sums = jnp.zeros((16, width), F32)

        def products(which, layer, right, sums):
            outer = dot_cols(lefts[which, layer], right)
            total = jnp.sum(right.astype(F32), axis=0, keepdims=True)
            squares = (
                outer[:width, :width] + outer[width:, width:],
                outer[:width, width:] - outer[width:, :width],
            )
            for r in range(2):
                all_ref[(which * LAYERS + layer) * 2 + r] = squares[r]
                slot = (layer * 2 + which) * 2 + r
                sums = sums + jnp.where(index == slot, total[:, r * width : (r + 1) * width], 0.0)
            return sums

        for layer in range(LAYERS):
            z_low = z.astype(BF16)
            lefts[0, layer] = z_low
            pre = dot(z_low, w_ref[2 * layer]) + b_ref[2 * layer]
            sig = jax.nn.sigmoid(pre)
            hidden = (pre * sig).astype(BF16)
            lefts[1, layer] = hidden
            slopes.append(sig * (1.0 + pre * (1.0 - sig)))
            if layer + 1 < LAYERS:
                out = dot(hidden, w_ref[2 * layer + 1]) + b_ref[2 * layer + 1]
                z = z + through_grid((out * mask_of(layer)).astype(BF16))
        grad = mixed(1)
        total = None
        for layer in reversed(range(LAYERS)):
            dout = (grad * mask_of(layer)).astype(BF16)
            sums = products(1, layer, dout, sums)
            dpre = (dot_rows(dout, w_ref[2 * layer + 1]) * slopes[layer]).astype(BF16)
            sums = products(0, layer, dpre, sums)
            dz = dot_rows(dpre, w_ref[2 * layer])
            if layer:
                grad = grad + through_grid(dz.astype(BF16))
            total = dz if total is None else total + dz
        total = total.astype(BF16)
        for k in range(per):
            part = total[k * lat : (k + 1) * lat]
            part = jnp.concatenate([part[:, :width], part[:, width:]], axis=0)
            tmp[0, pl.ds(k, 2 * lat, stride=per), :] = dot(mix_t, part)
        da_ref[...] = tmp[0].astype(BF16).reshape(chunk)
        for square in range(4 * LAYERS):
            part = all_ref[square].astype(BF16)
            for q in range(quarters):
                send_ref[q, square * own : (square + 1) * own] = part[q * own : (q + 1) * own]
        for q in range(quarters):
            send_ref[q, 4 * LAYERS * own :] = sums.astype(BF16)

    return pl.pallas_call(
        body,
        in_specs=[SMEM] + [VMEM] * 5,
        out_specs=[VMEM] * 2,
        scratch_shapes=[
            pltpu.VMEM((2, 2 * lat * per, width), F32),
            pltpu.VMEM((4 * LAYERS, width, width), F32),
        ],
        out_shape=[
            jax.ShapeDtypeStruct(chunk, BF16),
            jax.ShapeDtypeStruct((quarters, count, width), BF16),
        ],
        compiler_params=params(),
        name="spectral_chain",
    )(scalars, parts, mixer, mixer_t, weights, biases)


def gradient_sum(scalars, parts, width):
    quarters = parts.shape[0]
    own = width // quarters
    half = 2 * LAYERS * own

    def body(s_ref, p_ref, first_hbm, second_hbm, bias_hbm, buf, bias_buf, sem):
        def added(start, size):
            total = p_ref[0, start : start + size].astype(F32)
            for q in range(1, quarters):
                total = total + p_ref[q, start : start + size].astype(F32)
            return total

        copies = [
            pltpu.make_async_copy(bias_buf, bias_hbm, sem.at[2]),
            pltpu.make_async_copy(buf.at[0], first_hbm, sem.at[0]),
            pltpu.make_async_copy(buf.at[1], second_hbm, sem.at[1]),
        ]
        sums = added(2 * half, 16)[:8]
        part = sums[:, :own]
        for q in range(1, quarters):
            part = jnp.where(s_ref[2] == q, sums[:, q * own : (q + 1) * own], part)
        bias_buf[...] = part
        copies[0].start()
        for which in range(2):
            buf[which] = added(which * half, half)
            copies[1 + which].start()
        for copy in copies:
            copy.wait()

    return pl.pallas_call(
        body,
        in_specs=[SMEM, VMEM],
        out_specs=[HBM] * 3,
        scratch_shapes=[
            pltpu.VMEM((2, half, width), F32),
            pltpu.VMEM((8, own), F32),
            pltpu.SemaphoreType.DMA((3,)),
        ],
        out_shape=[
            jax.ShapeDtypeStruct((half, width), F32),
            jax.ShapeDtypeStruct((half, width), F32),
            jax.ShapeDtypeStruct((8, own), F32),
        ],
        compiler_params=params(),
        name="gradient_sum",
    )(scalars, parts)


def on_device(section_input, handoff, loss_grad, w_first, w_second, bias, kept):
    lat_count = lax.axis_size("lat")
    sections = lax.axis_size("section")
    _, rows, lon, channels = section_input.shape
    width = w_first.shape[-1]
    blocks = channels // width
    quarters = lat_count // blocks
    lat = rows * lat_count
    forward = lon_table(lon, rows, quarters, False)
    inverse = lon_table(lon, rows, quarters, True)
    mixer = lat_table(lat, rows)
    place = lax.axis_index("lat")
    section = lax.axis_index("section")
    block = place // quarters
    limits = lax.dynamic_slice(kept, (0, 0, block), (1, LAYERS, 1)).reshape(-1)
    scalars = jnp.concatenate([jnp.stack([section, block, place % quarters]), limits])
    ring = [(s, (s - 1) % sections) for s in range(sections)]
    cells = (rows * lon, channels)

    handed_du = (handoff.reshape(cells), loss_grad.reshape(cells))
    du = to_spectral(section.reshape(1), handed_du, inverse, quarters, width)
    du = lax.ppermute(du, "section", ring)
    spec = to_spectral(section.reshape(1), (section_input.reshape(cells),), forward, quarters, width)
    later, spec = lax.optimization_barrier((handoff, spec))
    both = jnp.concatenate([spec, du], axis=1)
    both = lax.all_to_all(both, "lat", split_axis=0, concat_axis=0, tiled=True)
    received = lax.ppermute(later, "section", ring)
    cot = jnp.where(section == sections - 1, loss_grad, received[0]).reshape(cells)
    weights, biases = block_params(scalars, w_first, w_second, bias, width)
    cot, both = lax.optimization_barrier((cot, both))
    da, parts = spectral_chain(
        scalars, both, mixer, mixer.T.copy(), weights, biases, lat, width, quarters
    )
    da = lax.all_to_all(da, "lat", split_axis=0, concat_axis=0, tiled=True)
    groups = [[b * quarters + q for q in range(quarters)] for b in range(blocks)]

    def exchanged(value):
        return lax.all_to_all(
            value, "lat", split_axis=0, concat_axis=0, tiled=True, axis_index_groups=groups
        )

    parts = lax.cond(jnp.max(limits) > 0, exchanged, jnp.zeros_like, parts)
    handed = to_cells(da, forward.T.copy(), cot, quarters, width)
    first, second, biases = gradient_sum(scalars, parts, width)
    own = width // quarters
    return (
        handed.reshape(1, rows, lon, channels),
        first.reshape(1, LAYERS, 2, own, width),
        second.reshape(1, LAYERS, 2, own, width),
        biases.reshape(1, LAYERS, 2, 2, own),
    )


def solution(mesh):
    return jax.shard_map(
        on_device,
        mesh=mesh,
        in_specs=(
            P("section", "lat", None, None),
            P("section", "lat", None, None),
            P("lat", None, None),
            P("section", None, None, None, None),
            P("section", None, None, None, None),
            P("section", None, None, None, None),
            P("section", None, None),
        ),
        out_specs=(
            P("section", "lat", None, None),
            P("section", None, None, "lat", None),
            P("section", None, None, "lat", None),
            P("section", None, None, None, "lat"),
        ),
        check_vma=False,
    )
```

```python
import math

import jax
import jax.numpy as jnp
import numpy as np
from jax import lax
from jax.experimental import pallas as pl
from jax.experimental.pallas import tpu as pltpu
from jax.sharding import PartitionSpec as P

LAYERS = 2
MAXK = 32
F32 = jnp.float32
BF16 = jnp.bfloat16


def lon_table(lon, rows, quarters, weighted):
    per = MAXK // quarters
    freqs = np.arange(MAXK)
    phase = 2.0 * math.pi * ((freqs[:, None] * np.arange(lon)[None, :]) % lon) / lon
    table = np.stack([np.cos(phase), -np.sin(phase)]) / math.sqrt(lon)
    table[1, 0] = 0.0
    table = table.astype(jnp.bfloat16).astype(np.float32)
    if weighted:
        table = table * np.where(freqs == 0, 1.0, 2.0)[None, :, None]
    split = table.reshape(2, quarters, per, lon).transpose(1, 0, 2, 3)
    full = np.zeros((quarters, 2, rows, per, rows, lon), np.float32)
    for row in range(rows):
        full[:, :, row, :, row, :] = split
    return full.reshape(quarters * 2 * rows * per, rows * lon).astype(jnp.bfloat16)


def lat_table(lat, rows):
    phase = 2.0 * math.pi * ((np.arange(lat)[:, None] * np.arange(lat)[None, :]) % lat) / lat
    cosine = np.cos(phase) / math.sqrt(lat)
    sine = np.sin(phase) / math.sqrt(lat)
    mixer = np.block([[cosine, sine], [-sine, cosine]])
    mixer = mixer.reshape(2 * lat, 2, lat // rows, rows).transpose(0, 2, 1, 3)
    return mixer.reshape(2 * lat, 2 * lat).astype(jnp.bfloat16)


def dot(left, right):
    return jnp.dot(left, right, preferred_element_type=F32)


def dot_rows(left, right):
    return lax.dot_general(left, right, (((1,), (1,)), ((), ())), preferred_element_type=F32)


def dot_cols(left, right):
    return lax.dot_general(left, right, (((0,), (0,)), ((), ())), preferred_element_type=F32)


def params(**kw):
    return pltpu.CompilerParams(vmem_limit_bytes=12 * 1024 * 1024, **kw)


VMEM = pl.BlockSpec(memory_space=pltpu.VMEM)
SMEM = pl.BlockSpec(memory_space=pltpu.SMEM)
HBM = pl.BlockSpec(memory_space=pltpu.HBM)


def in_hbm(value):
    return pltpu.with_memory_space_constraint(value, pltpu.HBM)


def to_spectral(scalars, sources, table, quarters, width):
    cells, channels = sources[0].shape
    rows = table.shape[0] // quarters
    blocks = channels // width
    cuts = 2
    span = cells // cuts

    def body(s_ref, t_hbm, *refs):
        given = refs[: len(sources)]
        o_ref, t_buf, x_buf, t_sem, x_sem = refs[len(sources) :]

        def piece(source, cut):
            part = pl.ds(cut * span, span)
            return pltpu.make_async_copy(source.at[part, :], x_buf.at[part, :], x_sem.at[cut])

        def begin(source):
            for cut in range(cuts):
                piece(source, cut).start()

        table_copy = pltpu.make_async_copy(t_hbm, t_buf, t_sem)
        table_copy.start()
        if len(given) == 1:
            begin(given[0])
        else:
            pl.when(s_ref[0] != 0)(lambda: begin(given[0]))
            pl.when(s_ref[0] == 0)(lambda: begin(given[1]))
        table_copy.wait()
        t = t_buf[...]
        for cut in range(cuts):
            piece(given[0], cut).wait()
        step = 2 * width
        for cut in range(channels // step):
            y = dot(t, x_buf[:, cut * step : (cut + 1) * step]).astype(BF16)
            for b in range(2):
                for q in range(quarters):
                    owner = (cut * 2 + b) * quarters + q
                    o_ref[owner] = y[q * rows : (q + 1) * rows, b * width : (b + 1) * width]

    return pl.pallas_call(
        body,
        in_specs=[SMEM, HBM] + [HBM] * len(sources),
        out_specs=VMEM,
        scratch_shapes=[
            pltpu.VMEM(table.shape, BF16),
            pltpu.VMEM((cells, channels), BF16),
            pltpu.SemaphoreType.DMA(()),
            pltpu.SemaphoreType.DMA((cuts,)),
        ],
        out_shape=jax.ShapeDtypeStruct((blocks * quarters, rows, width), BF16),
        compiler_params=params(),
        name="to_spectral",
    )(scalars, in_hbm(jnp.asarray(table)), *[in_hbm(source) for source in sources])


def to_cells(parts, table_t, grid_add, quarters, width):
    cells, channels = grid_add.shape
    rows = parts.shape[1]
    blocks = channels // width
    cuts = 2
    span = cells // cuts

    def body(t_ref, p_ref, g_ref, o_hbm, buf, sem):
        copies = []
        for cut in range(cuts):
            own = slice(cut * span, (cut + 1) * span)
            table = t_ref[own]
            for block in range(blocks):
                part = p_ref[block * quarters : (block + 1) * quarters]
                part = part.reshape(quarters * rows, width)
                lanes = slice(block * width, (block + 1) * width)
                mixed = g_ref[own, lanes].astype(F32) + dot(table, part)
                buf[own, lanes] = mixed.astype(BF16)
            copies.append(pltpu.make_async_copy(buf.at[own], o_hbm.at[own], sem.at[cut]))
            copies[-1].start()
        for copy in copies:
            copy.wait()

    return pl.pallas_call(
        body,
        in_specs=[VMEM, VMEM, VMEM],
        out_specs=HBM,
        scratch_shapes=[
            pltpu.VMEM((cells, channels), BF16),
            pltpu.SemaphoreType.DMA((cuts,)),
        ],
        out_shape=jax.ShapeDtypeStruct((cells, channels), BF16),
        compiler_params=params(),
        name="to_cells",
    )(table_t, parts, grid_add)


def block_params(scalars, w_first, w_second, bias, width):
    def body(s_ref, w1_hbm, w2_hbm, b_ref, w_ref, rows_ref, buf, sem):
        start = pl.multiple_of(s_ref[1] * width, width)
        copies = [
            pltpu.make_async_copy(w.at[0, :, :, pl.ds(start, width), :], buf.at[which], sem.at[which])
            for which, w in enumerate((w1_hbm, w2_hbm))
        ]
        for copy in copies:
            copy.start()
        for layer in range(LAYERS):
            for which in range(2):
                for r in range(2):
                    rows_ref[2 * layer + which, :, r * width : (r + 1) * width] = b_ref[
                        0, layer, which, pl.ds(r, 1), pl.ds(start, width)
                    ]
        for which in range(2):
            copies[which].wait()
            for layer in range(LAYERS):
                real, imag = (buf[which, layer, 0], buf[which, layer, 1])
                w_ref[2 * layer + which, :width, :width] = real
                w_ref[2 * layer + which, :width, width:] = imag
                w_ref[2 * layer + which, width:, :width] = -imag
                w_ref[2 * layer + which, width:, width:] = real

    return pl.pallas_call(
        body,
        in_specs=[SMEM, HBM, HBM, VMEM],
        out_specs=[VMEM, VMEM],
        scratch_shapes=[
            pltpu.VMEM((2, LAYERS, 2, width, width), BF16),
            pltpu.SemaphoreType.DMA((2,)),
        ],
        out_shape=[
            jax.ShapeDtypeStruct((2 * LAYERS, 2 * width, 2 * width), BF16),
            jax.ShapeDtypeStruct((2 * LAYERS, 1, 2 * width), F32),
        ],
        compiler_params=params(),
        name="block_params",
    )(scalars, in_hbm(w_first), in_hbm(w_second), bias)


def spectral_chain(scalars, parts, mixer, weights, biases, lat, width, quarters):
    sources, both, _ = parts.shape
    per = sources * (both // 2) // (2 * lat)
    tall = per * lat

    own = width // quarters
    count = 4 * LAYERS * own + 16

    def body(s_ref, parts_ref, l_ref, w_ref, b_ref, dz_ref, mine_ref, send_ref, tmp, all_ref):
        quarter = s_ref[2]
        mix = l_ref[...]

        def mixed(slot):
            part = parts_ref[:, slot * (both // 2) : (slot + 1) * (both // 2), :]
            tmp[slot] = part.reshape(2 * lat * per, width).astype(F32)
            cells = []
            for k in range(per):
                column = tmp[slot, pl.ds(k, 2 * lat, stride=per), :].astype(BF16)
                z = dot(mix, column)
                cells.append(jnp.concatenate([z[:lat], z[lat:]], axis=1))
            return jnp.concatenate(cells, axis=0)

        rows = lax.broadcasted_iota(jnp.int32, (lat, lat), 0)
        cols = lax.broadcasted_iota(jnp.int32, (lat, lat), 1)
        eye = (rows == cols).astype(F32)
        back = ((rows + cols) % lat == 0).astype(F32)
        has_zero = (quarter == 0).astype(F32)
        even = (eye + 0.5 * has_zero * (back - eye)).astype(BF16)
        odd = (eye - 0.5 * has_zero * (back + eye)).astype(BF16)

        def through_grid(v):
            first = v[:lat]
            first = jnp.concatenate(
                [dot(even, first[:, :width]), dot(odd, first[:, width:])], axis=1
            )
            return jnp.concatenate([first, v[lat:].astype(F32)], axis=0)

        def mask_of(layer):
            mode = quarter * per + lax.broadcasted_iota(jnp.int32, (tall, 1), 0) // lat
            return (mode < s_ref[3 + layer]).astype(F32)

        z = mixed(0)
        slopes = []
        lefts = {}
        index = lax.broadcasted_iota(jnp.int32, (16, width), 0)
        sums = jnp.zeros((16, width), F32)

        def products(which, layer, right, sums):
            outer = dot_cols(lefts[which, layer], right)
            total = jnp.sum(right.astype(F32), axis=0, keepdims=True)
            squares = (
                outer[:width, :width] + outer[width:, width:],
                outer[:width, width:] - outer[width:, :width],
            )
            for r in range(2):
                all_ref[(which * LAYERS + layer) * 2 + r] = squares[r]
                slot = (layer * 2 + which) * 2 + r
                sums = sums + jnp.where(index == slot, total[:, r * width : (r + 1) * width], 0.0)
            return sums

        for layer in range(LAYERS):
            z_low = z.astype(BF16)
            lefts[0, layer] = z_low
            pre = dot(z_low, w_ref[2 * layer]) + b_ref[2 * layer]
            sig = jax.nn.sigmoid(pre)
            hidden = (pre * sig).astype(BF16)
            lefts[1, layer] = hidden
            slopes.append(sig * (1.0 + pre * (1.0 - sig)))
            if layer + 1 < LAYERS:
                out = dot(hidden, w_ref[2 * layer + 1]) + b_ref[2 * layer + 1]
                z = z + through_grid((out * mask_of(layer)).astype(BF16))
        grad = mixed(1)
        total = None
        for layer in reversed(range(LAYERS)):
            dout = (grad * mask_of(layer)).astype(BF16)
            sums = products(1, layer, dout, sums)
            dpre = (dot_rows(dout, w_ref[2 * layer + 1]) * slopes[layer]).astype(BF16)
            sums = products(0, layer, dpre, sums)
            dz = dot_rows(dpre, w_ref[2 * layer])
            if layer:
                grad = grad + through_grid(dz.astype(BF16))
            total = dz if total is None else total + dz
        dz_ref[...] = total.astype(BF16)
        targets = (quarter, quarter ^ 2, quarter ^ 1, quarter ^ 3)
        for slot, target in enumerate(targets):
            o_ref = (mine_ref, send_ref)[slot // 2].at[slot % 2]
            start = pl.multiple_of(target * own, own)
            for square in range(4 * LAYERS):
                part = all_ref[square, pl.ds(start, own), :]
                o_ref[square * own : (square + 1) * own] = part.astype(o_ref.dtype)
            o_ref[4 * LAYERS * own :] = sums.astype(o_ref.dtype)

    return pl.pallas_call(
        body,
        in_specs=[SMEM] + [VMEM] * 4,
        out_specs=[VMEM] * 3,
        scratch_shapes=[
            pltpu.VMEM((2, 2 * lat * per, width), F32),
            pltpu.VMEM((4 * LAYERS, width, width), F32),
        ],
        out_shape=[
            jax.ShapeDtypeStruct((tall, 2 * width), BF16),
            jax.ShapeDtypeStruct((2, count, width), F32),
            jax.ShapeDtypeStruct((2, count, width), BF16),
        ],
        compiler_params=params(),
        name="spectral_chain",
    )(scalars, parts, mixer, weights, biases)


def to_bands(dz, mixer_t, lat, width, sources):
    per = dz.shape[0] // lat
    chunk = (sources, 2 * lat * per // sources, width)

    def body(dz_ref, lt_ref, da_ref, tmp):
        mix_t = lt_ref[...]
        for k in range(per):
            part = dz_ref[k * lat : (k + 1) * lat]
            part = jnp.concatenate([part[:, :width], part[:, width:]], axis=0)
            tmp[pl.ds(k, 2 * lat, stride=per), :] = dot(mix_t, part)
        da_ref[...] = tmp[...].astype(BF16).reshape(chunk)

    return pl.pallas_call(
        body,
        in_specs=[VMEM, VMEM],
        out_specs=VMEM,
        scratch_shapes=[pltpu.VMEM((2 * lat * per, width), F32)],
        out_shape=jax.ShapeDtypeStruct(chunk, BF16),
        compiler_params=params(),
        name="to_bands",
    )(dz, mixer_t)


def gradient_sum(scalars, mine, near, far, width, quarters):
    own = width // quarters
    half = 2 * LAYERS * own

    def body(s_ref, m_ref, n_ref, f_ref, first_hbm, second_hbm, bias_hbm, buf, bias_buf, sem):
        def added(start, size):
            part = slice(start, start + size)
            return m_ref[0, part] + n_ref[0, part].astype(F32) + f_ref[part].astype(F32)

        copies = [
            pltpu.make_async_copy(bias_buf, bias_hbm, sem.at[2]),
            pltpu.make_async_copy(buf.at[0], first_hbm, sem.at[0]),
            pltpu.make_async_copy(buf.at[1], second_hbm, sem.at[1]),
        ]
        sums = added(2 * half, 16)[:8]
        part = sums[:, :own]
        for q in range(1, quarters):
            part = jnp.where(s_ref[2] == q, sums[:, q * own : (q + 1) * own], part)
        bias_buf[...] = part
        copies[0].start()
        for which in range(2):
            buf[which] = added(which * half, half)
            copies[1 + which].start()
        for copy in copies:
            copy.wait()

    return pl.pallas_call(
        body,
        in_specs=[SMEM] + [VMEM] * 3,
        out_specs=[HBM] * 3,
        scratch_shapes=[
            pltpu.VMEM((2, half, width), F32),
            pltpu.VMEM((8, own), F32),
            pltpu.SemaphoreType.DMA((3,)),
        ],
        out_shape=[
            jax.ShapeDtypeStruct((half, width), F32),
            jax.ShapeDtypeStruct((half, width), F32),
            jax.ShapeDtypeStruct((8, own), F32),
        ],
        compiler_params=params(),
        cost_estimate=pl.CostEstimate(flops=2 * 10**9, transcendentals=0, bytes_accessed=1 << 20),
        name="gradient_sum",
    )(scalars, mine, near, far)


def on_device(section_input, handoff, loss_grad, w_first, w_second, bias, kept):
    lat_count = lax.axis_size("lat")
    sections = lax.axis_size("section")
    _, rows, lon, channels = section_input.shape
    width = w_first.shape[-1]
    blocks = channels // width
    quarters = lat_count // blocks
    lat = rows * lat_count
    forward = lon_table(lon, rows, quarters, False)
    inverse = lon_table(lon, rows, quarters, True)
    mixer = lat_table(lat, rows)
    place = lax.axis_index("lat")
    section = lax.axis_index("section")
    block = place // quarters
    limits = lax.dynamic_slice(kept, (0, 0, block), (1, LAYERS, 1)).reshape(-1)
    scalars = jnp.concatenate([jnp.stack([section, block, place % quarters]), limits])
    ring = [(s, (s - 1) % sections) for s in range(sections)]
    cells = (rows * lon, channels)

    handed_du = (handoff.reshape(cells), loss_grad.reshape(cells))
    du = to_spectral(section.reshape(1), handed_du, inverse, quarters, width)
    du = lax.ppermute(du, "section", ring)
    spec = to_spectral(section.reshape(1), (section_input.reshape(cells),), forward, quarters, width)
    both = jnp.concatenate([spec, du], axis=1)
    later, both = lax.optimization_barrier((handoff, both))
    both = lax.all_to_all(both, "lat", split_axis=0, concat_axis=0, tiled=True)
    received = lax.ppermute(later, "section", ring)
    cot = jnp.where(section == sections - 1, loss_grad, received[0]).reshape(cells)
    weights, biases = block_params(scalars, w_first, w_second, bias, width)
    cot, both = lax.optimization_barrier((cot, both))
    dz, mine, send = spectral_chain(
        scalars, both, mixer, weights, biases, lat, width, quarters
    )

    def swapped(value, bit):
        return lax.ppermute(value, "lat", [(d, d ^ bit) for d in range(lat_count)])

    near = swapped(send, 1)
    da = to_bands(dz, mixer.T.copy(), lat, width, lat_count)
    da = lax.all_to_all(da, "lat", split_axis=0, concat_axis=0, tiled=True)
    far = swapped((mine[1] + near[1].astype(F32)).astype(BF16), 2)
    first, second, biases = gradient_sum(scalars, mine, near, far, width, quarters)
    handed = to_cells(da, forward.T.copy(), cot, quarters, width)
    own = width // quarters
    return (
        handed.reshape(1, rows, lon, channels),
        first.reshape(1, LAYERS, 2, own, width),
        second.reshape(1, LAYERS, 2, own, width),
        biases.reshape(1, LAYERS, 2, 2, own),
    )


def solution(mesh):
    return jax.shard_map(
        on_device,
        mesh=mesh,
        in_specs=(
            P("section", "lat", None, None),
            P("section", "lat", None, None),
            P("lat", None, None),
            P("section", None, None, None, None),
            P("section", None, None, None, None),
            P("section", None, None, None, None),
            P("section", None, None),
        ),
        out_specs=(
            P("section", "lat", None, None),
            P("section", None, None, "lat", None),
            P("section", None, None, "lat", None),
            P("section", None, None, None, "lat"),
        ),
        check_vma=False,
    )
```

```python
import math

import jax
import jax.numpy as jnp
import numpy as np
from jax import lax
from jax.experimental import pallas as pl
from jax.experimental.pallas import tpu as pltpu
from jax.sharding import PartitionSpec as P

LAYERS = 2
MAXK = 32
F32 = jnp.float32
BF16 = jnp.bfloat16


def lon_table(lon, rows, quarters, weighted):
    per = MAXK // quarters
    freqs = np.arange(MAXK)
    phase = 2.0 * math.pi * ((freqs[:, None] * np.arange(lon)[None, :]) % lon) / lon
    table = np.stack([np.cos(phase), -np.sin(phase)]) / math.sqrt(lon)
    table[1, 0] = 0.0
    table = table.astype(jnp.bfloat16).astype(np.float32)
    if weighted:
        table = table * np.where(freqs == 0, 1.0, 2.0)[None, :, None]
    split = table.reshape(2, quarters, per, lon).transpose(1, 0, 2, 3)
    full = np.zeros((quarters, 2, rows, per, rows, lon), np.float32)
    for row in range(rows):
        full[:, :, row, :, row, :] = split
    return full.reshape(quarters * 2 * rows * per, rows * lon).astype(jnp.bfloat16)


def lat_table(lat, rows):
    phase = 2.0 * math.pi * ((np.arange(lat)[:, None] * np.arange(lat)[None, :]) % lat) / lat
    cosine = np.cos(phase) / math.sqrt(lat)
    sine = np.sin(phase) / math.sqrt(lat)
    mixer = np.block([[cosine, sine], [-sine, cosine]])
    mixer = mixer.reshape(2 * lat, 2, lat // rows, rows).transpose(0, 2, 1, 3)
    return mixer.reshape(2 * lat, 2 * lat).astype(jnp.bfloat16)


def dot(left, right):
    return jnp.dot(left, right, preferred_element_type=F32)


def dot_rows(left, right):
    return lax.dot_general(left, right, (((1,), (1,)), ((), ())), preferred_element_type=F32)


def dot_cols(left, right):
    return lax.dot_general(left, right, (((0,), (0,)), ((), ())), preferred_element_type=F32)


def params(**kw):
    return pltpu.CompilerParams(vmem_limit_bytes=12 * 1024 * 1024, **kw)


VMEM = pl.BlockSpec(memory_space=pltpu.VMEM)
SMEM = pl.BlockSpec(memory_space=pltpu.SMEM)
HBM = pl.BlockSpec(memory_space=pltpu.HBM)


def in_hbm(value):
    return pltpu.with_memory_space_constraint(value, pltpu.HBM)


def to_spectral(x, table, quarters, width):
    cells, channels = x.shape
    rows = table.shape[0] // quarters
    blocks = channels // width
    cuts = 2
    span = cells // cuts

    def body(t_hbm, x_hbm, o_ref, t_buf, x_buf, t_sem, x_sem):
        copies = [pltpu.make_async_copy(t_hbm, t_buf, t_sem)]
        for cut in range(cuts):
            part = pl.ds(cut * span, span)
            copies.append(
                pltpu.make_async_copy(x_hbm.at[part, :], x_buf.at[part, :], x_sem.at[cut])
            )
        for copy in copies:
            copy.start()
        for copy in copies:
            copy.wait()
        transform(t_buf[...], x_buf, o_ref, 0, quarters, width)

    return pl.pallas_call(
        body,
        in_specs=[HBM, HBM],
        out_specs=VMEM,
        scratch_shapes=[
            pltpu.VMEM(table.shape, BF16),
            pltpu.VMEM((cells, channels), BF16),
            pltpu.SemaphoreType.DMA(()),
            pltpu.SemaphoreType.DMA((cuts,)),
        ],
        out_shape=jax.ShapeDtypeStruct((blocks * quarters, rows, width), BF16),
        compiler_params=params(),
        name="to_spectral",
    )(in_hbm(jnp.asarray(table)), in_hbm(x))


def transform(table, x_ref, o_ref, at, quarters, width):
    rows = table.shape[0] // quarters
    step = 2 * width
    for cut in range(x_ref.shape[1] // step):
        y = dot(table, x_ref[:, cut * step : (cut + 1) * step]).astype(BF16)
        for b in range(2):
            for q in range(quarters):
                owner = (cut * 2 + b) * quarters + q
                part = y[q * rows : (q + 1) * rows, b * width : (b + 1) * width]
                o_ref[owner, at : at + rows] = part


def to_spectral_joined(scalars, spec, received, loss_grad, table, quarters, width):
    cells, channels = loss_grad.shape
    owners, rows, _ = spec.shape
    cuts = 2
    span = cells // cuts

    def body(s_ref, t_ref, spec_ref, received_ref, loss_hbm, o_hbm, cot_ref, buf, x_sem, o_sem):
        def piece(source, cut):
            part = pl.ds(cut * span, span)
            return pltpu.make_async_copy(source.at[part, :], cot_ref.at[part, :], x_sem.at[cut])

        def begin(source):
            for cut in range(cuts):
                piece(source, cut).start()

        pl.when(s_ref[0] == 0)(lambda: begin(received_ref))
        pl.when(s_ref[0] != 0)(lambda: begin(loss_hbm))
        buf[:, :rows] = spec_ref[...]
        for cut in range(cuts):
            piece(received_ref, cut).wait()
        copies = []
        half = owners // 2
        for cut in range(2):
            lanes = pl.ds(cut * (channels // 2), channels // 2)
            own = pl.ds(cut * half, half)
            transform(t_ref[...], cot_ref.at[:, lanes], buf.at[own], rows, quarters, width)
            copies.append(pltpu.make_async_copy(buf.at[own], o_hbm.at[own], o_sem.at[cut]))
            copies[-1].start()
        for copy in copies:
            copy.wait()

    return pl.pallas_call(
        body,
        in_specs=[SMEM, VMEM, VMEM, VMEM, HBM],
        out_specs=[HBM, VMEM],
        scratch_shapes=[
            pltpu.VMEM((owners, 2 * rows, width), BF16),
            pltpu.SemaphoreType.DMA((cuts,)),
            pltpu.SemaphoreType.DMA((2,)),
        ],
        out_shape=[
            jax.ShapeDtypeStruct((owners, 2 * rows, width), BF16),
            jax.ShapeDtypeStruct((cells, channels), BF16),
        ],
        compiler_params=params(),
        name="to_spectral_joined",
    )(scalars, table, spec, received, in_hbm(loss_grad))


def to_cells(parts, table_t, grid_add, quarters, width):
    cells, channels = grid_add.shape
    rows = parts.shape[1]
    blocks = channels // width
    cuts = 2
    span = cells // cuts

    def body(t_ref, p_ref, g_ref, o_hbm, buf, sem):
        copies = []
        for cut in range(cuts):
            own = slice(cut * span, (cut + 1) * span)
            table = t_ref[own]
            for block in range(blocks):
                part = p_ref[block * quarters : (block + 1) * quarters]
                part = part.reshape(quarters * rows, width)
                lanes = slice(block * width, (block + 1) * width)
                mixed = g_ref[own, lanes].astype(F32) + dot(table, part)
                buf[own, lanes] = mixed.astype(BF16)
            copies.append(pltpu.make_async_copy(buf.at[own], o_hbm.at[own], sem.at[cut]))
            copies[-1].start()
        for copy in copies:
            copy.wait()

    return pl.pallas_call(
        body,
        in_specs=[VMEM, VMEM, VMEM],
        out_specs=HBM,
        scratch_shapes=[
            pltpu.VMEM((cells, channels), BF16),
            pltpu.SemaphoreType.DMA((cuts,)),
        ],
        out_shape=jax.ShapeDtypeStruct((cells, channels), BF16),
        compiler_params=params(),
        name="to_cells",
    )(table_t, parts, grid_add)


def block_params(scalars, w_first, w_second, bias, width):
    def body(s_ref, w1_hbm, w2_hbm, b_ref, w_ref, rows_ref, buf, sem):
        start = pl.multiple_of(s_ref[1] * width, width)
        copies = [
            pltpu.make_async_copy(w.at[0, :, :, pl.ds(start, width), :], buf.at[which], sem.at[which])
            for which, w in enumerate((w1_hbm, w2_hbm))
        ]
        for copy in copies:
            copy.start()
        for layer in range(LAYERS):
            for which in range(2):
                for r in range(2):
                    rows_ref[2 * layer + which, :, r * width : (r + 1) * width] = b_ref[
                        0, layer, which, pl.ds(r, 1), pl.ds(start, width)
                    ]
        for which in range(2):
            copies[which].wait()
            for layer in range(LAYERS):
                real, imag = (buf[which, layer, 0], buf[which, layer, 1])
                w_ref[2 * layer + which, :width, :width] = real
                w_ref[2 * layer + which, :width, width:] = imag
                w_ref[2 * layer + which, width:, :width] = -imag
                w_ref[2 * layer + which, width:, width:] = real

    return pl.pallas_call(
        body,
        in_specs=[SMEM, HBM, HBM, VMEM],
        out_specs=[VMEM, VMEM],
        scratch_shapes=[
            pltpu.VMEM((2, LAYERS, 2, width, width), BF16),
            pltpu.SemaphoreType.DMA((2,)),
        ],
        out_shape=[
            jax.ShapeDtypeStruct((2 * LAYERS, 2 * width, 2 * width), BF16),
            jax.ShapeDtypeStruct((2 * LAYERS, 1, 2 * width), F32),
        ],
        compiler_params=params(),
        name="block_params",
    )(scalars, in_hbm(w_first), in_hbm(w_second), bias)


def spectral_chain(scalars, parts, mixer, weights, biases, lat, width, quarters):
    sources, both, _ = parts.shape
    per = sources * (both // 2) // (2 * lat)
    tall = per * lat

    own = width // quarters
    count = 4 * LAYERS * own + 16

    def body(s_ref, parts_ref, l_ref, w_ref, b_ref, dz_ref, mine_ref, send_ref, tmp, all_ref):
        quarter = s_ref[2]
        mix = l_ref[...]

        def mixed(slot):
            part = parts_ref[:, slot * (both // 2) : (slot + 1) * (both // 2), :]
            tmp[slot] = part.reshape(2 * lat * per, width).astype(F32)
            cells = []
            for k in range(per):
                column = tmp[slot, pl.ds(k, 2 * lat, stride=per), :].astype(BF16)
                z = dot(mix, column)
                cells.append(jnp.concatenate([z[:lat], z[lat:]], axis=1))
            return jnp.concatenate(cells, axis=0)

        rows = lax.broadcasted_iota(jnp.int32, (lat, lat), 0)
        cols = lax.broadcasted_iota(jnp.int32, (lat, lat), 1)
        eye = (rows == cols).astype(F32)
        back = ((rows + cols) % lat == 0).astype(F32)
        has_zero = (quarter == 0).astype(F32)
        even = (eye + 0.5 * has_zero * (back - eye)).astype(BF16)
        odd = (eye - 0.5 * has_zero * (back + eye)).astype(BF16)

        def through_grid(v):
            first = v[:lat]
            first = jnp.concatenate(
                [dot(even, first[:, :width]), dot(odd, first[:, width:])], axis=1
            )
            return jnp.concatenate([first, v[lat:].astype(F32)], axis=0)

        def mask_of(layer):
            mode = quarter * per + lax.broadcasted_iota(jnp.int32, (tall, 1), 0) // lat
            return (mode < s_ref[3 + layer]).astype(F32)

        z = mixed(0)
        slopes = []
        lefts = {}
        index = lax.broadcasted_iota(jnp.int32, (16, width), 0)
        sums = jnp.zeros((16, width), F32)

        def products(which, layer, right, sums):
            outer = dot_cols(lefts[which, layer], right)
            total = jnp.sum(right.astype(F32), axis=0, keepdims=True)
            squares = (
                outer[:width, :width] + outer[width:, width:],
                outer[:width, width:] - outer[width:, :width],
            )
            for r in range(2):
                all_ref[(which * LAYERS + layer) * 2 + r] = squares[r]
                slot = (layer * 2 + which) * 2 + r
                sums = sums + jnp.where(index == slot, total[:, r * width : (r + 1) * width], 0.0)
            return sums

        for layer in range(LAYERS):
            z_low = z.astype(BF16)
            lefts[0, layer] = z_low
            pre = dot(z_low, w_ref[2 * layer]) + b_ref[2 * layer]
            sig = jax.nn.sigmoid(pre)
            hidden = (pre * sig).astype(BF16)
            lefts[1, layer] = hidden
            slopes.append(sig * (1.0 + pre * (1.0 - sig)))
            if layer + 1 < LAYERS:
                out = dot(hidden, w_ref[2 * layer + 1]) + b_ref[2 * layer + 1]
                z = z + through_grid((out * mask_of(layer)).astype(BF16))
        grad = mixed(1)
        total = None
        for layer in reversed(range(LAYERS)):
            dout = (grad * mask_of(layer)).astype(BF16)
            sums = products(1, layer, dout, sums)
            dpre = (dot_rows(dout, w_ref[2 * layer + 1]) * slopes[layer]).astype(BF16)
            sums = products(0, layer, dpre, sums)
            dz = dot_rows(dpre, w_ref[2 * layer])
            if layer:
                grad = grad + through_grid(dz.astype(BF16))
            total = dz if total is None else total + dz
        dz_ref[...] = total.astype(BF16)
        targets = (quarter, quarter ^ 2, quarter ^ 1, quarter ^ 3)
        for slot, target in enumerate(targets):
            o_ref = (mine_ref, send_ref)[slot // 2].at[slot % 2]
            start = pl.multiple_of(target * own, own)
            for square in range(4 * LAYERS):
                part = all_ref[square, pl.ds(start, own), :]
                o_ref[square * own : (square + 1) * own] = part.astype(o_ref.dtype)
            o_ref[4 * LAYERS * own :] = sums.astype(o_ref.dtype)

    return pl.pallas_call(
        body,
        in_specs=[SMEM] + [VMEM] * 4,
        out_specs=[VMEM] * 3,
        scratch_shapes=[
            pltpu.VMEM((2, 2 * lat * per, width), F32),
            pltpu.VMEM((4 * LAYERS, width, width), F32),
        ],
        out_shape=[
            jax.ShapeDtypeStruct((tall, 2 * width), BF16),
            jax.ShapeDtypeStruct((2, count, width), F32),
            jax.ShapeDtypeStruct((2, count, width), BF16),
        ],
        compiler_params=params(),
        name="spectral_chain",
    )(scalars, parts, mixer, weights, biases)


def to_bands(dz, mixer_t, lat, width, sources):
    per = dz.shape[0] // lat
    chunk = (sources, 2 * lat * per // sources, width)

    def body(dz_ref, lt_ref, da_ref, tmp):
        mix_t = lt_ref[...]
        for k in range(per):
            part = dz_ref[k * lat : (k + 1) * lat]
            part = jnp.concatenate([part[:, :width], part[:, width:]], axis=0)
            tmp[pl.ds(k, 2 * lat, stride=per), :] = dot(mix_t, part)
        da_ref[...] = tmp[...].astype(BF16).reshape(chunk)

    return pl.pallas_call(
        body,
        in_specs=[VMEM, VMEM],
        out_specs=VMEM,
        scratch_shapes=[pltpu.VMEM((2 * lat * per, width), F32)],
        out_shape=jax.ShapeDtypeStruct(chunk, BF16),
        compiler_params=params(),
        name="to_bands",
    )(dz, mixer_t)


def gradient_sum(scalars, mine, near, far, width, quarters):
    own = width // quarters
    half = 2 * LAYERS * own

    def body(s_ref, m_ref, n_ref, f_ref, first_hbm, second_hbm, bias_hbm, buf, bias_buf, sem):
        def added(start, size):
            part = slice(start, start + size)
            return m_ref[0, part] + n_ref[0, part].astype(F32) + f_ref[part].astype(F32)

        copies = [
            pltpu.make_async_copy(bias_buf, bias_hbm, sem.at[2]),
            pltpu.make_async_copy(buf.at[0], first_hbm, sem.at[0]),
            pltpu.make_async_copy(buf.at[1], second_hbm, sem.at[1]),
        ]
        sums = added(2 * half, 16)[:8]
        part = sums[:, :own]
        for q in range(1, quarters):
            part = jnp.where(s_ref[2] == q, sums[:, q * own : (q + 1) * own], part)
        bias_buf[...] = part
        copies[0].start()
        for which in range(2):
            buf[which] = added(which * half, half)
            copies[1 + which].start()
        for copy in copies:
            copy.wait()

    return pl.pallas_call(
        body,
        in_specs=[SMEM] + [VMEM] * 3,
        out_specs=[HBM] * 3,
        scratch_shapes=[
            pltpu.VMEM((2, half, width), F32),
            pltpu.VMEM((8, own), F32),
            pltpu.SemaphoreType.DMA((3,)),
        ],
        out_shape=[
            jax.ShapeDtypeStruct((half, width), F32),
            jax.ShapeDtypeStruct((half, width), F32),
            jax.ShapeDtypeStruct((8, own), F32),
        ],
        compiler_params=params(),
        cost_estimate=pl.CostEstimate(flops=2 * 10**9, transcendentals=0, bytes_accessed=1 << 20),
        name="gradient_sum",
    )(scalars, mine, near, far)


def on_device(section_input, handoff, loss_grad, w_first, w_second, bias, kept):
    lat_count = lax.axis_size("lat")
    sections = lax.axis_size("section")
    _, rows, lon, channels = section_input.shape
    width = w_first.shape[-1]
    blocks = channels // width
    quarters = lat_count // blocks
    lat = rows * lat_count
    forward = lon_table(lon, rows, quarters, False)
    inverse = lon_table(lon, rows, quarters, True)
    mixer = lat_table(lat, rows)
    place = lax.axis_index("lat")
    section = lax.axis_index("section")
    block = place // quarters
    limits = lax.dynamic_slice(kept, (0, 0, block), (1, LAYERS, 1)).reshape(-1)
    scalars = jnp.concatenate([jnp.stack([section, block, place % quarters]), limits])
    ring = [(s, (s - 1) % sections) for s in range(sections)]
    cells = (rows * lon, channels)

    received = lax.ppermute(handoff.reshape(cells), "section", ring)
    spec = to_spectral(section_input.reshape(cells), forward, quarters, width)
    last = (section == sections - 1).astype(jnp.int32).reshape(1)
    both, cot = to_spectral_joined(
        last, spec, received, loss_grad.reshape(cells), inverse, quarters, width
    )
    both = lax.all_to_all(both, "lat", split_axis=0, concat_axis=0, tiled=True)
    weights, biases = block_params(scalars, w_first, w_second, bias, width)
    dz, mine, send = spectral_chain(
        scalars, both, mixer, weights, biases, lat, width, quarters
    )

    def swapped(value, bit):
        return lax.ppermute(value, "lat", [(d, d ^ bit) for d in range(lat_count)])

    near = swapped(send, 1)
    da = to_bands(dz, mixer.T.copy(), lat, width, lat_count)
    da = lax.all_to_all(da, "lat", split_axis=0, concat_axis=0, tiled=True)
    far = swapped((mine[1] + near[1].astype(F32)).astype(BF16), 2)
    first, second, biases = gradient_sum(scalars, mine, near, far, width, quarters)
    handed = to_cells(da, forward.T.copy(), cot, quarters, width)
    own = width // quarters
    return (
        handed.reshape(1, rows, lon, channels),
        first.reshape(1, LAYERS, 2, own, width),
        second.reshape(1, LAYERS, 2, own, width),
        biases.reshape(1, LAYERS, 2, 2, own),
    )


def solution(mesh):
    return jax.shard_map(
        on_device,
        mesh=mesh,
        in_specs=(
            P("section", "lat", None, None),
            P("section", "lat", None, None),
            P("lat", None, None),
            P("section", None, None, None, None),
            P("section", None, None, None, None),
            P("section", None, None, None, None),
            P("section", None, None),
        ),
        out_specs=(
            P("section", "lat", None, None),
            P("section", None, None, "lat", None),
            P("section", None, None, "lat", None),
            P("section", None, None, None, "lat"),
        ),
        check_vma=False,
    )
```

```python
import math

import jax
import jax.numpy as jnp
import numpy as np
from jax import lax
from jax.experimental import pallas as pl
from jax.experimental.pallas import tpu as pltpu
from jax.sharding import PartitionSpec as P

LAYERS = 2
MAXK = 32
F32 = jnp.float32
BF16 = jnp.bfloat16


def lon_table(lon, rows, quarters, weighted):
    per = MAXK // quarters
    freqs = np.arange(MAXK)
    phase = 2.0 * math.pi * ((freqs[:, None] * np.arange(lon)[None, :]) % lon) / lon
    table = np.stack([np.cos(phase), -np.sin(phase)]) / math.sqrt(lon)
    table[1, 0] = 0.0
    table = table.astype(jnp.bfloat16).astype(np.float32)
    if weighted:
        table = table * np.where(freqs == 0, 1.0, 2.0)[None, :, None]
    split = table.reshape(2, quarters, per, lon).transpose(1, 0, 2, 3)
    full = np.zeros((quarters, 2, rows, per, rows, lon), np.float32)
    for row in range(rows):
        full[:, :, row, :, row, :] = split
    return full.reshape(quarters * 2 * rows * per, rows * lon).astype(jnp.bfloat16)


def lat_table(lat, rows):
    phase = 2.0 * math.pi * ((np.arange(lat)[:, None] * np.arange(lat)[None, :]) % lat) / lat
    cosine = np.cos(phase) / math.sqrt(lat)
    sine = np.sin(phase) / math.sqrt(lat)
    mixer = np.block([[cosine, sine], [-sine, cosine]])
    mixer = mixer.reshape(2 * lat, 2, lat // rows, rows).transpose(0, 2, 1, 3)
    return mixer.reshape(2 * lat, 2 * lat).astype(jnp.bfloat16)


def dot(left, right):
    return jnp.dot(left, right, preferred_element_type=F32)


def dot_rows(left, right):
    return lax.dot_general(left, right, (((1,), (1,)), ((), ())), preferred_element_type=F32)


def dot_cols(left, right):
    return lax.dot_general(left, right, (((0,), (0,)), ((), ())), preferred_element_type=F32)


def params(**kw):
    return pltpu.CompilerParams(vmem_limit_bytes=12 * 1024 * 1024, **kw)


VMEM = pl.BlockSpec(memory_space=pltpu.VMEM)
SMEM = pl.BlockSpec(memory_space=pltpu.SMEM)
HBM = pl.BlockSpec(memory_space=pltpu.HBM)


def in_hbm(value):
    return pltpu.with_memory_space_constraint(value, pltpu.HBM)


def to_spectral(scalars, sources, table, quarters, width):
    cells, channels = sources[0].shape
    rows = table.shape[0] // quarters
    blocks = channels // width
    cuts = 2
    span = cells // cuts

    def body(s_ref, t_hbm, *refs):
        given = refs[: len(sources)]
        o_ref, t_buf, x_buf, t_sem, x_sem = refs[len(sources) :]

        def piece(source, cut):
            part = pl.ds(cut * span, span)
            return pltpu.make_async_copy(source.at[part, :], x_buf.at[part, :], x_sem.at[cut])

        def begin(source):
            for cut in range(cuts):
                piece(source, cut).start()

        table_copy = pltpu.make_async_copy(t_hbm, t_buf, t_sem)
        table_copy.start()
        if len(given) == 1:
            begin(given[0])
        else:
            pl.when(s_ref[0] != 0)(lambda: begin(given[0]))
            pl.when(s_ref[0] == 0)(lambda: begin(given[1]))
        table_copy.wait()
        t = t_buf[...]
        for cut in range(cuts):
            piece(given[0], cut).wait()
        step = 2 * width
        for cut in range(channels // step):
            y = dot(t, x_buf[:, cut * step : (cut + 1) * step]).astype(BF16)
            for b in range(2):
                for q in range(quarters):
                    owner = (cut * 2 + b) * quarters + q
                    o_ref[owner] = y[q * rows : (q + 1) * rows, b * width : (b + 1) * width]

    return pl.pallas_call(
        body,
        in_specs=[SMEM, HBM] + [HBM] * len(sources),
        out_specs=VMEM,
        scratch_shapes=[
            pltpu.VMEM(table.shape, BF16),
            pltpu.VMEM((cells, channels), BF16),
            pltpu.SemaphoreType.DMA(()),
            pltpu.SemaphoreType.DMA((cuts,)),
        ],
        out_shape=jax.ShapeDtypeStruct((blocks * quarters, rows, width), BF16),
        compiler_params=params(),
        name="to_spectral",
    )(scalars, in_hbm(jnp.asarray(table)), *[in_hbm(source) for source in sources])


def to_cells(parts, table_t, grid_add, quarters, width):
    cells, channels = grid_add.shape
    rows = parts.shape[1]
    blocks = channels // width
    cuts = 2
    span = cells // cuts

    def body(t_ref, p_ref, g_ref, o_hbm, buf, sem):
        copies = []
        for cut in range(cuts):
            own = slice(cut * span, (cut + 1) * span)
            table = t_ref[own]
            for block in range(blocks):
                part = p_ref[block * quarters : (block + 1) * quarters]
                part = part.reshape(quarters * rows, width)
                lanes = slice(block * width, (block + 1) * width)
                mixed = g_ref[own, lanes].astype(F32) + dot(table, part)
                buf[own, lanes] = mixed.astype(BF16)
            copies.append(pltpu.make_async_copy(buf.at[own], o_hbm.at[own], sem.at[cut]))
            copies[-1].start()
        for copy in copies:
            copy.wait()

    return pl.pallas_call(
        body,
        in_specs=[VMEM, VMEM, VMEM],
        out_specs=HBM,
        scratch_shapes=[
            pltpu.VMEM((cells, channels), BF16),
            pltpu.SemaphoreType.DMA((cuts,)),
        ],
        out_shape=jax.ShapeDtypeStruct((cells, channels), BF16),
        compiler_params=params(),
        name="to_cells",
    )(table_t, parts, grid_add)


def block_params(scalars, w_first, w_second, bias, lat, per, width):
    def body(s_ref, w1_hbm, w2_hbm, b_ref, w_ref, rows_ref, mask_ref, grid_ref, buf, sem):
        start = pl.multiple_of(s_ref[0] * width, width)
        quarter = s_ref[1]
        copies = [
            pltpu.make_async_copy(w.at[0, :, :, pl.ds(start, width), :], buf.at[which], sem.at[which])
            for which, w in enumerate((w1_hbm, w2_hbm))
        ]
        for copy in copies:
            copy.start()
        for layer in range(LAYERS):
            for which in range(2):
                for r in range(2):
                    rows_ref[2 * layer + which, :, r * width : (r + 1) * width] = b_ref[
                        0, layer, which, pl.ds(r, 1), pl.ds(start, width)
                    ]
            mode = quarter * per + lax.broadcasted_iota(jnp.int32, (per, 1, 2 * width), 0)
            mask_ref[layer] = (mode < s_ref[2 + layer]).astype(F32)
        rows = lax.broadcasted_iota(jnp.int32, (lat, lat), 0)
        cols = lax.broadcasted_iota(jnp.int32, (lat, lat), 1)
        eye = (rows == cols).astype(F32)
        back = ((rows + cols) % lat == 0).astype(F32)
        has_zero = (quarter == 0).astype(F32)
        grid_ref[0] = (eye + 0.5 * has_zero * (back - eye)).astype(BF16)
        grid_ref[1] = (eye - 0.5 * has_zero * (back + eye)).astype(BF16)
        for which in range(2):
            copies[which].wait()
            for layer in range(LAYERS):
                real, imag = (buf[which, layer, 0], buf[which, layer, 1])
                w_ref[2 * layer + which, :width, :width] = real
                w_ref[2 * layer + which, :width, width:] = imag
                w_ref[2 * layer + which, width:, :width] = -imag
                w_ref[2 * layer + which, width:, width:] = real

    return pl.pallas_call(
        body,
        in_specs=[SMEM, HBM, HBM, VMEM],
        out_specs=[VMEM] * 4,
        scratch_shapes=[
            pltpu.VMEM((2, LAYERS, 2, width, width), BF16),
            pltpu.SemaphoreType.DMA((2,)),
        ],
        out_shape=[
            jax.ShapeDtypeStruct((2 * LAYERS, 2 * width, 2 * width), BF16),
            jax.ShapeDtypeStruct((2 * LAYERS, 1, 2 * width), F32),
            jax.ShapeDtypeStruct((LAYERS, per, 1, 2 * width), F32),
            jax.ShapeDtypeStruct((2, lat, lat), BF16),
        ],
        compiler_params=params(),
        name="block_params",
    )(scalars, in_hbm(w_first), in_hbm(w_second), bias)


def spectral_chain(quarter, parts, mixer, mixer_t, block, lat, width, quarters):
    sources, both, _ = parts.shape
    chunk = (sources, both // 2, width)
    per = sources * (both // 2) // (2 * lat)
    tall = per * lat
    own = width // quarters
    count = 4 * LAYERS * own + 16

    def body(q_ref, parts_ref, l_ref, lt_ref, w_ref, b_ref, mask_ref, grid_ref, da_ref, *rest):
        mine_and_sent, tmp, all_ref = (rest[:quarters], rest[quarters], rest[quarters + 1])
        quarter = q_ref[0]
        mix, mix_t = (l_ref[...], lt_ref[...])

        def mixed(slot):
            part = parts_ref[:, slot * (both // 2) : (slot + 1) * (both // 2), :]
            tmp[slot] = part.reshape(2 * lat * per, width).astype(F32)
            cells = []
            for k in range(per):
                column = tmp[slot, pl.ds(k, 2 * lat, stride=per), :].astype(BF16)
                z = dot(mix, column)
                cells.append(jnp.concatenate([z[:lat], z[lat:]], axis=1))
            return jnp.concatenate(cells, axis=0)

        def through_grid(v):
            first = v[:lat]
            first = jnp.concatenate(
                [dot(grid_ref[0], first[:, :width]), dot(grid_ref[1], first[:, width:])], axis=1
            )
            return jnp.concatenate([first, v[lat:].astype(F32)], axis=0)

        def masked(v, layer):
            split = v.reshape(per, lat, 2 * width) * mask_ref[layer]
            return split.reshape(tall, 2 * width).astype(BF16)

        z = mixed(0)
        slopes = []
        lefts = {}
        index = lax.broadcasted_iota(jnp.int32, (16, width), 0)
        sums = jnp.zeros((16, width), F32)

        def products(which, layer, right, sums):
            outer = dot_cols(lefts[which, layer], right)
            total = jnp.sum(right.astype(F32), axis=0, keepdims=True)
            squares = (
                outer[:width, :width] + outer[width:, width:],
                outer[:width, width:] - outer[width:, :width],
            )
            for r in range(2):
                all_ref[(which * LAYERS + layer) * 2 + r] = squares[r]
                slot = (layer * 2 + which) * 2 + r
                sums = sums + jnp.where(index == slot, total[:, r * width : (r + 1) * width], 0.0)
            return sums

        for layer in range(LAYERS):
            z_low = z.astype(BF16)
            lefts[0, layer] = z_low
            pre = dot(z_low, w_ref[2 * layer]) + b_ref[2 * layer]
            sig = jax.nn.sigmoid(pre)
            hidden = (pre * sig).astype(BF16)
            lefts[1, layer] = hidden
            slopes.append(sig * (1.0 + pre * (1.0 - sig)))
            if layer + 1 < LAYERS:
                out = dot(hidden, w_ref[2 * layer + 1]) + b_ref[2 * layer + 1]
                z = z + through_grid(masked(out, layer))
        grad = mixed(1)
        total = None
        for layer in reversed(range(LAYERS)):
            dout = masked(grad, layer)
            sums = products(1, layer, dout, sums)
            dpre = (dot_rows(dout, w_ref[2 * layer + 1]) * slopes[layer]).astype(BF16)
            sums = products(0, layer, dpre, sums)
            dz = dot_rows(dpre, w_ref[2 * layer])
            if layer:
                grad = grad + through_grid(dz.astype(BF16))
            total = dz if total is None else total + dz
        total = total.astype(BF16)
        for k in range(per):
            part = total[k * lat : (k + 1) * lat]
            part = jnp.concatenate([part[:, :width], part[:, width:]], axis=0)
            tmp[0, pl.ds(k, 2 * lat, stride=per), :] = dot(mix_t, part)
        da_ref[...] = tmp[0].astype(BF16).reshape(chunk)
        for step, o_ref in enumerate(mine_and_sent):
            start = pl.multiple_of((quarter + step) % quarters * own, own)
            for square in range(4 * LAYERS):
                part = all_ref[square, pl.ds(start, own), :]
                o_ref[square * own : (square + 1) * own] = part.astype(o_ref.dtype)
            o_ref[4 * LAYERS * own :] = sums.astype(o_ref.dtype)

    return pl.pallas_call(
        body,
        in_specs=[SMEM] + [VMEM] * 7,
        out_specs=[VMEM] * (1 + quarters),
        scratch_shapes=[
            pltpu.VMEM((2, 2 * lat * per, width), F32),
            pltpu.VMEM((4 * LAYERS, width, width), F32),
        ],
        out_shape=[
            jax.ShapeDtypeStruct(chunk, BF16),
            jax.ShapeDtypeStruct((count, width), F32),
        ]
        + [jax.ShapeDtypeStruct((count, width), BF16)] * (quarters - 1),
        compiler_params=params(),
        name="spectral_chain",
    )(quarter, parts, mixer, mixer_t, *block)


def gradient_sum(quarter, parts, width):
    quarters = len(parts)
    own = width // quarters
    half = 2 * LAYERS * own

    def body(q_ref, *refs):
        first_hbm, second_hbm, bias_hbm, buf, bias_buf, sem = refs[quarters:]

        def added(start, size):
            total = refs[0][start : start + size]
            for ref in refs[1:quarters]:
                total = total + ref[start : start + size].astype(F32)
            return total

        copies = [
            pltpu.make_async_copy(bias_buf, bias_hbm, sem.at[2]),
            pltpu.make_async_copy(buf.at[0], first_hbm, sem.at[0]),
            pltpu.make_async_copy(buf.at[1], second_hbm, sem.at[1]),
        ]
        sums = added(2 * half, 16)[:8]
        bias_buf[...] = pltpu.roll(sums, (width - q_ref[0] * own) % width, 1)[:, :own]
        copies[0].start()
        for which in range(2):
            buf[which] = added(which * half, half)
            copies[1 + which].start()
        for copy in copies:
            copy.wait()

    return pl.pallas_call(
        body,
        in_specs=[SMEM] + [VMEM] * quarters,
        out_specs=[HBM] * 3,
        scratch_shapes=[
            pltpu.VMEM((2, half, width), F32),
            pltpu.VMEM((8, own), F32),
            pltpu.SemaphoreType.DMA((3,)),
        ],
        out_shape=[
            jax.ShapeDtypeStruct((half, width), F32),
            jax.ShapeDtypeStruct((half, width), F32),
            jax.ShapeDtypeStruct((8, own), F32),
        ],
        compiler_params=params(),
        name="gradient_sum",
    )(quarter, *parts)


def on_device(section_input, handoff, loss_grad, w_first, w_second, bias, kept):
    lat_count = lax.axis_size("lat")
    sections = lax.axis_size("section")
    _, rows, lon, channels = section_input.shape
    width = w_first.shape[-1]
    blocks = channels // width
    quarters = lat_count // blocks
    lat = rows * lat_count
    forward = lon_table(lon, rows, quarters, False)
    inverse = lon_table(lon, rows, quarters, True)
    mixer = lat_table(lat, rows)
    place = lax.axis_index("lat")
    section = lax.axis_index("section")
    block = place // quarters
    quarter = (place % quarters).reshape(1)
    limits = lax.dynamic_slice(kept, (0, 0, block), (1, LAYERS, 1)).reshape(-1)
    scalars = jnp.concatenate([jnp.stack([block, place % quarters]), limits])
    ring = [(s, (s - 1) % sections) for s in range(sections)]
    cells = (rows * lon, channels)

    handed_du = (handoff.reshape(cells), loss_grad.reshape(cells))
    du = to_spectral(section.reshape(1), handed_du, inverse, quarters, width)
    du = lax.ppermute(du, "section", ring)
    spec = to_spectral(section.reshape(1), (section_input.reshape(cells),), forward, quarters, width)
    later, spec = lax.optimization_barrier((handoff, spec))
    both = jnp.concatenate([spec, du], axis=1)
    both = lax.all_to_all(both, "lat", split_axis=0, concat_axis=0, tiled=True)
    received = lax.ppermute(later, "section", ring)
    cot = jnp.where(section == sections - 1, loss_grad, received[0]).reshape(cells)
    per = MAXK // quarters
    own_params = block_params(scalars, w_first, w_second, bias, lat, per, width)
    cot, both = lax.optimization_barrier((cot, both))
    da, *parts = spectral_chain(
        quarter, both, mixer, mixer.T.copy(), own_params, lat, width, quarters
    )
    da = lax.all_to_all(da, "lat", split_axis=0, concat_axis=0, tiled=True)
    for step in range(1, quarters):
        pairs = [
            (b * quarters + q, b * quarters + (q + step) % quarters)
            for b in range(blocks)
            for q in range(quarters)
        ]
        parts[step] = lax.ppermute(parts[step], "lat", pairs)
    handed = to_cells(da, forward.T.copy(), cot, quarters, width)
    handed, parts[0] = lax.optimization_barrier((handed, parts[0]))
    first, second, biases = gradient_sum(quarter, parts, width)
    own = width // quarters
    return (
        handed.reshape(1, rows, lon, channels),
        first.reshape(1, LAYERS, 2, own, width),
        second.reshape(1, LAYERS, 2, own, width),
        biases.reshape(1, LAYERS, 2, 2, own),
    )


def solution(mesh):
    return jax.shard_map(
        on_device,
        mesh=mesh,
        in_specs=(
            P("section", "lat", None, None),
            P("section", "lat", None, None),
            P("lat", None, None),
            P("section", None, None, None, None),
            P("section", None, None, None, None),
            P("section", None, None, None, None),
            P("section", None, None),
        ),
        out_specs=(
            P("section", "lat", None, None),
            P("section", None, None, "lat", None),
            P("section", None, None, "lat", None),
            P("section", None, None, None, "lat"),
        ),
        check_vma=False,
    )
```

```python
import math

import jax
import jax.numpy as jnp
import numpy as np
from jax import lax
from jax.experimental import pallas as pl
from jax.experimental.pallas import tpu as pltpu
from jax.sharding import PartitionSpec as P

LAYERS = 2
MAXK = 32
F32 = jnp.float32
BF16 = jnp.bfloat16


def lon_table(lon, rows, quarters, weighted):
    per = MAXK // quarters
    freqs = np.arange(MAXK)
    phase = 2.0 * math.pi * ((freqs[:, None] * np.arange(lon)[None, :]) % lon) / lon
    table = np.stack([np.cos(phase), -np.sin(phase)]) / math.sqrt(lon)
    table[1, 0] = 0.0
    table = table.astype(jnp.bfloat16).astype(np.float32)
    if weighted:
        table = table * np.where(freqs == 0, 1.0, 2.0)[None, :, None]
    split = table.reshape(2, quarters, per, lon).transpose(1, 0, 2, 3)
    full = np.zeros((quarters, 2, rows, per, rows, lon), np.float32)
    for row in range(rows):
        full[:, :, row, :, row, :] = split
    return full.reshape(quarters * 2 * rows * per, rows * lon).astype(jnp.bfloat16)


def lat_table(lat, rows):
    phase = 2.0 * math.pi * ((np.arange(lat)[:, None] * np.arange(lat)[None, :]) % lat) / lat
    cosine = np.cos(phase) / math.sqrt(lat)
    sine = np.sin(phase) / math.sqrt(lat)
    mixer = np.block([[cosine, sine], [-sine, cosine]])
    mixer = mixer.reshape(2 * lat, 2, lat // rows, rows).transpose(0, 2, 1, 3)
    return mixer.reshape(2 * lat, 2 * lat).astype(jnp.bfloat16)


def dot(left, right):
    return jnp.dot(left, right, preferred_element_type=F32)


def dot_cols(left, right):
    return lax.dot_general(left, right, (((0,), (0,)), ((), ())), preferred_element_type=F32)


def params(**kw):
    return pltpu.CompilerParams(vmem_limit_bytes=12 * 1024 * 1024, **kw)


VMEM = pl.BlockSpec(memory_space=pltpu.VMEM)
SMEM = pl.BlockSpec(memory_space=pltpu.SMEM)
HBM = pl.BlockSpec(memory_space=pltpu.HBM)


def in_hbm(value):
    return pltpu.with_memory_space_constraint(value, pltpu.HBM)


def to_spectral(scalars, sources, table, quarters, width, joined):
    cells, channels = sources[0].shape
    rows = table.shape[0] // quarters
    blocks = channels // width
    cuts = 2
    span = cells // cuts

    def body(s_ref, t_hbm, *refs):
        given = refs[: len(sources)]
        out, t_buf, x_buf, o_buf, t_sem, x_sem, o_sem = refs[len(sources) :]
        o_ref = o_buf if joined else out

        def piece(source, cut):
            part = pl.ds(cut * span, span)
            return pltpu.make_async_copy(source.at[part, :], x_buf.at[part, :], x_sem.at[cut])

        def begin(source):
            for cut in range(cuts):
                piece(source, cut).start()

        table_copy = pltpu.make_async_copy(t_hbm, t_buf, t_sem)
        table_copy.start()
        if len(given) == 1:
            begin(given[0])
        else:
            pl.when(s_ref[0] != 0)(lambda: begin(given[0]))
            pl.when(s_ref[0] == 0)(lambda: begin(given[1]))
        table_copy.wait()
        t = t_buf[...]
        for cut in range(cuts):
            piece(given[0], cut).wait()
        step = 2 * width
        for cut in range(channels // step):
            y = dot(t, x_buf[:, cut * step : (cut + 1) * step]).astype(BF16)
            for b in range(2):
                for q in range(quarters):
                    owner = (cut * 2 + b) * quarters + q
                    o_ref[owner] = y[q * rows : (q + 1) * rows, b * width : (b + 1) * width]
        if joined:
            out_copy = pltpu.make_async_copy(o_buf, out.at[:, pl.ds(0, rows), :], o_sem)
            out_copy.start()
            out_copy.wait()

    return pl.pallas_call(
        body,
        in_specs=[SMEM, HBM] + [HBM] * len(sources),
        out_specs=HBM if joined else VMEM,
        scratch_shapes=[
            pltpu.VMEM(table.shape, BF16),
            pltpu.VMEM((cells, channels), BF16),
            pltpu.VMEM((blocks * quarters, rows, width), BF16),
            pltpu.SemaphoreType.DMA(()),
            pltpu.SemaphoreType.DMA((cuts,)),
            pltpu.SemaphoreType.DMA(()),
        ],
        out_shape=jax.ShapeDtypeStruct((blocks * quarters, (1 + joined) * rows, width), BF16),
        compiler_params=params(),
        name="to_spectral",
    )(scalars, in_hbm(jnp.asarray(table)), *[in_hbm(source) for source in sources])


def lower_halves(both, du):
    rows = du.shape[1]

    def body(_, du_ref, o_hbm, sem):
        copy = pltpu.make_async_copy(du_ref, o_hbm.at[:, pl.ds(rows, rows), :], sem)
        copy.start()
        copy.wait()

    return pl.pallas_call(
        body,
        in_specs=[HBM, VMEM],
        out_specs=HBM,
        scratch_shapes=[pltpu.SemaphoreType.DMA(())],
        out_shape=jax.ShapeDtypeStruct(both.shape, BF16),
        input_output_aliases={0: 0},
        compiler_params=params(),
        name="lower_halves",
    )(both, du)


def to_cells(parts, table_t, grid_add, quarters, width):
    cells, channels = grid_add.shape
    rows = parts.shape[1]
    blocks = channels // width
    cuts = 2
    span = cells // cuts

    def body(t_ref, p_ref, g_ref, o_hbm, buf, sem):
        copies = []
        for cut in range(cuts):
            own = slice(cut * span, (cut + 1) * span)
            table = t_ref[own]
            for block in range(0, blocks, 2):
                part = p_ref[block * quarters : (block + 2) * quarters]
                part = part.reshape(2, quarters * rows, width)
                part = jnp.concatenate([part[0], part[1]], axis=1)
                lanes = slice(block * width, (block + 2) * width)
                mixed = g_ref[own, lanes].astype(F32) + dot(table, part)
                buf[own, lanes] = mixed.astype(BF16)
            copies.append(pltpu.make_async_copy(buf.at[own], o_hbm.at[own], sem.at[cut]))
            copies[-1].start()
        for copy in copies:
            copy.wait()

    return pl.pallas_call(
        body,
        in_specs=[VMEM, VMEM, VMEM],
        out_specs=HBM,
        scratch_shapes=[
            pltpu.VMEM((cells, channels), BF16),
            pltpu.SemaphoreType.DMA((cuts,)),
        ],
        out_shape=jax.ShapeDtypeStruct((cells, channels), BF16),
        compiler_params=params(),
        name="to_cells",
    )(table_t, parts, grid_add)


def block_params(scalars, w_first, w_second, bias, lat, per, width):
    def body(s_ref, w1_hbm, w2_hbm, b_ref, w_ref, wt_ref, rows_ref, mask_ref, grid_ref, buf, sem):
        start = pl.multiple_of(s_ref[0] * width, width)
        quarter = s_ref[1]
        copies = [
            pltpu.make_async_copy(w.at[0, :, :, pl.ds(start, width), :], buf.at[which], sem.at[which])
            for which, w in enumerate((w1_hbm, w2_hbm))
        ]
        for copy in copies:
            copy.start()
        for layer in range(LAYERS):
            for which in range(2):
                for r in range(2):
                    rows_ref[2 * layer + which, :, r * width : (r + 1) * width] = b_ref[
                        0, layer, which, pl.ds(r, 1), pl.ds(start, width)
                    ]
            mode = quarter * per + lax.broadcasted_iota(jnp.int32, (per, 1, 2 * width), 0)
            mask_ref[layer] = (mode < s_ref[2 + layer]).astype(F32)
        rows = lax.broadcasted_iota(jnp.int32, (lat, lat), 0)
        cols = lax.broadcasted_iota(jnp.int32, (lat, lat), 1)
        eye = (rows == cols).astype(F32)
        back = ((rows + cols) % lat == 0).astype(F32)
        has_zero = (quarter == 0).astype(F32)
        grid_ref[0] = (eye + 0.5 * has_zero * (back - eye)).astype(BF16)
        grid_ref[1] = (eye - 0.5 * has_zero * (back + eye)).astype(BF16)
        for which in range(2):
            copies[which].wait()
            for layer in range(LAYERS):
                real, imag = (buf[which, layer, 0], buf[which, layer, 1])
                w_ref[2 * layer + which, :width, :width] = real
                w_ref[2 * layer + which, :width, width:] = imag
                w_ref[2 * layer + which, width:, :width] = -imag
                w_ref[2 * layer + which, width:, width:] = real
                real, imag = (real.astype(F32).T.astype(BF16), imag.astype(F32).T.astype(BF16))
                wt_ref[2 * layer + which, :width, :width] = real
                wt_ref[2 * layer + which, :width, width:] = -imag
                wt_ref[2 * layer + which, width:, :width] = imag
                wt_ref[2 * layer + which, width:, width:] = real

    return pl.pallas_call(
        body,
        in_specs=[SMEM, HBM, HBM, VMEM],
        out_specs=[VMEM] * 5,
        scratch_shapes=[
            pltpu.VMEM((2, LAYERS, 2, width, width), BF16),
            pltpu.SemaphoreType.DMA((2,)),
        ],
        out_shape=[
            jax.ShapeDtypeStruct((2 * LAYERS, 2 * width, 2 * width), BF16),
            jax.ShapeDtypeStruct((2 * LAYERS, 2 * width, 2 * width), BF16),
            jax.ShapeDtypeStruct((2 * LAYERS, 1, 2 * width), F32),
            jax.ShapeDtypeStruct((LAYERS, per, 1, 2 * width), F32),
            jax.ShapeDtypeStruct((2, lat, lat), BF16),
        ],
        compiler_params=params(),
        name="block_params",
    )(scalars, in_hbm(w_first), in_hbm(w_second), bias)


def spectral_chain(quarter, parts, mixer, mixer_t, block, lat, width, quarters):
    sources, both, _ = parts.shape
    chunk = (sources, both // 2, width)
    per = sources * (both // 2) // (2 * lat)
    tall = per * lat
    own = width // quarters
    count = 4 * LAYERS * own + 16

    def body(q_ref, parts_ref, l_ref, lt_ref, w_ref, wt_ref, b_ref, mask_ref, *more):
        grid_ref, da_ref, *mine_and_sent = more[:-2]
        tmp, all_ref = more[-2:]
        quarter = q_ref[0]
        mix, mix_t = (l_ref[...], lt_ref[...])

        for slot in range(2):
            part = parts_ref[:, slot * (both // 2) : (slot + 1) * (both // 2), :]
            tmp[slot] = part.reshape(2 * lat * per, width).astype(F32)
        mixed = ([], [])
        for k in range(per):
            columns = [tmp[slot, pl.ds(k, 2 * lat, stride=per), :] for slot in range(2)]
            cells = dot(mix, jnp.concatenate(columns, axis=1).astype(BF16))
            for slot in range(2):
                lanes = slice(slot * width, (slot + 1) * width)
                mixed[slot].append(
                    jnp.concatenate([cells[:lat, lanes], cells[lat:, lanes]], axis=1)
                )

        def through_grid(v):
            first = v[:lat]
            first = jnp.concatenate(
                [dot(grid_ref[0], first[:, :width]), dot(grid_ref[1], first[:, width:])], axis=1
            )
            return jnp.concatenate([first, v[lat:].astype(F32)], axis=0)

        def masked(v, layer):
            split = v.reshape(per, lat, 2 * width) * mask_ref[layer]
            return split.reshape(tall, 2 * width).astype(BF16)

        z = jnp.concatenate(mixed[0], axis=0)
        slopes = []
        lefts = {}
        index = lax.broadcasted_iota(jnp.int32, (16, width), 0)
        sums = jnp.zeros((16, width), F32)

        def products(which, layer, right, sums):
            outer = dot_cols(lefts[which, layer], right)
            total = jnp.sum(right.astype(F32), axis=0, keepdims=True)
            squares = (
                outer[:width, :width] + outer[width:, width:],
                outer[:width, width:] - outer[width:, :width],
            )
            for r in range(2):
                all_ref[(which * LAYERS + layer) * 2 + r] = squares[r]
                slot = (layer * 2 + which) * 2 + r
                sums = sums + jnp.where(index == slot, total[:, r * width : (r + 1) * width], 0.0)
            return sums

        for layer in range(LAYERS):
            z_low = z.astype(BF16)
            lefts[0, layer] = z_low
            pre = dot(z_low, w_ref[2 * layer]) + b_ref[2 * layer]
            sig = jax.nn.sigmoid(pre)
            hidden = (pre * sig).astype(BF16)
            lefts[1, layer] = hidden
            slopes.append(sig * (1.0 + pre * (1.0 - sig)))
            if layer + 1 < LAYERS:
                out = dot(hidden, w_ref[2 * layer + 1]) + b_ref[2 * layer + 1]
                z = z + through_grid(masked(out, layer))
        grad = jnp.concatenate(mixed[1], axis=0)
        total = None
        for layer in reversed(range(LAYERS)):
            dout = masked(grad, layer)
            sums = products(1, layer, dout, sums)
            dpre = (dot(dout, wt_ref[2 * layer + 1]) * slopes[layer]).astype(BF16)
            sums = products(0, layer, dpre, sums)
            dz = dot(dpre, wt_ref[2 * layer])
            if layer:
                grad = grad + through_grid(dz.astype(BF16))
            total = dz if total is None else total + dz
        total = total.astype(BF16)
        for k in range(0, per, 2):
            pair = [total[j * lat : (j + 1) * lat] for j in (k, k + 1)]
            pair = [jnp.concatenate([v[:, :width], v[:, width:]], axis=0) for v in pair]
            bands = dot(mix_t, jnp.concatenate(pair, axis=1))
            for j in range(2):
                lanes = slice(j * width, (j + 1) * width)
                tmp[0, pl.ds(k + j, 2 * lat, stride=per), :] = bands[:, lanes]
        da_ref[...] = tmp[0].astype(BF16).reshape(chunk)
        for step, o_ref in enumerate(mine_and_sent):
            start = pl.multiple_of((quarter + step) % quarters * own, own)
            for square in range(4 * LAYERS):
                part = all_ref[square, pl.ds(start, own), :]
                o_ref[square * own : (square + 1) * own] = part.astype(o_ref.dtype)
            o_ref[4 * LAYERS * own :] = sums.astype(o_ref.dtype)

    return pl.pallas_call(
        body,
        in_specs=[SMEM] + [VMEM] * 8,
        out_specs=[VMEM] * (1 + quarters),
        scratch_shapes=[
            pltpu.VMEM((2, 2 * lat * per, width), F32),
            pltpu.VMEM((4 * LAYERS, width, width), F32),
        ],
        out_shape=[
            jax.ShapeDtypeStruct(chunk, BF16),
            jax.ShapeDtypeStruct((count, width), F32),
        ]
        + [jax.ShapeDtypeStruct((count, width), BF16)] * (quarters - 1),
        compiler_params=params(),
        name="spectral_chain",
    )(quarter, parts, mixer, mixer_t, *block)


def gradient_sum(quarter, parts, width):
    quarters = len(parts)
    own = width // quarters
    half = 2 * LAYERS * own

    def body(q_ref, *refs):
        first_hbm, second_hbm, bias_hbm, buf, bias_buf, sem = refs[quarters:]

        def added(start, size):
            total = refs[0][start : start + size]
            for ref in refs[1:quarters]:
                total = total + ref[start : start + size].astype(F32)
            return total

        copies = [
            pltpu.make_async_copy(bias_buf, bias_hbm, sem.at[2]),
            pltpu.make_async_copy(buf.at[0], first_hbm, sem.at[0]),
            pltpu.make_async_copy(buf.at[1], second_hbm, sem.at[1]),
        ]
        sums = added(2 * half, 16)[:8]
        bias_buf[...] = pltpu.roll(sums, (width - q_ref[0] * own) % width, 1)[:, :own]
        copies[0].start()
        for which in range(2):
            buf[which] = added(which * half, half)
            copies[1 + which].start()
        for copy in copies:
            copy.wait()

    return pl.pallas_call(
        body,
        in_specs=[SMEM] + [VMEM] * quarters,
        out_specs=[HBM] * 3,
        scratch_shapes=[
            pltpu.VMEM((2, half, width), F32),
            pltpu.VMEM((8, own), F32),
            pltpu.SemaphoreType.DMA((3,)),
        ],
        out_shape=[
            jax.ShapeDtypeStruct((half, width), F32),
            jax.ShapeDtypeStruct((half, width), F32),
            jax.ShapeDtypeStruct((8, own), F32),
        ],
        compiler_params=params(),
        name="gradient_sum",
    )(quarter, *parts)


def on_device(section_input, handoff, loss_grad, w_first, w_second, bias, kept):
    lat_count = lax.axis_size("lat")
    sections = lax.axis_size("section")
    _, rows, lon, channels = section_input.shape
    width = w_first.shape[-1]
    blocks = channels // width
    quarters = lat_count // blocks
    lat = rows * lat_count
    forward = lon_table(lon, rows, quarters, False)
    inverse = lon_table(lon, rows, quarters, True)
    mixer = lat_table(lat, rows)
    place = lax.axis_index("lat")
    section = lax.axis_index("section")
    block = place // quarters
    quarter = (place % quarters).reshape(1)
    limits = lax.dynamic_slice(kept, (0, 0, block), (1, LAYERS, 1)).reshape(-1)
    scalars = jnp.concatenate([jnp.stack([block, place % quarters]), limits])
    ring = [(s, (s - 1) % sections) for s in range(sections)]
    cells = (rows * lon, channels)

    handed_du = (handoff.reshape(cells), loss_grad.reshape(cells))
    du = to_spectral(section.reshape(1), handed_du, inverse, quarters, width, False)
    du = lax.ppermute(du, "section", ring)
    x = section_input.reshape(cells)
    both = to_spectral(section.reshape(1), (x,), forward, quarters, width, True)
    later, both = lax.optimization_barrier((handoff, both))
    both = lower_halves(both, du)
    both = lax.all_to_all(both, "lat", split_axis=0, concat_axis=0, tiled=True)
    received = lax.ppermute(later, "section", ring)
    cot = jnp.where(section == sections - 1, loss_grad, received[0]).reshape(cells)
    per = MAXK // quarters
    own_params = block_params(scalars, w_first, w_second, bias, lat, per, width)
    cot, both = lax.optimization_barrier((cot, both))
    da, *parts = spectral_chain(
        quarter, both, mixer, mixer.T.copy(), own_params, lat, width, quarters
    )
    da = lax.all_to_all(da, "lat", split_axis=0, concat_axis=0, tiled=True)
    for step in (2, 1, 3):
        pairs = [
            (b * quarters + q, b * quarters + (q + step) % quarters)
            for b in range(blocks)
            for q in range(quarters)
        ]
        parts[step] = lax.ppermute(parts[step], "lat", pairs)
    handed = to_cells(da, forward.T.copy(), cot, quarters, width)
    handed, parts[0] = lax.optimization_barrier((handed, parts[0]))
    first, second, biases = gradient_sum(quarter, parts, width)
    own = width // quarters
    return (
        handed.reshape(1, rows, lon, channels),
        first.reshape(1, LAYERS, 2, own, width),
        second.reshape(1, LAYERS, 2, own, width),
        biases.reshape(1, LAYERS, 2, 2, own),
    )


def solution(mesh):
    return jax.shard_map(
        on_device,
        mesh=mesh,
        in_specs=(
            P("section", "lat", None, None),
            P("section", "lat", None, None),
            P("lat", None, None),
            P("section", None, None, None, None),
            P("section", None, None, None, None),
            P("section", None, None, None, None),
            P("section", None, None),
        ),
        out_specs=(
            P("section", "lat", None, None),
            P("section", None, None, "lat", None),
            P("section", None, None, "lat", None),
            P("section", None, None, None, "lat"),
        ),
        check_vma=False,
    )
```

```python
import math

import jax
import jax.numpy as jnp
import numpy as np
from jax import lax
from jax.experimental import pallas as pl
from jax.experimental.pallas import tpu as pltpu
from jax.sharding import PartitionSpec as P

LAYERS = 2
MAXK = 32
F32 = jnp.float32
BF16 = jnp.bfloat16


def lon_table(lon, rows, quarters, weighted):
    per = MAXK // quarters
    freqs = np.arange(MAXK)
    phase = 2.0 * math.pi * ((freqs[:, None] * np.arange(lon)[None, :]) % lon) / lon
    table = np.stack([np.cos(phase), -np.sin(phase)]) / math.sqrt(lon)
    table[1, 0] = 0.0
    table = table.astype(jnp.bfloat16).astype(np.float32)
    if weighted:
        table = table * np.where(freqs == 0, 1.0, 2.0)[None, :, None]
    split = table.reshape(2, quarters, per, lon).transpose(1, 0, 2, 3)
    full = np.zeros((quarters, 2, rows, per, rows, lon), np.float32)
    for row in range(rows):
        full[:, :, row, :, row, :] = split
    return full.reshape(quarters * 2 * rows * per, rows * lon).astype(jnp.bfloat16)


def lat_table(lat, rows):
    phase = 2.0 * math.pi * ((np.arange(lat)[:, None] * np.arange(lat)[None, :]) % lat) / lat
    cosine = np.cos(phase) / math.sqrt(lat)
    sine = np.sin(phase) / math.sqrt(lat)
    mixer = np.block([[cosine, sine], [-sine, cosine]])
    mixer = mixer.reshape(2 * lat, 2, lat // rows, rows).transpose(0, 2, 1, 3)
    return mixer.reshape(2 * lat, 2 * lat).astype(jnp.bfloat16)


def dot(left, right):
    return jnp.dot(left, right, preferred_element_type=F32)


def dot_cols(left, right):
    return lax.dot_general(left, right, (((0,), (0,)), ((), ())), preferred_element_type=F32)


def params(**kw):
    return pltpu.CompilerParams(vmem_limit_bytes=12 * 1024 * 1024, **kw)


VMEM = pl.BlockSpec(memory_space=pltpu.VMEM)
SMEM = pl.BlockSpec(memory_space=pltpu.SMEM)
HBM = pl.BlockSpec(memory_space=pltpu.HBM)


def in_hbm(value):
    return pltpu.with_memory_space_constraint(value, pltpu.HBM)


def to_spectral(scalars, sources, table, quarters, width, joined):
    cells, channels = sources[0].shape
    rows = table.shape[0] // quarters
    blocks = channels // width
    cuts = 2
    span = cells // cuts

    def body(s_ref, t_hbm, *refs):
        given = refs[: len(sources)]
        out, t_buf, x_buf, o_buf, t_sem, x_sem, o_sem = refs[len(sources) :]
        o_ref = o_buf if joined else out

        def piece(source, cut):
            part = pl.ds(cut * span, span)
            return pltpu.make_async_copy(source.at[part, :], x_buf.at[part, :], x_sem.at[cut])

        def begin(source):
            for cut in range(cuts):
                piece(source, cut).start()

        table_copy = pltpu.make_async_copy(t_hbm, t_buf, t_sem)
        table_copy.start()
        if len(given) == 1:
            begin(given[0])
        else:
            pl.when(s_ref[0] != 0)(lambda: begin(given[0]))
            pl.when(s_ref[0] == 0)(lambda: begin(given[1]))
        table_copy.wait()
        t = t_buf[...]
        for cut in range(cuts):
            piece(given[0], cut).wait()
        step = 2 * width
        for cut in range(channels // step):
            y = dot(t, x_buf[:, cut * step : (cut + 1) * step]).astype(BF16)
            for b in range(2):
                for q in range(quarters):
                    owner = (cut * 2 + b) * quarters + q
                    o_ref[owner] = y[q * rows : (q + 1) * rows, b * width : (b + 1) * width]
        if joined:
            out_copy = pltpu.make_async_copy(o_buf, out.at[:, pl.ds(0, rows), :], o_sem)
            out_copy.start()
            out_copy.wait()

    return pl.pallas_call(
        body,
        in_specs=[SMEM, HBM] + [HBM] * len(sources),
        out_specs=HBM if joined else VMEM,
        scratch_shapes=[
            pltpu.VMEM(table.shape, BF16),
            pltpu.VMEM((cells, channels), BF16),
            pltpu.VMEM((blocks * quarters, rows, width), BF16),
            pltpu.SemaphoreType.DMA(()),
            pltpu.SemaphoreType.DMA((cuts,)),
            pltpu.SemaphoreType.DMA(()),
        ],
        out_shape=jax.ShapeDtypeStruct((blocks * quarters, (1 + joined) * rows, width), BF16),
        compiler_params=params(),
        name="to_spectral",
    )(scalars, in_hbm(jnp.asarray(table)), *[in_hbm(source) for source in sources])


def lower_halves(both, du):
    rows = du.shape[1]

    def body(_, du_ref, o_hbm, sem):
        copy = pltpu.make_async_copy(du_ref, o_hbm.at[:, pl.ds(rows, rows), :], sem)
        copy.start()
        copy.wait()

    return pl.pallas_call(
        body,
        in_specs=[HBM, VMEM],
        out_specs=HBM,
        scratch_shapes=[pltpu.SemaphoreType.DMA(())],
        out_shape=jax.ShapeDtypeStruct(both.shape, BF16),
        input_output_aliases={0: 0},
        compiler_params=params(),
        name="lower_halves",
    )(both, du)


def to_cells(parts, table_t, grid_add, quarters, width):
    cells, channels = grid_add.shape
    rows = parts.shape[1]
    blocks = channels // width
    cuts = 2
    span = cells // cuts

    def body(t_ref, p_ref, g_ref, o_hbm, buf, sem):
        copies = []
        for cut in range(cuts):
            own = slice(cut * span, (cut + 1) * span)
            table = t_ref[own]
            for block in range(0, blocks, 2):
                part = p_ref[block * quarters : (block + 2) * quarters]
                part = part.reshape(2, quarters * rows, width)
                part = jnp.concatenate([part[0], part[1]], axis=1)
                lanes = slice(block * width, (block + 2) * width)
                mixed = g_ref[own, lanes].astype(F32) + dot(table, part)
                buf[own, lanes] = mixed.astype(BF16)
            copies.append(pltpu.make_async_copy(buf.at[own], o_hbm.at[own], sem.at[cut]))
            copies[-1].start()
        for copy in copies:
            copy.wait()

    return pl.pallas_call(
        body,
        in_specs=[VMEM, VMEM, VMEM],
        out_specs=HBM,
        scratch_shapes=[
            pltpu.VMEM((cells, channels), BF16),
            pltpu.SemaphoreType.DMA((cuts,)),
        ],
        out_shape=jax.ShapeDtypeStruct((cells, channels), BF16),
        compiler_params=params(),
        name="to_cells",
    )(table_t, parts, grid_add)


def block_params(scalars, w_first, w_second, bias, lat, per, width):
    def body(s_ref, w1_hbm, w2_hbm, b_ref, w_ref, wt_ref, rows_ref, mask_ref, grid_ref, buf, sem):
        start = pl.multiple_of(s_ref[0] * width, width)
        quarter = s_ref[1]
        copies = [
            pltpu.make_async_copy(w.at[0, :, :, pl.ds(start, width), :], buf.at[which], sem.at[which])
            for which, w in enumerate((w1_hbm, w2_hbm))
        ]
        for copy in copies:
            copy.start()
        for layer in range(LAYERS):
            for which in range(2):
                for r in range(2):
                    rows_ref[2 * layer + which, :, r * width : (r + 1) * width] = b_ref[
                        0, layer, which, pl.ds(r, 1), pl.ds(start, width)
                    ]
            mode = quarter * per + lax.broadcasted_iota(jnp.int32, (per, 1, 2 * width), 0)
            mask_ref[layer] = (mode < s_ref[2 + layer]).astype(F32)
        rows = lax.broadcasted_iota(jnp.int32, (lat, lat), 0)
        cols = lax.broadcasted_iota(jnp.int32, (lat, lat), 1)
        eye = (rows == cols).astype(F32)
        back = ((rows + cols) % lat == 0).astype(F32)
        has_zero = (quarter == 0).astype(F32)
        grid_ref[0] = (eye + 0.5 * has_zero * (back - eye)).astype(BF16)
        grid_ref[1] = (eye - 0.5 * has_zero * (back + eye)).astype(BF16)
        for which in range(2):
            copies[which].wait()
            for layer in range(LAYERS):
                real, imag = (buf[which, layer, 0], buf[which, layer, 1])
                w_ref[2 * layer + which, :width, :width] = real
                w_ref[2 * layer + which, :width, width:] = imag
                w_ref[2 * layer + which, width:, :width] = -imag
                w_ref[2 * layer + which, width:, width:] = real
                real, imag = (real.astype(F32).T.astype(BF16), imag.astype(F32).T.astype(BF16))
                wt_ref[2 * layer + which, :width, :width] = real
                wt_ref[2 * layer + which, :width, width:] = -imag
                wt_ref[2 * layer + which, width:, :width] = imag
                wt_ref[2 * layer + which, width:, width:] = real

    return pl.pallas_call(
        body,
        in_specs=[SMEM, HBM, HBM, VMEM],
        out_specs=[VMEM] * 5,
        scratch_shapes=[
            pltpu.VMEM((2, LAYERS, 2, width, width), BF16),
            pltpu.SemaphoreType.DMA((2,)),
        ],
        out_shape=[
            jax.ShapeDtypeStruct((2 * LAYERS, 2 * width, 2 * width), BF16),
            jax.ShapeDtypeStruct((2 * LAYERS, 2 * width, 2 * width), BF16),
            jax.ShapeDtypeStruct((2 * LAYERS, 1, 2 * width), F32),
            jax.ShapeDtypeStruct((LAYERS, per, 1, 2 * width), F32),
            jax.ShapeDtypeStruct((2, lat, lat), BF16),
        ],
        compiler_params=params(),
        cost_estimate=pl.CostEstimate(flops=2 * 10**10, transcendentals=0, bytes_accessed=1 << 20),
        name="block_params",
    )(scalars, in_hbm(w_first), in_hbm(w_second), bias)


def spectral_chain(quarter, parts, mixer, mixer_t, block, lat, width, quarters):
    sources, both, _ = parts.shape
    chunk = (sources, both // 2, width)
    per = sources * (both // 2) // (2 * lat)
    tall = per * lat
    own = width // quarters
    count = 4 * LAYERS * own + 16

    def body(q_ref, parts_ref, l_ref, lt_ref, w_ref, wt_ref, b_ref, mask_ref, *more):
        grid_ref, da_ref, *mine_and_sent = more[:-2]
        tmp, all_ref = more[-2:]
        quarter = q_ref[0]
        mix, mix_t = (l_ref[...], lt_ref[...])

        for slot in range(2):
            part = parts_ref[:, slot * (both // 2) : (slot + 1) * (both // 2), :]
            tmp[slot] = part.reshape(2 * lat * per, width).astype(F32)
        mixed = ([], [])
        for k in range(per):
            columns = [tmp[slot, pl.ds(k, 2 * lat, stride=per), :] for slot in range(2)]
            cells = dot(mix, jnp.concatenate(columns, axis=1).astype(BF16))
            for slot in range(2):
                lanes = slice(slot * width, (slot + 1) * width)
                mixed[slot].append(
                    jnp.concatenate([cells[:lat, lanes], cells[lat:, lanes]], axis=1)
                )

        def through_grid(v):
            first = v[:lat]
            first = jnp.concatenate(
                [dot(grid_ref[0], first[:, :width]), dot(grid_ref[1], first[:, width:])], axis=1
            )
            return jnp.concatenate([first, v[lat:].astype(F32)], axis=0)

        def masked(v, layer):
            split = v.reshape(per, lat, 2 * width) * mask_ref[layer]
            return split.reshape(tall, 2 * width).astype(BF16)

        z = jnp.concatenate(mixed[0], axis=0)
        slopes = []
        lefts = {}
        index = lax.broadcasted_iota(jnp.int32, (16, width), 0)
        sums = jnp.zeros((16, width), F32)

        def products(which, layer, right, sums):
            outer = dot_cols(lefts[which, layer], right)
            total = jnp.sum(right.astype(F32), axis=0, keepdims=True)
            squares = (
                outer[:width, :width] + outer[width:, width:],
                outer[:width, width:] - outer[width:, :width],
            )
            for r in range(2):
                all_ref[(which * LAYERS + layer) * 2 + r] = squares[r]
                slot = (layer * 2 + which) * 2 + r
                sums = sums + jnp.where(index == slot, total[:, r * width : (r + 1) * width], 0.0)
            return sums

        for layer in range(LAYERS):
            z_low = z.astype(BF16)
            lefts[0, layer] = z_low
            pre = dot(z_low, w_ref[2 * layer]) + b_ref[2 * layer]
            sig = jax.nn.sigmoid(pre)
            hidden = (pre * sig).astype(BF16)
            lefts[1, layer] = hidden
            slopes.append(sig * (1.0 + pre * (1.0 - sig)))
            if layer + 1 < LAYERS:
                out = dot(hidden, w_ref[2 * layer + 1]) + b_ref[2 * layer + 1]
                z = z + through_grid(masked(out, layer))
        grad = jnp.concatenate(mixed[1], axis=0)
        total = None
        for layer in reversed(range(LAYERS)):
            dout = masked(grad, layer)
            sums = products(1, layer, dout, sums)
            dpre = (dot(dout, wt_ref[2 * layer + 1]) * slopes[layer]).astype(BF16)
            sums = products(0, layer, dpre, sums)
            dz = dot(dpre, wt_ref[2 * layer])
            if layer:
                grad = grad + through_grid(dz.astype(BF16))
            total = dz if total is None else total + dz
        total = total.astype(BF16)
        for k in range(0, per, 2):
            pair = [total[j * lat : (j + 1) * lat] for j in (k, k + 1)]
            pair = [jnp.concatenate([v[:, :width], v[:, width:]], axis=0) for v in pair]
            bands = dot(mix_t, jnp.concatenate(pair, axis=1))
            for j in range(2):
                lanes = slice(j * width, (j + 1) * width)
                tmp[0, pl.ds(k + j, 2 * lat, stride=per), :] = bands[:, lanes]
        da_ref[...] = tmp[0].astype(BF16).reshape(chunk)
        for step, o_ref in enumerate(mine_and_sent):
            start = pl.multiple_of((quarter + step) % quarters * own, own)
            for square in range(4 * LAYERS):
                part = all_ref[square, pl.ds(start, own), :]
                o_ref[square * own : (square + 1) * own] = part.astype(o_ref.dtype)
            o_ref[4 * LAYERS * own :] = sums.astype(o_ref.dtype)

    return pl.pallas_call(
        body,
        in_specs=[SMEM] + [VMEM] * 8,
        out_specs=[VMEM] * (1 + quarters),
        scratch_shapes=[
            pltpu.VMEM((2, 2 * lat * per, width), F32),
            pltpu.VMEM((4 * LAYERS, width, width), F32),
        ],
        out_shape=[
            jax.ShapeDtypeStruct(chunk, BF16),
            jax.ShapeDtypeStruct((count, width), F32),
        ]
        + [jax.ShapeDtypeStruct((count, width), BF16)] * (quarters - 1),
        compiler_params=params(),
        name="spectral_chain",
    )(quarter, parts, mixer, mixer_t, *block)


def gradient_sum(quarter, parts, width):
    quarters = len(parts)
    own = width // quarters
    half = 2 * LAYERS * own

    def body(q_ref, *refs):
        first_hbm, second_hbm, bias_hbm, buf, bias_buf, sem = refs[quarters:]

        def added(start, size):
            total = refs[0][start : start + size]
            for ref in refs[1:quarters]:
                total = total + ref[start : start + size].astype(F32)
            return total

        copies = [
            pltpu.make_async_copy(bias_buf, bias_hbm, sem.at[2]),
            pltpu.make_async_copy(buf.at[0], first_hbm, sem.at[0]),
            pltpu.make_async_copy(buf.at[1], second_hbm, sem.at[1]),
        ]
        sums = added(2 * half, 16)[:8]
        bias_buf[...] = pltpu.roll(sums, (width - q_ref[0] * own) % width, 1)[:, :own]
        copies[0].start()
        for which in range(2):
            buf[which] = added(which * half, half)
            copies[1 + which].start()
        for copy in copies:
            copy.wait()

    return pl.pallas_call(
        body,
        in_specs=[SMEM] + [VMEM] * quarters,
        out_specs=[HBM] * 3,
        scratch_shapes=[
            pltpu.VMEM((2, half, width), F32),
            pltpu.VMEM((8, own), F32),
            pltpu.SemaphoreType.DMA((3,)),
        ],
        out_shape=[
            jax.ShapeDtypeStruct((half, width), F32),
            jax.ShapeDtypeStruct((half, width), F32),
            jax.ShapeDtypeStruct((8, own), F32),
        ],
        compiler_params=params(),
        name="gradient_sum",
    )(quarter, *parts)


def on_device(section_input, handoff, loss_grad, w_first, w_second, bias, kept):
    lat_count = lax.axis_size("lat")
    sections = lax.axis_size("section")
    _, rows, lon, channels = section_input.shape
    width = w_first.shape[-1]
    blocks = channels // width
    quarters = lat_count // blocks
    lat = rows * lat_count
    forward = lon_table(lon, rows, quarters, False)
    inverse = lon_table(lon, rows, quarters, True)
    mixer = lat_table(lat, rows)
    place = lax.axis_index("lat")
    section = lax.axis_index("section")
    block = place // quarters
    quarter = (place % quarters).reshape(1)
    limits = lax.dynamic_slice(kept, (0, 0, block), (1, LAYERS, 1)).reshape(-1)
    scalars = jnp.concatenate([jnp.stack([block, place % quarters]), limits])
    ring = [(s, (s - 1) % sections) for s in range(sections)]
    cells = (rows * lon, channels)

    handed_du = (handoff.reshape(cells), loss_grad.reshape(cells))
    du = to_spectral(section.reshape(1), handed_du, inverse, quarters, width, False)
    du = lax.ppermute(du, "section", ring)
    x = section_input.reshape(cells)
    both = to_spectral(section.reshape(1), (x,), forward, quarters, width, True)
    later, both = lax.optimization_barrier((handoff, both))
    both = lower_halves(both, du)
    both = lax.all_to_all(both, "lat", split_axis=0, concat_axis=0, tiled=True)
    received = lax.ppermute(later, "section", ring)
    cot = jnp.where(section == sections - 1, loss_grad, received[0]).reshape(cells)
    per = MAXK // quarters
    own_params = block_params(scalars, w_first, w_second, bias, lat, per, width)
    cot, both = lax.optimization_barrier((cot, both))
    da, *parts = spectral_chain(
        quarter, both, mixer, mixer.T.copy(), own_params, lat, width, quarters
    )
    da = lax.all_to_all(da, "lat", split_axis=0, concat_axis=0, tiled=True)
    for step in (2, 1, 3):
        pairs = [
            (b * quarters + q, b * quarters + (q + step) % quarters)
            for b in range(blocks)
            for q in range(quarters)
        ]
        parts[step] = lax.ppermute(parts[step], "lat", pairs)
    handed = to_cells(da, forward.T.copy(), cot, quarters, width)
    handed, parts[0] = lax.optimization_barrier((handed, parts[0]))
    first, second, biases = gradient_sum(quarter, parts, width)
    own = width // quarters
    return (
        handed.reshape(1, rows, lon, channels),
        first.reshape(1, LAYERS, 2, own, width),
        second.reshape(1, LAYERS, 2, own, width),
        biases.reshape(1, LAYERS, 2, 2, own),
    )


def solution(mesh):
    return jax.shard_map(
        on_device,
        mesh=mesh,
        in_specs=(
            P("section", "lat", None, None),
            P("section", "lat", None, None),
            P("lat", None, None),
            P("section", None, None, None, None),
            P("section", None, None, None, None),
            P("section", None, None, None, None),
            P("section", None, None),
        ),
        out_specs=(
            P("section", "lat", None, None),
            P("section", None, None, "lat", None),
            P("section", None, None, "lat", None),
            P("section", None, None, None, "lat"),
        ),
        check_vma=False,
    )
```

```python
import math

import jax
import jax.numpy as jnp
import numpy as np
from jax import lax
from jax.experimental import pallas as pl
from jax.experimental.pallas import tpu as pltpu
from jax.sharding import PartitionSpec as P

LAYERS = 2
MAXK = 32
F32 = jnp.float32
BF16 = jnp.bfloat16


def lon_table(lon, rows, quarters, weighted):
    per = MAXK // quarters
    freqs = np.arange(MAXK)
    phase = 2.0 * math.pi * ((freqs[:, None] * np.arange(lon)[None, :]) % lon) / lon
    table = np.stack([np.cos(phase), -np.sin(phase)]) / math.sqrt(lon)
    table[1, 0] = 0.0
    table = table.astype(jnp.bfloat16).astype(np.float32)
    if weighted:
        table = table * np.where(freqs == 0, 1.0, 2.0)[None, :, None]
    split = table.reshape(2, quarters, per, lon).transpose(1, 0, 2, 3)
    full = np.zeros((quarters, 2, rows, per, rows, lon), np.float32)
    for row in range(rows):
        full[:, :, row, :, row, :] = split
    return full.reshape(quarters * 2 * rows * per, rows * lon).astype(jnp.bfloat16)


def lat_table(lat, rows):
    phase = 2.0 * math.pi * ((np.arange(lat)[:, None] * np.arange(lat)[None, :]) % lat) / lat
    cosine = np.cos(phase) / math.sqrt(lat)
    sine = np.sin(phase) / math.sqrt(lat)
    mixer = np.block([[cosine, sine], [-sine, cosine]])
    mixer = mixer.reshape(2 * lat, 2, lat // rows, rows).transpose(0, 2, 1, 3)
    return mixer.reshape(2 * lat, 2 * lat).astype(jnp.bfloat16)


def dot(left, right):
    return jnp.dot(left, right, preferred_element_type=F32)


def dot_cols(left, right):
    return lax.dot_general(left, right, (((0,), (0,)), ((), ())), preferred_element_type=F32)


def params(**kw):
    return pltpu.CompilerParams(vmem_limit_bytes=12 * 1024 * 1024, **kw)


VMEM = pl.BlockSpec(memory_space=pltpu.VMEM)
SMEM = pl.BlockSpec(memory_space=pltpu.SMEM)
HBM = pl.BlockSpec(memory_space=pltpu.HBM)


def in_hbm(value):
    return pltpu.with_memory_space_constraint(value, pltpu.HBM)


def to_spectral(scalars, sources, table, quarters, width, joined):
    cells, channels = sources[0].shape
    rows = table.shape[0] // quarters
    blocks = channels // width
    cuts = 2
    span = cells // cuts

    def body(s_ref, t_hbm, *refs):
        given = refs[: len(sources)]
        out, t_buf, x_buf, o_buf, t_sem, x_sem, o_sem = refs[len(sources) :]
        o_ref = o_buf if joined else out

        def piece(source, cut):
            part = pl.ds(cut * span, span)
            return pltpu.make_async_copy(source.at[part, :], x_buf.at[part, :], x_sem.at[cut])

        def begin(source):
            for cut in range(cuts):
                piece(source, cut).start()

        table_copy = pltpu.make_async_copy(t_hbm, t_buf, t_sem)
        table_copy.start()
        if len(given) == 1:
            begin(given[0])
        else:
            pl.when(s_ref[0] != 0)(lambda: begin(given[0]))
            pl.when(s_ref[0] == 0)(lambda: begin(given[1]))
        table_copy.wait()
        t = t_buf[...]
        for cut in range(cuts):
            piece(given[0], cut).wait()
        step = 2 * width
        for cut in range(channels // step):
            y = dot(t, x_buf[:, cut * step : (cut + 1) * step]).astype(BF16)
            for b in range(2):
                for q in range(quarters):
                    owner = (cut * 2 + b) * quarters + q
                    o_ref[owner] = y[q * rows : (q + 1) * rows, b * width : (b + 1) * width]
        if joined:
            out_copy = pltpu.make_async_copy(o_buf, out.at[:, pl.ds(0, rows), :], o_sem)
            out_copy.start()
            out_copy.wait()

    return pl.pallas_call(
        body,
        in_specs=[SMEM, HBM] + [HBM] * len(sources),
        out_specs=HBM if joined else VMEM,
        scratch_shapes=[
            pltpu.VMEM(table.shape, BF16),
            pltpu.VMEM((cells, channels), BF16),
            pltpu.VMEM((blocks * quarters, rows, width), BF16),
            pltpu.SemaphoreType.DMA(()),
            pltpu.SemaphoreType.DMA((cuts,)),
            pltpu.SemaphoreType.DMA(()),
        ],
        out_shape=jax.ShapeDtypeStruct((blocks * quarters, (1 + joined) * rows, width), BF16),
        compiler_params=params(),
        name="to_spectral",
    )(scalars, in_hbm(jnp.asarray(table)), *[in_hbm(source) for source in sources])


def lower_halves(both, du):
    rows = du.shape[1]

    def body(_, du_ref, o_hbm, sem):
        copy = pltpu.make_async_copy(du_ref, o_hbm.at[:, pl.ds(rows, rows), :], sem)
        copy.start()
        copy.wait()

    return pl.pallas_call(
        body,
        in_specs=[HBM, VMEM],
        out_specs=HBM,
        scratch_shapes=[pltpu.SemaphoreType.DMA(())],
        out_shape=jax.ShapeDtypeStruct(both.shape, BF16),
        input_output_aliases={0: 0},
        compiler_params=params(),
        name="lower_halves",
    )(both, du)


def to_cells(parts, table_t, grid_add, quarters, width):
    cells, channels = grid_add.shape
    rows = parts.shape[1]
    blocks = channels // width
    cuts = 2
    span = cells // cuts

    def body(t_ref, p_ref, g_ref, o_hbm, buf, sem):
        copies = []
        for cut in range(cuts):
            own = slice(cut * span, (cut + 1) * span)
            table = t_ref[own]
            for block in range(0, blocks, 2):
                part = p_ref[block * quarters : (block + 2) * quarters]
                part = part.reshape(2, quarters * rows, width)
                part = jnp.concatenate([part[0], part[1]], axis=1)
                lanes = slice(block * width, (block + 2) * width)
                mixed = g_ref[own, lanes].astype(F32) + dot(table, part)
                buf[own, lanes] = mixed.astype(BF16)
            copies.append(pltpu.make_async_copy(buf.at[own], o_hbm.at[own], sem.at[cut]))
            copies[-1].start()
        for copy in copies:
            copy.wait()

    return pl.pallas_call(
        body,
        in_specs=[VMEM, VMEM, VMEM],
        out_specs=HBM,
        scratch_shapes=[
            pltpu.VMEM((cells, channels), BF16),
            pltpu.SemaphoreType.DMA((cuts,)),
        ],
        out_shape=jax.ShapeDtypeStruct((cells, channels), BF16),
        compiler_params=params(),
        name="to_cells",
    )(table_t, parts, grid_add)


def block_params(scalars, w_first, w_second, bias, lat, per, width):
    def body(s_ref, w1_hbm, w2_hbm, b_ref, w_ref, wt_ref, rows_ref, mask_ref, grid_ref, buf, sem):
        start = pl.multiple_of(s_ref[0] * width, width)
        quarter = s_ref[1]
        copies = [
            pltpu.make_async_copy(w.at[0, :, :, pl.ds(start, width), :], buf.at[which], sem.at[which])
            for which, w in enumerate((w1_hbm, w2_hbm))
        ]
        for copy in copies:
            copy.start()
        for layer in range(LAYERS):
            for which in range(2):
                for r in range(2):
                    rows_ref[2 * layer + which, :, r * width : (r + 1) * width] = b_ref[
                        0, layer, which, pl.ds(r, 1), pl.ds(start, width)
                    ]
            mode = quarter * per + lax.broadcasted_iota(jnp.int32, (per, 1, 2 * width), 0)
            mask_ref[layer] = (mode < s_ref[2 + layer]).astype(F32)
        rows = lax.broadcasted_iota(jnp.int32, (lat, lat), 0)
        cols = lax.broadcasted_iota(jnp.int32, (lat, lat), 1)
        eye = (rows == cols).astype(F32)
        back = ((rows + cols) % lat == 0).astype(F32)
        has_zero = (quarter == 0).astype(F32)
        grid_ref[0] = (eye + 0.5 * has_zero * (back - eye)).astype(BF16)
        grid_ref[1] = (eye - 0.5 * has_zero * (back + eye)).astype(BF16)
        for which in range(2):
            copies[which].wait()
            for layer in range(LAYERS):
                real, imag = (buf[which, layer, 0], buf[which, layer, 1])
                w_ref[2 * layer + which, :width, :width] = real
                w_ref[2 * layer + which, :width, width:] = imag
                w_ref[2 * layer + which, width:, :width] = -imag
                w_ref[2 * layer + which, width:, width:] = real
                real, imag = (real.astype(F32).T.astype(BF16), imag.astype(F32).T.astype(BF16))
                wt_ref[2 * layer + which, :width, :width] = real
                wt_ref[2 * layer + which, :width, width:] = -imag
                wt_ref[2 * layer + which, width:, :width] = imag
                wt_ref[2 * layer + which, width:, width:] = real

    return pl.pallas_call(
        body,
        in_specs=[SMEM, HBM, HBM, VMEM],
        out_specs=[VMEM] * 5,
        scratch_shapes=[
            pltpu.VMEM((2, LAYERS, 2, width, width), BF16),
            pltpu.SemaphoreType.DMA((2,)),
        ],
        out_shape=[
            jax.ShapeDtypeStruct((2 * LAYERS, 2 * width, 2 * width), BF16),
            jax.ShapeDtypeStruct((2 * LAYERS, 2 * width, 2 * width), BF16),
            jax.ShapeDtypeStruct((2 * LAYERS, 1, 2 * width), F32),
            jax.ShapeDtypeStruct((LAYERS, per, 1, 2 * width), F32),
            jax.ShapeDtypeStruct((2, lat, lat), BF16),
        ],
        compiler_params=params(),
        name="block_params",
    )(scalars, in_hbm(w_first), in_hbm(w_second), bias)


def spectral_chain(quarter, parts, mixer, mixer_t, block, lat, width, quarters):
    sources, both, _ = parts.shape
    chunk = (sources, both // 2, width)
    per = sources * (both // 2) // (2 * lat)
    tall = per * lat
    own = width // quarters
    count = 4 * LAYERS * own + 16

    def body(q_ref, parts_ref, l_ref, lt_ref, w_ref, wt_ref, b_ref, mask_ref, *more):
        grid_ref, da_ref, *mine_and_sent = more[:-2]
        tmp, all_ref = more[-2:]
        quarter = q_ref[0]
        mix, mix_t = (l_ref[...], lt_ref[...])

        for slot in range(2):
            part = parts_ref[:, slot * (both // 2) : (slot + 1) * (both // 2), :]
            tmp[slot] = part.reshape(2 * lat * per, width).astype(F32)
        mixed = ([], [])
        for k in range(per):
            columns = [tmp[slot, pl.ds(k, 2 * lat, stride=per), :] for slot in range(2)]
            cells = dot(mix, jnp.concatenate(columns, axis=1).astype(BF16))
            for slot in range(2):
                lanes = slice(slot * width, (slot + 1) * width)
                mixed[slot].append(
                    jnp.concatenate([cells[:lat, lanes], cells[lat:, lanes]], axis=1)
                )

        def through_grid(v):
            first = v[:lat]
            first = jnp.concatenate(
                [dot(grid_ref[0], first[:, :width]), dot(grid_ref[1], first[:, width:])], axis=1
            )
            return jnp.concatenate([first, v[lat:].astype(F32)], axis=0)

        def masked(v, layer):
            split = v.reshape(per, lat, 2 * width) * mask_ref[layer]
            return split.reshape(tall, 2 * width).astype(BF16)

        z = jnp.concatenate(mixed[0], axis=0)
        slopes = []
        lefts = {}
        index = lax.broadcasted_iota(jnp.int32, (16, width), 0)
        sums = jnp.zeros((16, width), F32)

        def products(which, layer, right, sums):
            outer = dot_cols(lefts[which, layer], right)
            total = jnp.sum(right.astype(F32), axis=0, keepdims=True)
            squares = (
                outer[:width, :width] + outer[width:, width:],
                outer[:width, width:] - outer[width:, :width],
            )
            for r in range(2):
                all_ref[(which * LAYERS + layer) * 2 + r] = squares[r]
                slot = (layer * 2 + which) * 2 + r
                sums = sums + jnp.where(index == slot, total[:, r * width : (r + 1) * width], 0.0)
            return sums

        for layer in range(LAYERS):
            z_low = z.astype(BF16)
            lefts[0, layer] = z_low
            pre = dot(z_low, w_ref[2 * layer]) + b_ref[2 * layer]
            sig = jax.nn.sigmoid(pre)
            hidden = (pre * sig).astype(BF16)
            lefts[1, layer] = hidden
            slopes.append(sig * (1.0 + pre * (1.0 - sig)))
            if layer + 1 < LAYERS:
                out = dot(hidden, w_ref[2 * layer + 1]) + b_ref[2 * layer + 1]
                z = z + through_grid(masked(out, layer))
        grad = jnp.concatenate(mixed[1], axis=0)
        total = None
        for layer in reversed(range(LAYERS)):
            dout = masked(grad, layer)
            sums = products(1, layer, dout, sums)
            dpre = (dot(dout, wt_ref[2 * layer + 1]) * slopes[layer]).astype(BF16)
            sums = products(0, layer, dpre, sums)
            dz = dot(dpre, wt_ref[2 * layer])
            if layer:
                grad = grad + through_grid(dz.astype(BF16))
            total = dz if total is None else total + dz
        total = total.astype(BF16)
        for k in range(0, per, 2):
            pair = [total[j * lat : (j + 1) * lat] for j in (k, k + 1)]
            pair = [jnp.concatenate([v[:, :width], v[:, width:]], axis=0) for v in pair]
            bands = dot(mix_t, jnp.concatenate(pair, axis=1))
            for j in range(2):
                lanes = slice(j * width, (j + 1) * width)
                tmp[0, pl.ds(k + j, 2 * lat, stride=per), :] = bands[:, lanes]
        da_ref[...] = tmp[0].astype(BF16).reshape(chunk)
        for step, o_ref in enumerate(mine_and_sent):
            start = pl.multiple_of((quarter ^ step) * own, own)
            for square in range(4 * LAYERS):
                part = all_ref[square, pl.ds(start, own), :]
                o_ref[square * own : (square + 1) * own] = part.astype(o_ref.dtype)
            o_ref[4 * LAYERS * own :] = sums.astype(o_ref.dtype)

    return pl.pallas_call(
        body,
        in_specs=[SMEM] + [VMEM] * 8,
        out_specs=[VMEM] * (1 + quarters),
        scratch_shapes=[
            pltpu.VMEM((2, 2 * lat * per, width), F32),
            pltpu.VMEM((4 * LAYERS, width, width), F32),
        ],
        out_shape=[
            jax.ShapeDtypeStruct(chunk, BF16),
            jax.ShapeDtypeStruct((count, width), F32),
        ]
        + [jax.ShapeDtypeStruct((count, width), BF16)] * (quarters - 1),
        compiler_params=params(),
        name="spectral_chain",
    )(quarter, parts, mixer, mixer_t, *block)


def gradient_sum(quarter, parts, width):
    quarters = len(parts)
    own = width // quarters
    half = 2 * LAYERS * own

    def body(q_ref, *refs):
        first_hbm, second_hbm, bias_hbm, buf, bias_buf, sem = refs[quarters:]

        def added(start, size):
            total = refs[0][start : start + size]
            for ref in refs[1:quarters]:
                total = total + ref[start : start + size].astype(F32)
            return total

        copies = [
            pltpu.make_async_copy(bias_buf, bias_hbm, sem.at[2]),
            pltpu.make_async_copy(buf.at[0], first_hbm, sem.at[0]),
            pltpu.make_async_copy(buf.at[1], second_hbm, sem.at[1]),
        ]
        sums = added(2 * half, 16)[:8]
        bias_buf[...] = pltpu.roll(sums, (width - q_ref[0] * own) % width, 1)[:, :own]
        copies[0].start()
        for which in range(2):
            buf[which] = added(which * half, half)
            copies[1 + which].start()
        for copy in copies:
            copy.wait()

    return pl.pallas_call(
        body,
        in_specs=[SMEM] + [VMEM] * quarters,
        out_specs=[HBM] * 3,
        scratch_shapes=[
            pltpu.VMEM((2, half, width), F32),
            pltpu.VMEM((8, own), F32),
            pltpu.SemaphoreType.DMA((3,)),
        ],
        out_shape=[
            jax.ShapeDtypeStruct((half, width), F32),
            jax.ShapeDtypeStruct((half, width), F32),
            jax.ShapeDtypeStruct((8, own), F32),
        ],
        compiler_params=params(),
        name="gradient_sum",
    )(quarter, *parts)


def on_device(section_input, handoff, loss_grad, w_first, w_second, bias, kept):
    lat_count = lax.axis_size("lat")
    sections = lax.axis_size("section")
    _, rows, lon, channels = section_input.shape
    width = w_first.shape[-1]
    blocks = channels // width
    quarters = lat_count // blocks
    lat = rows * lat_count
    forward = lon_table(lon, rows, quarters, False)
    inverse = lon_table(lon, rows, quarters, True)
    mixer = lat_table(lat, rows)
    place = lax.axis_index("lat")
    section = lax.axis_index("section")
    block = place // quarters
    quarter = (place % quarters).reshape(1)
    limits = lax.dynamic_slice(kept, (0, 0, block), (1, LAYERS, 1)).reshape(-1)
    scalars = jnp.concatenate([jnp.stack([block, place % quarters]), limits])
    ring = [(s, (s - 1) % sections) for s in range(sections)]
    cells = (rows * lon, channels)

    handed_du = (handoff.reshape(cells), loss_grad.reshape(cells))
    du = to_spectral(section.reshape(1), handed_du, inverse, quarters, width, False)
    du = lax.ppermute(du, "section", ring)
    x = section_input.reshape(cells)
    both = to_spectral(section.reshape(1), (x,), forward, quarters, width, True)
    later, both = lax.optimization_barrier((handoff, both))
    both = lower_halves(both, du)
    both = lax.all_to_all(both, "lat", split_axis=0, concat_axis=0, tiled=True)
    received = lax.ppermute(later, "section", ring)
    cot = jnp.where(section == sections - 1, loss_grad, received[0]).reshape(cells)
    per = MAXK // quarters
    own_params = block_params(scalars, w_first, w_second, bias, lat, per, width)
    cot, both = lax.optimization_barrier((cot, both))
    da, *parts = spectral_chain(
        quarter, both, mixer, mixer.T.copy(), own_params, lat, width, quarters
    )
    da = lax.all_to_all(da, "lat", split_axis=0, concat_axis=0, tiled=True)
    for step in range(1, quarters):
        pairs = [(d, d ^ step) for d in range(lat_count)]
        parts[step] = lax.ppermute(parts[step], "lat", pairs)
    handed = to_cells(da, forward.T.copy(), cot, quarters, width)
    handed, parts[0] = lax.optimization_barrier((handed, parts[0]))
    first, second, biases = gradient_sum(quarter, parts, width)
    own = width // quarters
    return (
        handed.reshape(1, rows, lon, channels),
        first.reshape(1, LAYERS, 2, own, width),
        second.reshape(1, LAYERS, 2, own, width),
        biases.reshape(1, LAYERS, 2, 2, own),
    )


def solution(mesh):
    return jax.shard_map(
        on_device,
        mesh=mesh,
        in_specs=(
            P("section", "lat", None, None),
            P("section", "lat", None, None),
            P("lat", None, None),
            P("section", None, None, None, None),
            P("section", None, None, None, None),
            P("section", None, None, None, None),
            P("section", None, None),
        ),
        out_specs=(
            P("section", "lat", None, None),
            P("section", None, None, "lat", None),
            P("section", None, None, "lat", None),
            P("section", None, None, None, "lat"),
        ),
        check_vma=False,
    )
```
